256 devices in a mesh: elem: 64 (over y, z, core), snap: 4 (over x).
Axes of the slice: x: 4, y: 4, z: 8, core: 2. Of those that a mesh axis runs over, the one named last changes fastest.
Arguments:
- node_basis: bfloat16 [65536, 1536], P('elem'), may hold values from -0.25 to 0.25
- stiff_terms: bfloat16 [16, 24, 24], replicated, may hold values from -1.25 to 1.25
- reduced_coords: bfloat16 [512, 32], P(None, 'snap'), may hold values from -6 to 6
- sample_list: int32 [512], replicated, may hold values from 0 to 2047, as said below
- connectivity: int32 [2048, 8], replicated, may hold values from -1 to 65535, as said below
- node_slot: int32 [65536], replicated, may hold values from 0 to 65535, as said below
- elem_device: int32 [512], replicated, may hold values from 0 to 63, as said below
Outputs:
- ortho_panel: float32 [1024, 512, 512], P('elem', 'snap')
- triangle_factor: float32 [512, 512], P('elem')
The draws below stay inside these ranges and needn't reach their ends.
Inputs may be any that keep to these rules, and one draw needn't show every extreme that they name: `sample_list`: distinct element ids. `connectivity`: each element lists 4, 6 or 8 live nodes first and -1 after them; the live nodes of one element are owned by distinct indices of elem (owner = node_slot // 1024); for every index d of elem and every owner o, at most 2 sampled elements computed on d have a live node owned by o, and some pair (d, o) reaches 2. `node_slot`: a permutation. `elem_device`: each index of elem computes at most 16 sampled elements; some index computes exactly 16.
All inputs are finite; a program needn't handle non-finite values.
Results may differ from the reference program's by a relative error of at most 0.0056.
Values may be sent and summed in bfloat16 or wider, within the bound.
A program may use at most 64 MiB of HBM per device.

```python
import jax
import jax.numpy as jnp
from jax import lax

MODES = 512
TERMS = 16
SNAPS = 32
ENODES = 8
NDOF = 3
EL_DEV = 8
NODE_DEV = 1024
CAP = 16
SAMPLED = 512
ELEMS = 2048
NODES = 65536
COLS = 512
N_ELEM = 64


def build_tables(key):
    subkeys = [jax.random.fold_in(key, 101 + number) for number in range(10)]
    sampled_ids = jax.random.permutation(subkeys[0], ELEMS)[:SAMPLED].astype(jnp.int32)
    halves = N_ELEM // 2
    extra_count = jax.random.randint(subkeys[1], (halves,), 0, CAP + 1).astype(jnp.int32).at[0].set(0)
    paired = jnp.stack([CAP - extra_count, extra_count], axis=1).reshape(N_ELEM)
    device_order = jax.random.permutation(subkeys[2], N_ELEM).astype(jnp.int32)
    counts = jnp.zeros((N_ELEM,), jnp.int32).at[device_order].set(paired)
    bounds = jnp.cumsum(counts)
    position_rank = jax.random.permutation(subkeys[3], SAMPLED).astype(jnp.int32)
    assigned = jnp.sum((bounds[None, :] <= position_rank[:, None]).astype(jnp.int32), axis=1).astype(jnp.int32)
    position_ids = jnp.arange(SAMPLED, dtype=jnp.int32)
    earlier = (position_ids[None, :] < position_ids[:, None]) & (assigned[None, :] == assigned[:, None])
    slots = jnp.sum(earlier.astype(jnp.int32), axis=1).astype(jnp.int32)
    slot_table = jax.random.permutation(subkeys[4], NODES).astype(jnp.int32)
    inverse = jnp.zeros((NODES,), jnp.int32).at[slot_table].set(jnp.arange(NODES, dtype=jnp.int32))
    owner_ids = jnp.arange(N_ELEM, dtype=jnp.int32)
    cycle_scores = jax.random.randint(subkeys[5], (N_ELEM, N_ELEM), 0, 1 << 20) * N_ELEM + owner_ids[None, :]
    cycles = jnp.argsort(cycle_scores, axis=1).astype(jnp.int32)
    positions = jnp.arange(ENODES, dtype=jnp.int32)
    cycle_index = (slots[:, None] * ENODES + positions[None, :]) % N_ELEM
    sampled_owners = cycles[assigned[:, None], cycle_index]
    scores = jax.random.randint(subkeys[6], (ELEMS, N_ELEM), 0, 1 << 20) * N_ELEM + owner_ids[None, :]
    owner_pick = jnp.argsort(scores, axis=1)[:, :ENODES].astype(jnp.int32)
    owner_pick = owner_pick.at[sampled_ids].set(sampled_owners)
    local_pick = jax.random.randint(subkeys[7], (ELEMS, ENODES), 0, NODE_DEV).astype(jnp.int32)
    node_ids = inverse[owner_pick * NODE_DEV + local_pick]
    elem_kinds = jax.random.randint(subkeys[8], (ELEMS,), 0, 3).astype(jnp.int32)
    linked = jnp.where(positions[None, :] < (4 + 2 * elem_kinds)[:, None], node_ids, -1).astype(jnp.int32)
    return (sampled_ids, linked, slot_table, assigned)


def draw_sample_list(key, part):
    return build_tables(key)[0]


def draw_connectivity(key, part):
    return build_tables(key)[1]


def draw_node_slot(key, part):
    return build_tables(key)[2]


def draw_elem_device(key, part):
    return build_tables(key)[3]


def shard_levels(own_key, shape, shards, low, largest):
    level, own = 1.0, jax.random.fold_in(own_key, 6)
    for axis_at, shards_of in shards:
        heights = jnp.exp(jax.random.uniform(jax.random.fold_in(own, axis_at), (shards_of,), jnp.float32, low / len(shards), largest / len(shards)))
        level = level * jnp.repeat(heights, shape[axis_at] // shards_of).reshape([-1 if axis == axis_at else 1 for axis in range(len(shape))])
    return level


def scatter_about(stream_key, extent, width, most, cuts=(), kind=jnp.bfloat16):
    factor_of = shard_levels(stream_key, extent, cuts, -0.22, 0.18) if cuts else 1.0
    entries = jax.random.normal(stream_key, extent, jnp.float32) * width * factor_of
    return jnp.minimum(jnp.maximum(entries, -most), most).astype(kind)


def setup_inputs(seed: int = 0) -> dict:
    key_of = jax.random.split(jax.random.key(seed), 8)
    node_basis = scatter_about(key_of[0], (NODES, NDOF * MODES), MODES ** -0.5, 0.25, ((0, 64),))
    stiff_terms = scatter_about(key_of[1], (TERMS, ENODES * NDOF, ENODES * NDOF), (ENODES * NDOF) ** -0.5, 1.25)
    reduced_coords = scatter_about(key_of[2], (MODES, SNAPS), 1.0, 6.0, ((1, 4),))
    sample_list = draw_sample_list(jax.random.fold_in(key_of[7], 71), 0)
    connectivity = draw_connectivity(jax.random.fold_in(key_of[7], 71), 0)
    node_slot = draw_node_slot(jax.random.fold_in(key_of[7], 71), 0)
    elem_device = draw_elem_device(jax.random.fold_in(key_of[7], 71), 0)
    return dict(node_basis=node_basis, stiff_terms=stiff_terms, reduced_coords=reduced_coords, sample_list=sample_list, connectivity=connectivity, node_slot=node_slot, elem_device=elem_device)


def count_slots(elem_device):
    position_ids = jnp.arange(elem_device.shape[0], dtype=jnp.int32)
    earlier = (position_ids[None, :] < position_ids[:, None]) & (elem_device[None, :] == elem_device[:, None])
    return jnp.sum(earlier.astype(jnp.int32), axis=1).astype(jnp.int32)

def reference(node_basis, stiff_terms, reduced_coords, sample_list, connectivity, node_slot, elem_device):
    sampled = EL_DEV * N_ELEM
    node_ids = connectivity[sample_list]
    live_nodes = node_ids >= 0
    stored_rows = jnp.where(live_nodes, node_slot[jnp.maximum(node_ids, 0)], 0).astype(jnp.int32)
    gathered = jnp.where(live_nodes[:, :, None], node_basis[stored_rows], jnp.zeros((), node_basis.dtype))
    local_basis = gathered.reshape(sampled, ENODES * NDOF, MODES)
    coords_wide = reduced_coords.astype(jnp.float32)
    terms_wide = stiff_terms.astype(jnp.float32)

    def project_one(element_basis):
        basis_wide = element_basis.astype(jnp.float32)
        displaced = jnp.einsum('km,ms->ks', basis_wide, coords_wide).astype(jnp.bfloat16)
        forces = jnp.einsum('tkl,ls->kst', terms_wide, displaced.astype(jnp.float32)).astype(jnp.bfloat16)
        forces = forces.reshape(ENODES * NDOF, COLS)
        return jnp.einsum('km,kc->mc', basis_wide, forces.astype(jnp.float32)).astype(jnp.bfloat16)
    projected = lax.map(project_one, local_basis)
    flat_rows = projected.reshape(sampled * MODES, COLS)
    gram_matrix = jnp.dot(flat_rows.T.astype(jnp.float32), flat_rows.astype(jnp.float32), preferred_element_type=jnp.float32) / (sampled * MODES)
    lower_factor = jnp.linalg.cholesky(gram_matrix)

    def solve_one(element_rows):
        return jax.scipy.linalg.solve_triangular(lower_factor, element_rows.astype(jnp.float32).T, lower=True).T
    live_panel = lax.map(solve_one, projected)
    slot_ids = count_slots(elem_device)
    ortho_panel = jnp.zeros((N_ELEM * CAP, MODES, COLS), jnp.float32).at[elem_device * CAP + slot_ids].set(live_panel)
    return (ortho_panel, lower_factor.T)
```

```python
import jax
import jax.numpy as jnp
from jax import lax
from jax.experimental import pallas as pl
from jax.experimental.pallas import tpu as pltpu
from jax.sharding import PartitionSpec as P

F32, BF16, I32 = jnp.float32, jnp.bfloat16, jnp.int32
HI = lax.Precision.HIGHEST
MESH = pl.DeviceIdType.MESH
MODES = 512
COLS = 512
ENODES = 8
NDOF = 3
CAP = 16
SAMPLED = 512
N_ELEM = 64
N_SNAP = 4
NODE_DEV = 1024
BAND = MODES // N_SNAP
KROWS = ENODES * NDOF
BLOCKS = [(k, i) for k in range(4) for i in range(k, 4)]


def iota(shape, axis):
    return lax.broadcasted_iota(I32, shape, axis)


def hot(mask):
    return jnp.where(mask, 1.0, 0.0).astype(BF16)


def dot_nt(a, b):
    return lax.dot_general(a, b, (((1,), (1,)), ((), ())), preferred_element_type=F32)


def dot_tn(a, b, precision=None):
    return lax.dot_general(
        a, b, (((0,), (0,)), ((), ())), precision=precision, preferred_element_type=F32
    )


def dot_nn(a, b):
    return jnp.dot(a, b, preferred_element_type=F32)


def index_kernel(
    sample_ref, conn_ref, slot_ref, dev_ref, basis_ref, out_ref, place_ref, basis_v, ids_s, st_s, tab_s, sem
):
    load = pltpu.make_async_copy(basis_ref, basis_v, sem)
    load.start()
    me = lax.axis_index("elem")
    conn = conn_ref[...] + 1
    conn_hi = (conn >> 8).astype(F32)
    conn_lo = (conn & 255).astype(F32)
    conn_t = jnp.concatenate([conn_hi.T, conn_lo.T], 0).astype(BF16)
    sample = sample_ref[...]
    ids = jnp.zeros((16, SAMPLED), F32)
    for part in range(4):
        picks = hot(iota((512, SAMPLED), 0) + 512 * part == sample)
        ids = ids + dot_nn(conn_t[:, 512 * part : 512 * part + 512], picks)
    ids1 = (ids[0:8] * 256.0 + ids[8:16]).astype(I32)
    live = ids1 > 0
    ids_s[...] = jnp.maximum(ids1 - 1, 0)
    table = slot_ref[...]
    tab_s[0:128, :] = (table >> 8).astype(F32).T.astype(BF16)
    tab_s[128:256, :] = (table & 255).astype(F32).T.astype(BF16)

    def lookup(p, carry):
        row = ids_s[pl.ds(p, 1), :]
        picks = hot(iota((512, SAMPLED), 0) == (row >> 7))
        found = dot_nn(tab_s[...], picks)
        here = iota((128, SAMPLED), 0) == (row & 127)
        hi = jnp.sum(jnp.where(here, found[0:128], 0.0), axis=0, keepdims=True)
        lo = jnp.sum(jnp.where(here, found[128:256], 0.0), axis=0, keepdims=True)
        st_s[pl.ds(p, 1), :] = (hi * 256.0 + lo).astype(I32)
        return carry

    lax.fori_loop(0, ENODES, lookup, 0)
    stored = st_s[...]
    owner = stored >> 10
    mine = live & (owner == me)
    has = jnp.max(jnp.where(mine, 1.0, 0.0), axis=0, keepdims=True)
    row = jnp.sum(jnp.where(mine, stored & (NODE_DEV - 1), 0), axis=0, keepdims=True)
    dev = dev_ref[...]
    dev_f = dev.astype(F32)
    dev_col = jnp.broadcast_to(dev_f, (8, SAMPLED)).T[:, 0:1]
    same = hot((dev_col == dev_f) & (iota((SAMPLED, SAMPLED), 0) < iota((SAMPLED, SAMPLED), 1)))
    counts = dot_nn(jnp.where(iota((8, SAMPLED), 0) == 0, has, 1.0).astype(BF16), same)
    rank = counts[0:1].astype(I32)
    slot = counts[1:2].astype(I32)
    q = iota((2 * N_ELEM, SAMPLED), 0)
    goes = hot(((q >> 1) == dev) & ((q & 1) == rank) & (has > 0.5))
    r8 = iota((8, SAMPLED), 0)
    vals = jnp.where(r8 == 0, (row >> 8).astype(F32), jnp.where(r8 == 1, (row & 255).astype(F32), 1.0))
    tab = dot_nt(goes, vals.astype(BF16))
    pick = (tab[:, 0:1] * 256.0 + tab[:, 1:2]).astype(I32)
    valid = tab[:, 2:3] > 0.5
    select = hot((iota((2 * N_ELEM, NODE_DEV), 1) == pick) & valid)
    here = hot((slot == iota((CAP, SAMPLED), 0)) & (dev == me))
    own = dot_nt(here, jnp.where(live, owner + 1, 0).astype(F32).astype(BF16))
    spread = jnp.where((iota((128, CAP), 0) >> 3) == iota((128, CAP), 1), 1.0, 0.0).astype(BF16)
    wide = dot_nn(spread, own.astype(BF16))
    col = jnp.sum(
        jnp.where((iota((128, ENODES), 0) & 7) == iota((128, ENODES), 1), wide, 0.0),
        axis=1,
        keepdims=True,
    )
    by_row = jnp.broadcast_to(col, (128, 128))
    by_col = by_row.T
    before = (iota((128, 128), 1) >> 3) < (iota((128, 128), 0) >> 3)
    ahead = jnp.sum(jnp.where(before & (by_row == by_col), 1.0, 0.0), axis=1, keepdims=True)
    source = ((col - 1.0) * 2.0 + ahead).astype(I32)
    place_ref[...] = hot((iota((128, 128), 1) == source) & (col > 0.5))
    load.wait()
    out_ref[...] = dot_nn(select, basis_v[...]).astype(BF16)


def index_call(sample, conn, slots, dev, basis):
    width = basis.shape[1]
    vm = pl.BlockSpec(memory_space=pltpu.VMEM)
    return pl.pallas_call(
        index_kernel,
        out_shape=(
            jax.ShapeDtypeStruct((2 * N_ELEM, width), BF16),
            jax.ShapeDtypeStruct((128, 128), BF16),
        ),
        in_specs=[vm, vm, vm, vm, pl.BlockSpec(memory_space=pl.ANY)],
        out_specs=(vm, vm),
        scratch_shapes=[
            pltpu.VMEM(basis.shape, BF16),
            pltpu.VMEM((ENODES, SAMPLED), I32),
            pltpu.VMEM((ENODES, SAMPLED), I32),
            pltpu.VMEM((256, 512), BF16),
            pltpu.SemaphoreType.DMA,
        ],
        name="index_tables",
    )(sample, conn, slots, dev, basis)


def split2(x):
    hi = x.astype(BF16)
    return hi, (x - hi.astype(F32)).astype(BF16)


def split3(x):
    h = x.astype(BF16).astype(F32)
    r = x - h
    m = r.astype(BF16).astype(F32)
    return h, m, r - m


def gram_part_kernel(basis_ref, forces_ref, c_ref):
    basis = basis_ref[...]
    forces = forces_ref[...]
    rows = CAP * KROWS
    inner = dot_nt(basis, basis)
    same = (iota((rows, rows), 0) // KROWS) == (iota((rows, rows), 1) // KROWS)
    inner = jnp.where(same, inner, 0.0)
    h, m, l = split3(inner)
    moved = dot_nn(h.astype(BF16), forces) + dot_nn(m.astype(BF16), forces) + dot_nn(l.astype(BF16), forces)
    moved = moved * (1.0 / (SAMPLED * MODES))
    h, m, l = split3(moved)
    h, m, l = h.astype(BF16), m.astype(BF16), l.astype(BF16)
    at = 0
    for k in range(4):
        left = forces[:, 128 * k : 128 * k + 128]
        part = dot_tn(left, h[:, 128 * k :]) + dot_tn(left, m[:, 128 * k :]) + dot_tn(left, l[:, 128 * k :])
        for i in range(4 - k):
            c_ref[at] = part[:, 128 * i : 128 * i + 128].reshape(16, 8, 128)
            at += 1


def gram_part(basis, forces):
    return pl.pallas_call(
        gram_part_kernel,
        out_shape=jax.ShapeDtypeStruct((10, 16, 8, 128), F32),
        name="gram_part",
    )(basis, forces)


def gram_sum_kernel(
    c_ref, o_ref, rbuf, rs_send, rs_recv, own_sem, z_send, z_recv, xy_send, xy_recv, c_send, c_recv
):
    e = lax.axis_index("elem")
    x = lax.axis_index("snap")
    y, z, c = e // 16, (e // 2) % 8, e % 2
    barrier = pltpu.get_barrier_semaphore()

    def greet(j, carry):
        pl.semaphore_signal(barrier, inc=1, device_id=((e + j) % N_ELEM, x), device_id_type=MESH)
        return carry

    lax.fori_loop(1, N_ELEM, greet, 0)

    def greet_x(j, carry):
        x2 = (x + 1 + j // 4) % 4
        y2 = j % 4
        pl.semaphore_signal(
            barrier, inc=1, device_id=(y2 * 16 + z * 2 + c, x2), device_id_type=MESH
        )
        return carry

    lax.fori_loop(0, 12, greet_x, 0)
    pl.semaphore_wait(barrier, N_ELEM - 1 + 12)

    line = y * 2 + c
    k_own = (5 * z + 7) // 8
    owns = (8 * k_own) // 5 == z

    def piece(i):
        t = (i + e) % 40
        ln, k = t // 5, t % 5
        peer = (ln // 2) * 16 + ((8 * k) // 5) * 2 + ln % 2
        copy = pltpu.make_async_remote_copy(
            src_ref=c_ref.at[x * 40 + t],
            dst_ref=rbuf.at[e],
            send_sem=rs_send.at[t],
            recv_sem=rs_recv.at[e],
            device_id=(peer, x),
            device_id_type=MESH,
        )
        return copy, peer

    def scatter(i, carry):
        copy, peer = piece(i)

        @pl.when(peer != e)
        def _():
            copy.start()

        return carry

    lax.fori_loop(0, 40, scatter, 0)
    tile = x * 40 + line * 5 + k_own

    @pl.when(owns)
    def _():
        mine = pltpu.make_async_copy(c_ref.at[tile], rbuf.at[e], own_sem)
        mine.start()
        mine.wait()

        def arrive(j, carry):
            s = (e + j) % N_ELEM
            pltpu.make_async_copy(rbuf.at[s], rbuf.at[s], rs_recv.at[s]).wait()
            return carry

        lax.fori_loop(1, N_ELEM, arrive, 0)
        o_ref[tile] = jnp.sum(rbuf[...], axis=0)
        for dz in range(1, 8):
            z2 = (z + dz) % 8
            pltpu.make_async_remote_copy(
                src_ref=o_ref.at[tile],
                dst_ref=o_ref.at[tile],
                send_sem=z_send.at[dz - 1],
                recv_sem=z_recv.at[k_own],
                device_id=(y * 16 + z2 * 2 + c, x),
                device_id_type=MESH,
            ).start()

    first = x * 40 + line * 5
    for k in range(5):

        @pl.when((8 * k) // 5 != z)
        def _():
            ref = o_ref.at[first + k]
            pltpu.make_async_copy(ref, ref, z_recv.at[k]).wait()

    def chunk_copy(j):
        x2, y2 = (x + j // 4) % 4, (y + j) % 4
        return pltpu.make_async_remote_copy(
            src_ref=o_ref.at[pl.ds(first, 5)],
            dst_ref=o_ref.at[pl.ds(first, 5)],
            send_sem=xy_send.at[j],
            recv_sem=xy_recv.at[x * 4 + y],
            device_id=(y2 * 16 + z * 2 + c, x2),
            device_id_type=MESH,
        )

    def send_chunk(j, carry):
        chunk_copy(j).start()
        return carry

    lax.fori_loop(1, 16, send_chunk, 0)

    def core_copy(j):
        x2, y2 = (x + j // 4) % 4, (y + j) % 4
        n = x2 * 4 + y2
        at = (x2 * 8 + y2 * 2 + c) * 5
        return n, at, pltpu.make_async_remote_copy(
            src_ref=o_ref.at[pl.ds(at, 5)],
            dst_ref=o_ref.at[pl.ds(at, 5)],
            send_sem=c_send.at[n],
            recv_sem=c_recv.at[n],
            device_id=(e + 1 - 2 * c, x),
            device_id_type=MESH,
        )

    core_copy(0)[2].start()

    def forward(j, carry):
        n, at, copy = core_copy(j)
        ref = o_ref.at[pl.ds(at, 5)]
        pltpu.make_async_copy(ref, ref, xy_recv.at[n]).wait()
        copy.start()
        return carry

    lax.fori_loop(1, 16, forward, 0)

    def finish(n, carry):
        other = (n * 2 + 1 - c) * 5
        ref = o_ref.at[pl.ds(other, 5)]
        pltpu.make_async_copy(ref, ref, c_recv.at[n]).wait()
        pltpu.make_async_copy(ref, ref, c_send.at[n]).wait()
        return carry

    lax.fori_loop(0, 16, finish, 0)

    def drain_xy(j, carry):
        ref = o_ref.at[pl.ds(first, 5)]
        pltpu.make_async_copy(ref, ref, xy_send.at[j]).wait()
        return carry

    lax.fori_loop(1, 16, drain_xy, 0)

    @pl.when(owns)
    def _():
        for dz in range(7):
            ref = o_ref.at[tile]
            pltpu.make_async_copy(ref, ref, z_send.at[dz]).wait()

    def drain_rs(i, carry):
        copy, peer = piece(i)

        @pl.when(peer != e)
        def _():
            copy.wait_send()

        return carry

    lax.fori_loop(0, 40, drain_rs, 0)


def gram_sum(parts):
    dma = pltpu.SemaphoreType.DMA
    vm = pl.BlockSpec(memory_space=pltpu.VMEM)
    return pl.pallas_call(
        gram_sum_kernel,
        out_shape=jax.ShapeDtypeStruct((160, 8, 128), F32),
        in_specs=[vm],
        out_specs=vm,
        scratch_shapes=[
            pltpu.VMEM((N_ELEM, 8, 128), F32),
            dma((40,)),
            dma((N_ELEM,)),
            dma,
            dma((7,)),
            dma((5,)),
            dma((16,)),
            dma((16,)),
            dma((16,)),
            dma((16,)),
        ],
        compiler_params=pltpu.CompilerParams(collective_id=1, has_side_effects=True),
        name="gram_sum",
    )(parts)


def panel(p0, p1, lane):
    def rep(v, i):
        return jnp.broadcast_to(v[i : i + 1, :], (8, 128))

    cols = [jnp.broadcast_to(p0[:, lane + j : lane + j + 1], (8, 128)) for j in range(8)]
    a = {(i, j): rep(cols[j], i) for j in range(8) for i in range(j + 1)}
    rows = [[rep(p0, i), rep(p1, i)] for i in range(8)]
    sub = iota((8, 128), 0)
    out = [None, None]
    for k in range(8):
        r = lax.rsqrt(a[k, k])
        u = {j: a[k, j] * r for j in range(k + 1, 8)}
        rows[k] = [v * r for v in rows[k]]
        for i in range(k + 1, 8):
            for j in range(i, 8):
                a[i, j] = a[i, j] - u[i] * u[j]
            rows[i] = [v - u[i] * w for v, w in zip(rows[i], rows[k])]
        for c in range(2):
            out[c] = rows[k][c] if k == 0 else jnp.where(sub == k, rows[k][c], out[c])
    return out


def factor(A, M, W):
    eye = jnp.where(iota((128, 128), 0) == iota((128, 128), 1), 1.0, 0.0)

    def block(k, carry):
        off = pl.multiple_of(k * 128, 128)
        M[:, 0:128] = A[pl.ds(off, 128), pl.ds(off, 128)]
        M[:, 128:256] = eye
        for p in range(16):
            top = 8 * p
            u0, u1 = panel(M[top : top + 8, 0:128], M[top : top + 8, 128:256], top)
            M[top : top + 8, 0:128] = u0
            M[top : top + 8, 128:256] = u1
            if p < 15:
                h0, m0, l0 = split3(u0)
                h1, m1, l1 = split3(u1)
                lhs = jnp.concatenate([h0, h0, m0, m0, h0, l0], 0).astype(BF16)
                r0 = jnp.concatenate([h0, m0, h0, m0, l0, h0], 0)
                r1 = jnp.concatenate([h1, m1, h1, m1, l1, h1], 0)
                upd = dot_tn(lhs, jnp.concatenate([r0, r1], 1).astype(BF16))
                M[top + 8 :, :] = M[top + 8 :, :] - upd[top + 8 :, :]
        inv = M[:, 128:256]
        W[k] = inv
        A[pl.ds(off, 128), :] = jnp.dot(
            inv, A[pl.ds(off, 128), :], precision=HI, preferred_element_type=F32
        )

        def trail(i, carry2):
            o2 = pl.multiple_of(i * 128, 128)
            A[pl.ds(o2, 128), :] = A[pl.ds(o2, 128), :] - dot_tn(
                A[pl.ds(off, 128), pl.ds(o2, 128)], A[pl.ds(off, 128), :], HI
            )
            return carry2

        lax.fori_loop(k + 1, 4, trail, 0)
        return carry

    lax.fori_loop(0, 4, block, 0)


STEP = 2


def finish_kernel(c_ref, f_ref, b_ref, o_ref, t_ref, A, M, W, G):
    @pl.when(pl.program_id(0) == 0)
    def _():
        for n, (k, i) in enumerate(BLOCKS):
            A[128 * k : 128 * k + 128, 128 * i : 128 * i + 128] = c_ref[n].reshape(128, 128)
        factor(A, M, W)
        share = COLS // N_ELEM
        start = pl.multiple_of(lax.axis_index("elem") * share, share)
        upper = A[pl.ds(start, share), :]
        keep = iota((share, COLS), 0) + start <= iota((share, COLS), 1)
        t_ref[...] = jnp.where(keep, upper, 0.0)
        for j in range(4):
            g = f_ref[:, 128 * j : 128 * j + 128].astype(F32)
            for i in range(j):
                g = g - jnp.dot(
                    G[:, 128 * i : 128 * i + 128],
                    A[128 * i : 128 * i + 128, 128 * j : 128 * j + 128],
                    precision=HI,
                    preferred_element_type=F32,
                )
            G[:, 128 * j : 128 * j + 128] = lax.dot_general(
                g, W[j], (((1,), (1,)), ((), ())), precision=HI, preferred_element_type=F32
            )

    for s in range(STEP):
        at = pl.multiple_of((pl.program_id(0) * STEP + s) * KROWS, KROWS)
        h, m, l = split3(G[pl.ds(at, KROWS), :])
        b = b_ref[pl.ds(at, KROWS), :]
        lhs = jnp.concatenate([b, b, b], 0).astype(BF16)
        rhs = jnp.concatenate([h, m, l], 0).astype(BF16)
        o_ref[s] = dot_tn(lhs, rhs)


def finish(gram, forces, band):
    share = COLS // N_ELEM
    whole = lambda shape: pl.BlockSpec(shape, lambda i: (0,) * len(shape))
    return pl.pallas_call(
        finish_kernel,
        grid=(CAP // STEP,),
        out_shape=(
            jax.ShapeDtypeStruct((CAP, BAND, COLS), F32),
            jax.ShapeDtypeStruct((share, COLS), F32),
        ),
        in_specs=[whole((10, 16, 8, 128)), whole((CAP * KROWS, COLS)), whole((CAP * KROWS, BAND))],
        out_specs=(
            pl.BlockSpec((STEP, BAND, COLS), lambda i: (i, 0, 0)),
            whole((share, COLS)),
        ),
        scratch_shapes=[
            pltpu.VMEM((COLS, COLS), F32),
            pltpu.VMEM((128, 256), F32),
            pltpu.VMEM((4, 128, 128), F32),
            pltpu.VMEM((CAP * KROWS, COLS), F32),
        ],
        name="factor_and_apply",
    )(gram, forces, band)


def shards(
    node_basis, stiff_terms, reduced_coords, sample_list, connectivity, node_slot, elem_device
):
    coords = jnp.broadcast_to(reduced_coords[None], (N_SNAP,) + reduced_coords.shape)
    coords = lax.all_to_all(coords, "snap", split_axis=0, concat_axis=0, tiled=True)
    coords = coords.transpose(1, 0, 2).reshape(MODES, -1)
    outgoing, place = index_call(
        sample_list.reshape(1, SAMPLED),
        connectivity,
        node_slot.reshape(512, 128),
        elem_device.reshape(1, SAMPLED),
        node_basis,
    )
    incoming = lax.all_to_all(
        outgoing.reshape(N_ELEM, 2, -1), "elem", split_axis=0, concat_axis=0, tiled=True
    )
    rows = jnp.dot(place, incoming.reshape(2 * N_ELEM, -1), preferred_element_type=F32)
    basis = rows.astype(BF16).reshape(CAP, KROWS, MODES)
    displaced = jnp.einsum(
        "ekm,ms->eks", basis, coords, preferred_element_type=F32
    ).astype(BF16)
    forces = jnp.einsum(
        "tkl,els->ekst", stiff_terms, displaced, preferred_element_type=F32
    ).astype(BF16)
    forces = forces.reshape(CAP * KROWS, COLS)
    basis = basis.reshape(CAP * KROWS, MODES)
    parts = gram_part(basis, forces)
    gram = gram_sum(parts.reshape(160, 8, 128)).reshape(10, 16, 8, 128)
    band = lax.dynamic_slice_in_dim(basis, lax.axis_index("snap") * BAND, BAND, 1)
    return finish(gram, forces, band.astype(F32))


def solution(mesh):
    placed = (P("elem", None), P(), P(None, "snap"), P(), P(), P(), P())
    return jax.shard_map(
        shards,
        mesh=mesh,
        in_specs=placed,
        out_specs=(P("elem", "snap", None), P("elem", None)),
        check_vma=False,
    )
```

```python
import jax
import jax.numpy as jnp
from jax import lax
from jax.experimental import pallas as pl
from jax.experimental.pallas import tpu as pltpu
from jax.sharding import PartitionSpec as P

F32, BF16, I32 = jnp.float32, jnp.bfloat16, jnp.int32
HI = lax.Precision.HIGHEST
MESH = pl.DeviceIdType.MESH
MODES = 512
COLS = 512
ENODES = 8
NDOF = 3
CAP = 16
SAMPLED = 512
N_ELEM = 64
N_SNAP = 4
NODE_DEV = 1024
BAND = MODES // N_SNAP
KROWS = ENODES * NDOF
BLOCKS = [(k, i) for k in range(4) for i in range(k, 4)]


def iota(shape, axis):
    return lax.broadcasted_iota(I32, shape, axis)


def hot(mask):
    return jnp.where(mask, 1.0, 0.0).astype(BF16)


def dot_nt(a, b):
    return lax.dot_general(a, b, (((1,), (1,)), ((), ())), preferred_element_type=F32)


def dot_tn(a, b, precision=None):
    return lax.dot_general(
        a, b, (((0,), (0,)), ((), ())), precision=precision, preferred_element_type=F32
    )


def dot_nn(a, b):
    return jnp.dot(a, b, preferred_element_type=F32)


def split3(x):
    h = x.astype(BF16).astype(F32)
    r = x - h
    m = r.astype(BF16).astype(F32)
    return h, m, r - m


def index_tables(sample_ref, conn_ref, slot_ref, dev_ref, ids_s, st_s, tab_s):
    me = lax.axis_index("elem")
    conn = conn_ref[...] + 1
    conn_t = jnp.concatenate([(conn >> 8).astype(F32), (conn & 255).astype(F32)], 0).astype(BF16)
    sample = sample_ref[...]
    ids = jnp.zeros((16, SAMPLED), F32)
    for part in range(4):
        picks = hot(iota((512, SAMPLED), 0) + 512 * part == sample)
        ids = ids + dot_nn(conn_t[:, 512 * part : 512 * part + 512], picks)
    ids1 = (ids[0:8] * 256.0 + ids[8:16]).astype(I32)
    live = ids1 > 0
    ids_s[...] = jnp.maximum(ids1 - 1, 0)
    table = slot_ref[...]
    tab_s[0:128, :] = (table >> 8).astype(F32).T.astype(BF16)
    tab_s[128:256, :] = (table & 255).astype(F32).T.astype(BF16)

    def lookup(p, carry):
        row = ids_s[pl.ds(p, 1), :]
        picks = hot(iota((512, SAMPLED), 0) == (row >> 7))
        found = dot_nn(tab_s[...], picks)
        here = iota((128, SAMPLED), 0) == (row & 127)
        hi = jnp.sum(jnp.where(here, found[0:128], 0.0), axis=0, keepdims=True)
        lo = jnp.sum(jnp.where(here, found[128:256], 0.0), axis=0, keepdims=True)
        st_s[pl.ds(p, 1), :] = (hi * 256.0 + lo).astype(I32)
        return carry

    lax.fori_loop(0, ENODES, lookup, 0)
    stored = st_s[...]
    owner = stored >> 10
    mine = live & (owner == me)
    has = jnp.max(jnp.where(mine, 1.0, 0.0), axis=0, keepdims=True)
    row = jnp.sum(jnp.where(mine, stored & (NODE_DEV - 1), 0), axis=0, keepdims=True)
    dev = dev_ref[...]
    dev_f = dev.astype(F32)
    dev_col = jnp.broadcast_to(dev_f, (8, SAMPLED)).T[:, 0:1]
    same = hot((dev_col == dev_f) & (iota((SAMPLED, SAMPLED), 0) < iota((SAMPLED, SAMPLED), 1)))
    counts = dot_nn(jnp.where(iota((8, SAMPLED), 0) == 0, has, 1.0).astype(BF16), same)
    rank = counts[0:1].astype(I32)
    slot = counts[1:2].astype(I32)
    q = iota((2 * N_ELEM, SAMPLED), 0)
    goes = hot(((q >> 1) == dev) & ((q & 1) == rank) & (has > 0.5))
    r8 = iota((8, SAMPLED), 0)
    vals = jnp.where(r8 == 0, (row >> 8).astype(F32), jnp.where(r8 == 1, (row & 255).astype(F32), 1.0))
    tab = dot_nt(goes, vals.astype(BF16))
    pick = (tab[:, 0:1] * 256.0 + tab[:, 1:2]).astype(I32)
    valid = tab[:, 2:3] > 0.5
    select = hot((iota((2 * N_ELEM, NODE_DEV), 1) == pick) & valid)
    here = hot((slot == iota((CAP, SAMPLED), 0)) & (dev == me))
    own = dot_nt(here, jnp.where(live, owner + 1, 0).astype(F32).astype(BF16))
    spread = hot((iota((128, CAP), 0) >> 3) == iota((128, CAP), 1))
    wide = dot_nn(spread, own.astype(BF16))
    col = jnp.sum(
        jnp.where((iota((128, ENODES), 0) & 7) == iota((128, ENODES), 1), wide, 0.0),
        axis=1,
        keepdims=True,
    )
    by_row = jnp.broadcast_to(col, (128, 128))
    by_col = by_row.T
    before = (iota((128, 128), 1) >> 3) < (iota((128, 128), 0) >> 3)
    ahead = jnp.sum(jnp.where(before & (by_row == by_col), 1.0, 0.0), axis=1, keepdims=True)
    source = ((col - 1.0) * 2.0 + ahead).astype(I32)
    place = hot((iota((128, 128), 1) == source) & (col > 0.5))
    return select, place


def local_forces(place, rows, coords, stiff, b_s, fc_s):
    n = CAP * KROWS
    rows = dot_nn(place, rows).astype(BF16)
    basis = jnp.zeros((n, MODES), F32)
    for dof in range(NDOF):
        at = iota((n, 128), 0)
        rep = hot((at // NDOF == iota((n, 128), 1)) & (at % NDOF == dof))
        basis = basis + dot_nn(rep, rows[:, MODES * dof : MODES * dof + MODES])
    basis = basis.astype(BF16)
    b_s[...] = basis
    displaced = dot_nt(basis, coords).astype(BF16)
    every = hot(iota((32, COLS), 1) % 32 == iota((32, COLS), 0))
    wide = dot_nn(displaced, every)
    wide = jnp.where(iota((n, COLS), 0) // KROWS == iota((n, COLS), 1) // 32, wide, 0.0).astype(BF16)
    fold = hot(iota((n, KROWS), 0) % KROWS == iota((n, KROWS), 1))
    by_elem = dot_tn(fold, wide).astype(BF16)
    v = dot_nn(stiff, by_elem).astype(BF16).astype(F32)
    rolled = {}
    for g in range(4):
        part = v[:, 128 * g : 128 * g + 128]
        for shift in range(4):
            rolled[shift, g] = part if shift == 0 else pltpu.roll(part, 32 * shift, 1)
    quarter = iota((KROWS, 128), 1) // 32
    for s in range(CAP):
        for c in range(4):
            out = None
            for b in range(4):
                t = 4 * c + b
                piece = rolled[(b - s) % 4, s // 4][KROWS * t : KROWS * t + KROWS, :]
                out = piece if b == 0 else jnp.where(quarter == b, piece, out)
            fc_s[KROWS * s : KROWS * s + KROWS, 128 * c : 128 * c + 128] = out
    i0 = iota((COLS, COLS), 0)
    order = hot((i0 % 32) * 16 + i0 // 32 == iota((COLS, COLS), 1))
    return basis, dot_nn(fc_s[...].astype(BF16), order).astype(BF16)


def local_gram(basis, forces, c_s):
    n = CAP * KROWS
    inner = dot_nt(basis, basis)
    inner = jnp.where(iota((n, n), 0) // KROWS == iota((n, n), 1) // KROWS, inner, 0.0)
    h, m, l = split3(inner)
    moved = dot_nn(h.astype(BF16), forces) + dot_nn(m.astype(BF16), forces) + dot_nn(l.astype(BF16), forces)
    moved = moved * (1.0 / (SAMPLED * MODES))
    h, m, l = split3(moved)
    h, m, l = h.astype(BF16), m.astype(BF16), l.astype(BF16)
    at = 0
    for k in range(4):
        left = forces[:, 128 * k : 128 * k + 128]
        part = dot_tn(left, h[:, 128 * k :]) + dot_tn(left, m[:, 128 * k :]) + dot_tn(left, l[:, 128 * k :])
        for i in range(4 - k):
            c_s[16 * at : 16 * at + 16] = part[:, 128 * i : 128 * i + 128].reshape(16, 8, 128)
            at += 1


def panel_kernel(
    sample_ref, conn_ref, slot_ref, dev_ref, coords_ref, stiff_ref, basis_ref,
    o_ref, f_ref, band_ref,
    basis_v, ids_s, st_s, tab_s, out_s, inc_s, ct_s, b_s, fc_s, c_ref, rbuf,
    load_sem, x_send, x_recv, b_send, b_recv,
    rs_send, rs_recv, own_sem, z_send, z_recv, xy_send, xy_recv, c_send, c_recv,
):
    load = pltpu.make_async_copy(basis_ref, basis_v, load_sem)
    load.start()
    e = lax.axis_index("elem")
    x = lax.axis_index("snap")
    y, z, c = e // 16, (e // 2) % 8, e % 2
    barrier = pltpu.get_barrier_semaphore()

    def greet(j, carry):
        pl.semaphore_signal(barrier, inc=1, device_id=((e + j) % N_ELEM, x), device_id_type=MESH)
        return carry

    lax.fori_loop(1, N_ELEM, greet, 0)

    def greet_x(j, carry):
        x2 = (x + 1 + j // 4) % 4
        y2 = j % 4
        pl.semaphore_signal(
            barrier, inc=1, device_id=(y2 * 16 + z * 2 + c, x2), device_id_type=MESH
        )
        return carry

    lax.fori_loop(0, 12, greet_x, 0)
    select, place = index_tables(sample_ref, conn_ref, slot_ref, dev_ref, ids_s, st_s, tab_s)
    load.wait()
    out_s[...] = dot_nn(select, basis_v[...]).astype(BF16).reshape(N_ELEM, 2, NDOF * MODES)
    pl.semaphore_wait(barrier, N_ELEM - 1 + 12)

    def rows_copy(j):
        peer = (e + j) % N_ELEM
        return pltpu.make_async_remote_copy(
            src_ref=out_s.at[peer],
            dst_ref=inc_s.at[e],
            send_sem=b_send,
            recv_sem=b_recv,
            device_id=(peer, x),
            device_id_type=MESH,
        )

    def send_rows(j, carry):
        rows_copy(j).start()
        return carry

    lax.fori_loop(1, N_ELEM, send_rows, 0)
    for j in range(1, N_SNAP):
        pltpu.make_async_remote_copy(
            src_ref=coords_ref,
            dst_ref=ct_s.at[x],
            send_sem=x_send.at[j - 1],
            recv_sem=x_recv.at[j - 1],
            device_id=(e, (x + j) % N_SNAP),
            device_id_type=MESH,
        ).start()
    inc_s[e] = out_s[e]
    ct_s[x] = coords_ref[...]
    for j in range(1, N_SNAP):
        ref = ct_s.at[(x + N_SNAP - j) % N_SNAP]
        pltpu.make_async_copy(ref, ref, x_recv.at[j - 1]).wait()
    most = inc_s.at[pl.ds(0, N_ELEM - 1)]
    pltpu.make_async_copy(most, most, b_recv).wait()
    basis, forces = local_forces(
        place,
        inc_s[...].reshape(2 * N_ELEM, NDOF * MODES),
        ct_s[...].reshape(32, MODES),
        stiff_ref[...],
        b_s,
        fc_s,
    )
    f_ref[...] = forces
    band_ref[...] = b_s[:, pl.ds(pl.multiple_of(x * BAND, BAND), BAND)]
    local_gram(basis, forces, c_ref)
    line = y * 2 + c
    k_own = (5 * z + 7) // 8
    owns = (8 * k_own) // 5 == z

    def piece(i):
        t = (i + e) % 40
        ln, k = t // 5, t % 5
        peer = (ln // 2) * 16 + ((8 * k) // 5) * 2 + ln % 2
        copy = pltpu.make_async_remote_copy(
            src_ref=c_ref.at[x * 40 + t],
            dst_ref=rbuf.at[e],
            send_sem=rs_send.at[t],
            recv_sem=rs_recv,
            device_id=(peer, x),
            device_id_type=MESH,
        )
        return copy, peer

    def scatter(i, carry):
        copy, peer = piece(i)

        @pl.when(peer != e)
        def _():
            copy.start()

        return carry

    lax.fori_loop(0, 40, scatter, 0)
    tile = x * 40 + line * 5 + k_own

    @pl.when(owns)
    def _():
        mine = pltpu.make_async_copy(c_ref.at[tile], rbuf.at[e], own_sem)
        mine.start()
        mine.wait()

        most = rbuf.at[pl.ds(0, N_ELEM - 1)]
        pltpu.make_async_copy(most, most, rs_recv).wait()
        o_ref[tile] = jnp.sum(rbuf[...], axis=0)
        for dz in range(1, 8):
            z2 = (z + dz) % 8
            pltpu.make_async_remote_copy(
                src_ref=o_ref.at[tile],
                dst_ref=o_ref.at[tile],
                send_sem=z_send.at[dz - 1],
                recv_sem=z_recv.at[k_own],
                device_id=(y * 16 + z2 * 2 + c, x),
                device_id_type=MESH,
            ).start()

    first = x * 40 + line * 5
    for k in range(5):

        @pl.when((8 * k) // 5 != z)
        def _():
            ref = o_ref.at[first + k]
            pltpu.make_async_copy(ref, ref, z_recv.at[k]).wait()

    def chunk_copy(j):
        x2, y2 = (x + j // 4) % 4, (y + j) % 4
        return pltpu.make_async_remote_copy(
            src_ref=o_ref.at[pl.ds(first, 5)],
            dst_ref=o_ref.at[pl.ds(first, 5)],
            send_sem=xy_send.at[j],
            recv_sem=xy_recv.at[x * 4 + y],
            device_id=(y2 * 16 + z * 2 + c, x2),
            device_id_type=MESH,
        )

    def send_chunk(j, carry):
        chunk_copy(j).start()
        return carry

    lax.fori_loop(1, 16, send_chunk, 0)

    def core_copy(j):
        x2, y2 = (x + j // 4) % 4, (y + j) % 4
        n = x2 * 4 + y2
        at = (x2 * 8 + y2 * 2 + c) * 5
        return n, at, pltpu.make_async_remote_copy(
            src_ref=o_ref.at[pl.ds(at, 5)],
            dst_ref=o_ref.at[pl.ds(at, 5)],
            send_sem=c_send.at[n],
            recv_sem=c_recv.at[n],
            device_id=(e + 1 - 2 * c, x),
            device_id_type=MESH,
        )

    core_copy(0)[2].start()

    def forward(j, carry):
        n, at, copy = core_copy(j)
        ref = o_ref.at[pl.ds(at, 5)]
        pltpu.make_async_copy(ref, ref, xy_recv.at[n]).wait()
        copy.start()
        return carry

    lax.fori_loop(1, 16, forward, 0)

    def finish(n, carry):
        other = (n * 2 + 1 - c) * 5
        ref = o_ref.at[pl.ds(other, 5)]
        pltpu.make_async_copy(ref, ref, c_recv.at[n]).wait()
        pltpu.make_async_copy(ref, ref, c_send.at[n]).wait()
        return carry

    lax.fori_loop(0, 16, finish, 0)

    def drain_xy(j, carry):
        ref = o_ref.at[pl.ds(first, 5)]
        pltpu.make_async_copy(ref, ref, xy_send.at[j]).wait()
        return carry

    lax.fori_loop(1, 16, drain_xy, 0)

    @pl.when(owns)
    def _():
        for dz in range(7):
            ref = o_ref.at[tile]
            pltpu.make_async_copy(ref, ref, z_send.at[dz]).wait()

    def drain_rs(i, carry):
        copy, peer = piece(i)

        @pl.when(peer != e)
        def _():
            copy.wait_send()

        return carry

    lax.fori_loop(0, 40, drain_rs, 0)


    most = inc_s.at[pl.ds(0, N_ELEM - 1)]
    pltpu.make_async_copy(most, most, b_send).wait()
    for j in range(1, N_SNAP):
        pltpu.make_async_copy(coords_ref, coords_ref, x_send.at[j - 1]).wait()


def panel_call(sample, conn, slots, dev, coords, stiff, basis):
    dma = pltpu.SemaphoreType.DMA
    vm = pl.BlockSpec(memory_space=pltpu.VMEM)
    n = CAP * KROWS
    width = NDOF * MODES
    return pl.pallas_call(
        panel_kernel,
        out_shape=(
            jax.ShapeDtypeStruct((160, 8, 128), F32),
            jax.ShapeDtypeStruct((n, COLS), BF16),
            jax.ShapeDtypeStruct((n, BAND), BF16),
        ),
        in_specs=[vm] * 6 + [pl.BlockSpec(memory_space=pl.ANY)],
        out_specs=(vm, vm, vm),
        scratch_shapes=[
            pltpu.VMEM((NODE_DEV, width), BF16),
            pltpu.VMEM((ENODES, SAMPLED), I32),
            pltpu.VMEM((ENODES, SAMPLED), I32),
            pltpu.VMEM((256, 512), BF16),
            pltpu.VMEM((N_ELEM, 2, width), BF16),
            pltpu.VMEM((N_ELEM, 2, width), BF16),
            pltpu.VMEM((N_SNAP, 8, MODES), BF16),
            pltpu.VMEM((n, MODES), BF16),
            pltpu.VMEM((n, COLS), F32),
            pltpu.VMEM((160, 8, 128), F32),
            pltpu.VMEM((N_ELEM, 8, 128), F32),
            dma,
            dma((3,)),
            dma((3,)),
            dma,
            dma,
            dma((40,)),
            dma,
            dma,
            dma((7,)),
            dma((5,)),
            dma((16,)),
            dma((16,)),
            dma((16,)),
            dma((16,)),
        ],
        compiler_params=pltpu.CompilerParams(collective_id=1, has_side_effects=True),
        name="panel_exchange",
    )(sample, conn, slots, dev, coords, stiff, basis)


def panel(p0, p1, lane):
    def rep(v, i):
        return jnp.broadcast_to(v[i : i + 1, :], (8, 128))

    cols = [jnp.broadcast_to(p0[:, lane + j : lane + j + 1], (8, 128)) for j in range(8)]
    a = {(i, j): rep(cols[j], i) for j in range(8) for i in range(j + 1)}
    rows = [[rep(p0, i), rep(p1, i)] for i in range(8)]
    sub = iota((8, 128), 0)
    out = [None, None]
    for k in range(8):
        r = lax.rsqrt(a[k, k])
        u = {j: a[k, j] * r for j in range(k + 1, 8)}
        rows[k] = [v * r for v in rows[k]]
        for i in range(k + 1, 8):
            for j in range(i, 8):
                a[i, j] = a[i, j] - u[i] * u[j]
            rows[i] = [v - u[i] * w for v, w in zip(rows[i], rows[k])]
        for c in range(2):
            out[c] = rows[k][c] if k == 0 else jnp.where(sub == k, rows[k][c], out[c])
    return out


def factor(A, M, W):
    eye = jnp.where(iota((128, 128), 0) == iota((128, 128), 1), 1.0, 0.0)

    def block(k, carry):
        off = pl.multiple_of(k * 128, 128)
        M[:, 0:128] = A[pl.ds(off, 128), pl.ds(off, 128)]
        M[:, 128:256] = eye
        for p in range(16):
            top = 8 * p
            u0, u1 = panel(M[top : top + 8, 0:128], M[top : top + 8, 128:256], top)
            M[top : top + 8, 0:128] = u0
            M[top : top + 8, 128:256] = u1
            if p < 15:
                h0, m0, l0 = split3(u0)
                h1, m1, l1 = split3(u1)
                lhs = jnp.concatenate([h0, h0, m0, m0, h0, l0], 0).astype(BF16)
                r0 = jnp.concatenate([h0, m0, h0, m0, l0, h0], 0)
                r1 = jnp.concatenate([h1, m1, h1, m1, l1, h1], 0)
                upd = dot_tn(lhs, jnp.concatenate([r0, r1], 1).astype(BF16))
                M[top + 8 :, :] = M[top + 8 :, :] - upd[top + 8 :, :]
        inv = M[:, 128:256]
        W[k] = inv
        A[pl.ds(off, 128), :] = jnp.dot(
            inv, A[pl.ds(off, 128), :], precision=HI, preferred_element_type=F32
        )

        def trail(i, carry2):
            o2 = pl.multiple_of(i * 128, 128)
            A[pl.ds(o2, 128), :] = A[pl.ds(o2, 128), :] - dot_tn(
                A[pl.ds(off, 128), pl.ds(o2, 128)], A[pl.ds(off, 128), :], HI
            )
            return carry2

        lax.fori_loop(k + 1, 4, trail, 0)
        return carry

    lax.fori_loop(0, 4, block, 0)


STEP = 2


def finish_kernel(c_ref, f_ref, b_ref, o_ref, t_ref, A, M, W, G):
    @pl.when(pl.program_id(0) == 0)
    def _():
        for n, (k, i) in enumerate(BLOCKS):
            A[128 * k : 128 * k + 128, 128 * i : 128 * i + 128] = c_ref[n].reshape(128, 128)
        factor(A, M, W)
        share = COLS // N_ELEM
        start = pl.multiple_of(lax.axis_index("elem") * share, share)
        upper = A[pl.ds(start, share), :]
        keep = iota((share, COLS), 0) + start <= iota((share, COLS), 1)
        t_ref[...] = jnp.where(keep, upper, 0.0)
        for j in range(4):
            g = f_ref[:, 128 * j : 128 * j + 128].astype(F32)
            for i in range(j):
                g = g - jnp.dot(
                    G[:, 128 * i : 128 * i + 128],
                    A[128 * i : 128 * i + 128, 128 * j : 128 * j + 128],
                    precision=HI,
                    preferred_element_type=F32,
                )
            G[:, 128 * j : 128 * j + 128] = lax.dot_general(
                g, W[j], (((1,), (1,)), ((), ())), precision=HI, preferred_element_type=F32
            )

    for s in range(STEP):
        at = pl.multiple_of((pl.program_id(0) * STEP + s) * KROWS, KROWS)
        h, m, l = split3(G[pl.ds(at, KROWS), :])
        b = b_ref[pl.ds(at, KROWS), :].astype(F32)
        lhs = jnp.concatenate([b, b, b], 0).astype(BF16)
        rhs = jnp.concatenate([h, m, l], 0).astype(BF16)
        o_ref[s] = dot_tn(lhs, rhs)


def finish(gram, forces, band):
    share = COLS // N_ELEM
    whole = lambda shape: pl.BlockSpec(shape, lambda i: (0,) * len(shape))
    return pl.pallas_call(
        finish_kernel,
        grid=(CAP // STEP,),
        out_shape=(
            jax.ShapeDtypeStruct((CAP, BAND, COLS), F32),
            jax.ShapeDtypeStruct((share, COLS), F32),
        ),
        in_specs=[whole((10, 16, 8, 128)), whole((CAP * KROWS, COLS)), whole((CAP * KROWS, BAND))],
        out_specs=(
            pl.BlockSpec((STEP, BAND, COLS), lambda i: (i, 0, 0)),
            whole((share, COLS)),
        ),
        scratch_shapes=[
            pltpu.VMEM((COLS, COLS), F32),
            pltpu.VMEM((128, 256), F32),
            pltpu.VMEM((4, 128, 128), F32),
            pltpu.VMEM((CAP * KROWS, COLS), F32),
        ],
        name="factor_and_apply",
    )(gram, forces, band)


def shards(
    node_basis, stiff_terms, reduced_coords, sample_list, connectivity, node_slot, elem_device
):
    gram, forces, band = panel_call(
        sample_list.reshape(1, SAMPLED),
        connectivity.T,
        node_slot.reshape(512, 128),
        elem_device.reshape(1, SAMPLED),
        reduced_coords.T,
        stiff_terms.reshape(16 * KROWS, KROWS),
        node_basis,
    )
    return finish(gram.reshape(10, 16, 8, 128), forces, band)


def solution(mesh):
    placed = (P("elem", None), P(), P(None, "snap"), P(), P(), P(), P())
    return jax.shard_map(
        shards,
        mesh=mesh,
        in_specs=placed,
        out_specs=(P("elem", "snap", None), P("elem", None)),
        check_vma=False,
    )
```

```python
import jax
import jax.numpy as jnp
from jax import lax
from jax.experimental import pallas as pl
from jax.experimental.pallas import tpu as pltpu
from jax.sharding import PartitionSpec as P

F32, BF16, I32 = jnp.float32, jnp.bfloat16, jnp.int32
HI = lax.Precision.HIGHEST
MESH = pl.DeviceIdType.MESH
MODES = 512
COLS = 512
ENODES = 8
NDOF = 3
CAP = 16
SAMPLED = 512
N_ELEM = 64
N_SNAP = 4
NODE_DEV = 1024
BAND = MODES // N_SNAP
KROWS = ENODES * NDOF
BLOCKS = [(k, i) for k in range(4) for i in range(k, 4)]


def iota(shape, axis):
    return lax.broadcasted_iota(I32, shape, axis)


def hot(mask):
    return jnp.where(mask, 1.0, 0.0).astype(BF16)


def dot_nt(a, b):
    return lax.dot_general(a, b, (((1,), (1,)), ((), ())), preferred_element_type=F32)


def dot_tn(a, b, precision=None):
    return lax.dot_general(
        a, b, (((0,), (0,)), ((), ())), precision=precision, preferred_element_type=F32
    )


def dot_nn(a, b):
    return jnp.dot(a, b, preferred_element_type=F32)


def split3(x):
    h = x.astype(BF16).astype(F32)
    r = x - h
    m = r.astype(BF16).astype(F32)
    return h, m, r - m


def index_tables(sample_ref, conn_ref, slot_ref, dev_ref, ids_s, st_s, tab_s):
    me = lax.axis_index("elem")
    conn = conn_ref[...] + 1
    conn_t = jnp.concatenate([(conn >> 8).astype(F32), (conn & 255).astype(F32)], 0).astype(BF16)
    sample = sample_ref[...]
    ids = jnp.zeros((16, SAMPLED), F32)
    for part in range(4):
        picks = hot(iota((512, SAMPLED), 0) + 512 * part == sample)
        ids = ids + dot_nn(conn_t[:, 512 * part : 512 * part + 512], picks)
    ids1 = (ids[0:8] * 256.0 + ids[8:16]).astype(I32)
    live = ids1 > 0
    ids_s[...] = jnp.maximum(ids1 - 1, 0)
    table = slot_ref[...]
    tab_s[0:128, :] = (table >> 8).astype(F32).T.astype(BF16)
    tab_s[128:256, :] = (table & 255).astype(F32).T.astype(BF16)

    def lookup(p, carry):
        row = ids_s[pl.ds(p, 1), :]
        picks = hot(iota((512, SAMPLED), 0) == (row >> 7))
        found = dot_nn(tab_s[...], picks)
        here = iota((128, SAMPLED), 0) == (row & 127)
        hi = jnp.sum(jnp.where(here, found[0:128], 0.0), axis=0, keepdims=True)
        lo = jnp.sum(jnp.where(here, found[128:256], 0.0), axis=0, keepdims=True)
        st_s[pl.ds(p, 1), :] = (hi * 256.0 + lo).astype(I32)
        return carry

    lax.fori_loop(0, ENODES, lookup, 0)
    stored = st_s[...]
    owner = stored >> 10
    mine = live & (owner == me)
    has = jnp.max(jnp.where(mine, 1.0, 0.0), axis=0, keepdims=True)
    row = jnp.sum(jnp.where(mine, stored & (NODE_DEV - 1), 0), axis=0, keepdims=True)
    dev = dev_ref[...]
    dev_f = dev.astype(F32)
    dev_col = jnp.broadcast_to(dev_f, (8, SAMPLED)).T[:, 0:1]
    same = hot((dev_col == dev_f) & (iota((SAMPLED, SAMPLED), 0) < iota((SAMPLED, SAMPLED), 1)))
    counts = dot_nn(jnp.where(iota((8, SAMPLED), 0) == 0, has, 1.0).astype(BF16), same)
    rank = counts[0:1].astype(I32)
    slot = counts[1:2].astype(I32)
    q = iota((2 * N_ELEM, SAMPLED), 0)
    goes = hot(((q >> 1) == dev) & ((q & 1) == rank) & (has > 0.5))
    r8 = iota((8, SAMPLED), 0)
    vals = jnp.where(r8 == 0, (row >> 8).astype(F32), jnp.where(r8 == 1, (row & 255).astype(F32), 1.0))
    tab = dot_nt(goes, vals.astype(BF16))
    pick = (tab[:, 0:1] * 256.0 + tab[:, 1:2]).astype(I32)
    valid = tab[:, 2:3] > 0.5
    select = hot((iota((2 * N_ELEM, NODE_DEV), 1) == pick) & valid)
    here = hot((slot == iota((CAP, SAMPLED), 0)) & (dev == me))
    own = dot_nt(here, jnp.where(live, owner + 1, 0).astype(F32).astype(BF16))
    spread = hot((iota((128, CAP), 0) >> 3) == iota((128, CAP), 1))
    wide = dot_nn(spread, own.astype(BF16))
    col = jnp.sum(
        jnp.where((iota((128, ENODES), 0) & 7) == iota((128, ENODES), 1), wide, 0.0),
        axis=1,
        keepdims=True,
    )
    by_row = jnp.broadcast_to(col, (128, 128))
    by_col = by_row.T
    before = (iota((128, 128), 1) >> 3) < (iota((128, 128), 0) >> 3)
    ahead = jnp.sum(jnp.where(before & (by_row == by_col), 1.0, 0.0), axis=1, keepdims=True)
    source = ((col - 1.0) * 2.0 + ahead).astype(I32)
    place = hot((iota((128, 128), 1) == source) & (col > 0.5))
    return select, place


def local_forces(place, rows, coords, stiff, b_s, fc_s):
    n = CAP * KROWS
    rows = dot_nn(place, rows).astype(BF16)
    basis = jnp.zeros((n, MODES), F32)
    for dof in range(NDOF):
        at = iota((n, 128), 0)
        rep = hot((at // NDOF == iota((n, 128), 1)) & (at % NDOF == dof))
        basis = basis + dot_nn(rep, rows[:, MODES * dof : MODES * dof + MODES])
    basis = basis.astype(BF16)
    b_s[...] = basis
    displaced = dot_nt(basis, coords).astype(BF16)
    every = hot(iota((32, COLS), 1) % 32 == iota((32, COLS), 0))
    wide = dot_nn(displaced, every)
    wide = jnp.where(iota((n, COLS), 0) // KROWS == iota((n, COLS), 1) // 32, wide, 0.0).astype(BF16)
    fold = hot(iota((n, KROWS), 0) % KROWS == iota((n, KROWS), 1))
    by_elem = dot_tn(fold, wide).astype(BF16)
    v = dot_nn(stiff, by_elem).astype(BF16).astype(F32)
    rolled = {}
    for g in range(4):
        part = v[:, 128 * g : 128 * g + 128]
        for shift in range(4):
            rolled[shift, g] = part if shift == 0 else pltpu.roll(part, 32 * shift, 1)
    quarter = iota((KROWS, 128), 1) // 32
    for s in range(CAP):
        for c in range(4):
            out = None
            for b in range(4):
                t = 4 * c + b
                piece = rolled[(b - s) % 4, s // 4][KROWS * t : KROWS * t + KROWS, :]
                out = piece if b == 0 else jnp.where(quarter == b, piece, out)
            fc_s[KROWS * s : KROWS * s + KROWS, 128 * c : 128 * c + 128] = out
    i0 = iota((COLS, COLS), 0)
    order = hot((i0 % 32) * 16 + i0 // 32 == iota((COLS, COLS), 1))
    return basis, dot_nn(fc_s[...].astype(BF16), order).astype(BF16)


def local_gram(basis, forces, c_s):
    n = CAP * KROWS
    inner = dot_nt(basis, basis)
    inner = jnp.where(iota((n, n), 0) // KROWS == iota((n, n), 1) // KROWS, inner, 0.0)
    h, m, l = split3(inner)
    moved = dot_nn(h.astype(BF16), forces) + dot_nn(m.astype(BF16), forces) + dot_nn(l.astype(BF16), forces)
    moved = moved * (1.0 / (SAMPLED * MODES))
    h, m, l = split3(moved)
    h, m, l = h.astype(BF16), m.astype(BF16), l.astype(BF16)
    at = 0
    for k in range(4):
        left = forces[:, 128 * k : 128 * k + 128]
        part = dot_tn(left, h[:, 128 * k :]) + dot_tn(left, m[:, 128 * k :]) + dot_tn(left, l[:, 128 * k :])
        for i in range(4 - k):
            c_s[16 * at : 16 * at + 16] = part[:, 128 * i : 128 * i + 128].reshape(16, 8, 128)
            at += 1


def panel_kernel(
    sample_ref, conn_ref, slot_ref, dev_ref, coords_ref, stiff_ref, basis_ref,
    o_ref, f_ref, band_ref,
    basis_v, ids_s, st_s, tab_s, out_s, inc_s, ct_s, b_s, fc_s, c_ref, rbuf,
    load_sem, x_send, x_recv, b_send, b_recv,
    rs_send, rs_recv, own_sem, z_send, z_recv, xy_send, xy_recv, c_send, c_recv,
):
    load = pltpu.make_async_copy(basis_ref, basis_v, load_sem)
    load.start()
    e = lax.axis_index("elem")
    x = lax.axis_index("snap")
    y, z, c = e // 16, (e // 2) % 8, e % 2
    barrier = pltpu.get_barrier_semaphore()

    def greet(j, carry):
        pl.semaphore_signal(barrier, inc=1, device_id=((e + j) % N_ELEM, x), device_id_type=MESH)
        return carry

    lax.fori_loop(1, N_ELEM, greet, 0)

    def greet_x(j, carry):
        x2 = (x + 1 + j // 4) % 4
        y2 = j % 4
        pl.semaphore_signal(
            barrier, inc=1, device_id=(y2 * 16 + z * 2 + c, x2), device_id_type=MESH
        )
        return carry

    lax.fori_loop(0, 12, greet_x, 0)
    select, place = index_tables(sample_ref, conn_ref, slot_ref, dev_ref, ids_s, st_s, tab_s)
    load.wait()
    out_s[...] = dot_nn(select, basis_v[...]).astype(BF16).reshape(N_ELEM, 2, NDOF * MODES)
    pl.semaphore_wait(barrier, N_ELEM - 1 + 12)

    def rows_copy(j):
        peer = (e + j) % N_ELEM
        return pltpu.make_async_remote_copy(
            src_ref=out_s.at[peer],
            dst_ref=inc_s.at[e],
            send_sem=b_send,
            recv_sem=b_recv,
            device_id=(peer, x),
            device_id_type=MESH,
        )

    def send_rows(j, carry):
        rows_copy(j).start()
        return carry

    lax.fori_loop(1, N_ELEM, send_rows, 0)
    for j in range(1, N_SNAP):
        pltpu.make_async_remote_copy(
            src_ref=coords_ref,
            dst_ref=ct_s.at[x],
            send_sem=x_send.at[j - 1],
            recv_sem=x_recv.at[j - 1],
            device_id=(e, (x + j) % N_SNAP),
            device_id_type=MESH,
        ).start()
    inc_s[e] = out_s[e]
    ct_s[x] = coords_ref[...]
    for j in range(1, N_SNAP):
        ref = ct_s.at[(x + N_SNAP - j) % N_SNAP]
        pltpu.make_async_copy(ref, ref, x_recv.at[j - 1]).wait()
    most = inc_s.at[pl.ds(0, N_ELEM - 1)]
    pltpu.make_async_copy(most, most, b_recv).wait()
    basis, forces = local_forces(
        place,
        inc_s[...].reshape(2 * N_ELEM, NDOF * MODES),
        ct_s[...].reshape(32, MODES),
        stiff_ref[...],
        b_s,
        fc_s,
    )
    f_ref[...] = forces
    band_ref[...] = b_s[:, pl.ds(pl.multiple_of(x * BAND, BAND), BAND)]
    local_gram(basis, forces, c_ref)
    line = y * 2 + c
    k_own = (5 * z + 7) // 8
    owns = (8 * k_own) // 5 == z

    def piece(i):
        t = (i + e) % 40
        ln, k = t // 5, t % 5
        peer = (ln // 2) * 16 + ((8 * k) // 5) * 2 + ln % 2
        copy = pltpu.make_async_remote_copy(
            src_ref=c_ref.at[x * 40 + t],
            dst_ref=rbuf.at[e],
            send_sem=rs_send.at[t],
            recv_sem=rs_recv,
            device_id=(peer, x),
            device_id_type=MESH,
        )
        return copy, peer

    def scatter(i, carry):
        copy, peer = piece(i)

        @pl.when(peer != e)
        def _():
            copy.start()

        return carry

    lax.fori_loop(0, 40, scatter, 0)
    tile = x * 40 + line * 5 + k_own

    @pl.when(owns)
    def _():
        mine = pltpu.make_async_copy(c_ref.at[tile], rbuf.at[e], own_sem)
        mine.start()
        mine.wait()

        most = rbuf.at[pl.ds(0, N_ELEM - 1)]
        pltpu.make_async_copy(most, most, rs_recv).wait()
        o_ref[tile] = jnp.sum(rbuf[...], axis=0)
        for dz in range(1, 8):
            z2 = (z + dz) % 8
            pltpu.make_async_remote_copy(
                src_ref=o_ref.at[tile],
                dst_ref=o_ref.at[tile],
                send_sem=z_send.at[dz - 1],
                recv_sem=z_recv.at[k_own],
                device_id=(y * 16 + z2 * 2 + c, x),
                device_id_type=MESH,
            ).start()

    first = x * 40 + line * 5
    for k in range(5):

        @pl.when((8 * k) // 5 != z)
        def _():
            ref = o_ref.at[first + k]
            pltpu.make_async_copy(ref, ref, z_recv.at[k]).wait()

    def chunk_copy(j):
        x2, y2 = (x + j // 4) % 4, (y + j) % 4
        return pltpu.make_async_remote_copy(
            src_ref=o_ref.at[pl.ds(first, 5)],
            dst_ref=o_ref.at[pl.ds(first, 5)],
            send_sem=xy_send.at[j],
            recv_sem=xy_recv.at[x * 4 + y],
            device_id=(y2 * 16 + z * 2 + c, x2),
            device_id_type=MESH,
        )

    def send_chunk(j, carry):
        chunk_copy(j).start()
        return carry

    lax.fori_loop(1, 16, send_chunk, 0)

    def core_copy(j):
        x2, y2 = (x + j // 4) % 4, (y + j) % 4
        n = x2 * 4 + y2
        at = (x2 * 8 + y2 * 2 + c) * 5
        return n, at, pltpu.make_async_remote_copy(
            src_ref=o_ref.at[pl.ds(at, 5)],
            dst_ref=o_ref.at[pl.ds(at, 5)],
            send_sem=c_send.at[n],
            recv_sem=c_recv.at[n],
            device_id=(e + 1 - 2 * c, x),
            device_id_type=MESH,
        )

    core_copy(0)[2].start()

    def forward(j, carry):
        n, at, copy = core_copy(j)
        ref = o_ref.at[pl.ds(at, 5)]
        pltpu.make_async_copy(ref, ref, xy_recv.at[n]).wait()
        copy.start()
        return carry

    lax.fori_loop(1, 16, forward, 0)

    def finish(n, carry):
        other = (n * 2 + 1 - c) * 5
        ref = o_ref.at[pl.ds(other, 5)]
        pltpu.make_async_copy(ref, ref, c_recv.at[n]).wait()
        pltpu.make_async_copy(ref, ref, c_send.at[n]).wait()
        return carry

    lax.fori_loop(0, 16, finish, 0)

    def drain_xy(j, carry):
        ref = o_ref.at[pl.ds(first, 5)]
        pltpu.make_async_copy(ref, ref, xy_send.at[j]).wait()
        return carry

    lax.fori_loop(1, 16, drain_xy, 0)

    @pl.when(owns)
    def _():
        for dz in range(7):
            ref = o_ref.at[tile]
            pltpu.make_async_copy(ref, ref, z_send.at[dz]).wait()

    def drain_rs(i, carry):
        copy, peer = piece(i)

        @pl.when(peer != e)
        def _():
            copy.wait_send()

        return carry

    lax.fori_loop(0, 40, drain_rs, 0)


    most = inc_s.at[pl.ds(0, N_ELEM - 1)]
    pltpu.make_async_copy(most, most, b_send).wait()
    for j in range(1, N_SNAP):
        pltpu.make_async_copy(coords_ref, coords_ref, x_send.at[j - 1]).wait()


def panel_call(sample, conn, slots, dev, coords, stiff, basis):
    dma = pltpu.SemaphoreType.DMA
    vm = pl.BlockSpec(memory_space=pltpu.VMEM)
    n = CAP * KROWS
    width = NDOF * MODES
    return pl.pallas_call(
        panel_kernel,
        out_shape=(
            jax.ShapeDtypeStruct((160, 8, 128), F32),
            jax.ShapeDtypeStruct((n, COLS), BF16),
            jax.ShapeDtypeStruct((n, BAND), BF16),
        ),
        in_specs=[vm] * 6 + [pl.BlockSpec(memory_space=pl.ANY)],
        out_specs=(vm, vm, vm),
        scratch_shapes=[
            pltpu.VMEM((NODE_DEV, width), BF16),
            pltpu.VMEM((ENODES, SAMPLED), I32),
            pltpu.VMEM((ENODES, SAMPLED), I32),
            pltpu.VMEM((256, 512), BF16),
            pltpu.VMEM((N_ELEM, 2, width), BF16),
            pltpu.VMEM((N_ELEM, 2, width), BF16),
            pltpu.VMEM((N_SNAP, 8, MODES), BF16),
            pltpu.VMEM((n, MODES), BF16),
            pltpu.VMEM((n, COLS), F32),
            pltpu.VMEM((160, 8, 128), F32),
            pltpu.VMEM((N_ELEM, 8, 128), F32),
            dma,
            dma((3,)),
            dma((3,)),
            dma,
            dma,
            dma((40,)),
            dma,
            dma,
            dma((7,)),
            dma((5,)),
            dma((16,)),
            dma((16,)),
            dma((16,)),
            dma((16,)),
        ],
        compiler_params=pltpu.CompilerParams(collective_id=1, has_side_effects=True),
        name="panel_exchange",
    )(sample, conn, slots, dev, coords, stiff, basis)


def split2(x):
    hi = x.astype(BF16)
    return hi, (x - hi.astype(F32)).astype(BF16)


def rep(v, i):
    return jnp.broadcast_to(v[i : i + 1, :], (8, 128))


def spread_cols(v, lane):
    return [jnp.broadcast_to(v[:, lane + j : lane + j + 1], (8, 128)) for j in range(8)]


def panel(diag, p0, p1, below, ahead):
    sub = iota((8, 128), 0)
    out = [None, None]
    for k in range(8):
        r = lax.rsqrt(rep(diag[k], k))
        c = diag[k] * r
        at = {j: rep(c, j) for j in range(k + 1, 8)}
        for j in range(k + 1, 8):
            diag[j] = diag[j] - c * at[j]
        x0, x1 = rep(p0, k) * r, rep(p1, k) * r
        p0, p1 = p0 - c * x0, p1 - c * x1
        if k == 0:
            out = [x0, x1]
        else:
            out = [jnp.where(sub == k, x, o) for x, o in zip((x0, x1), out)]
        if below is not None:
            c2 = below[k] * r
            for j in range(k + 1, 8):
                below[j] = below[j] - c2 * at[j]
            for j in range(8):
                ahead[j] = ahead[j] - c2 * rep(c2, j)
    return out, ahead


def product6(a, b):
    ah, am, al = (v.astype(BF16) for v in split3(a))
    bh, bm, bl = (v.astype(BF16) for v in split3(b))
    out = dot_nn(jnp.concatenate([ah, am], 1), jnp.concatenate([bh, bh], 0))
    out = out + dot_nn(jnp.concatenate([ah, am], 1), jnp.concatenate([bm, bm], 0))
    return out + dot_nn(jnp.concatenate([ah, al], 1), jnp.concatenate([bl, bh], 0))


def product6_tn(a, b):
    ah, am, al = (v.astype(BF16) for v in split3(a))
    bh, bm, bl = (v.astype(BF16) for v in split3(b))
    out = dot_tn(jnp.concatenate([ah, am], 0), jnp.concatenate([bh, bh], 0))
    out = out + dot_tn(jnp.concatenate([ah, am], 0), jnp.concatenate([bm, bm], 0))
    return out + dot_tn(jnp.concatenate([ah, al], 0), jnp.concatenate([bl, bh], 0))


def finish_kernel(c_ref, f_ref, b_ref, o_ref, t_ref, A, M, uh, um, gf, gh, gm, bf, o_v, sems):
    for n, (k, i) in enumerate(BLOCKS):
        A[128 * k : 128 * k + 128, 128 * i : 128 * i + 128] = c_ref[n].reshape(128, 128)
    for k in range(1, 4):
        A[128 * k : 128 * k + 128, 0 : 128 * k] = jnp.zeros((128, 128 * k), F32)
    bf[...] = b_ref[...].astype(F32)
    eye = jnp.where(iota((128, 128), 0) == iota((128, 128), 1), 1.0, 0.0)
    upper = iota((128, 128), 0) <= iota((128, 128), 1)

    def across(k, i, inv):
        def run():
            rows, cols = slice(128 * k, 128 * k + 128), slice(128 * i, 128 * i + 128)
            u = product6(inv, A[rows, cols])
            A[rows, cols] = u
            uh[rows, cols], um[rows, cols] = split2(u)

        return run

    def trail(k, i, j):
        def run():
            done = slice(128 * k, 128 * k + 128)
            rows, cols = slice(128 * i, 128 * i + 128), slice(128 * j, 128 * j + 128)
            A[rows, cols] = A[rows, cols] - product6_tn(A[done, rows], A[done, cols])

        return run

    def solve(k, r, inv_h, inv_m):
        def run():
            rows = slice(128 * r, 128 * r + 128)
            cols = slice(128 * k, 128 * k + 128)
            g = f_ref[rows, cols].astype(F32)
            if k:
                done = slice(0, 128 * k)
                g = g - dot_nn(gh[rows, done], uh[done, cols])
                g = g - dot_nn(gh[rows, done], um[done, cols])
                g = g - dot_nn(gm[rows, done], uh[done, cols])
            h, m = split2(g)
            g = dot_nt(h, inv_h) + dot_nt(h, inv_m) + dot_nt(m, inv_h)
            gf[rows, cols] = g
            h, m = split2(g)
            gh[rows, cols] = h
            gm[rows, cols] = m

        return run

    def apply(k, s):
        def run():
            rows = slice(KROWS * s, KROWS * s + KROWS)
            cols = slice(128 * k, 128 * k + 128)
            g = gf[rows, cols]
            h = g.astype(BF16).astype(F32)
            b = bf[rows, :]
            lhs = jnp.concatenate([b, b], 0).astype(BF16)
            rhs = jnp.concatenate([h, g - h], 0).astype(BF16)
            o_v[s, :, cols] = dot_tn(lhs, rhs)

        return run

    def store(k):
        cols = pl.ds(128 * k, 128)
        return pltpu.make_async_copy(o_v.at[:, :, cols], o_ref.at[:, :, cols], sems.at[k])

    fill = []
    for k in range(4):
        lo = 128 * k
        M[:, 0:128] = A[lo : lo + 128, lo : lo + 128]
        M[:, 128:256] = eye
        per = -(-len(fill) // 16)
        diag = spread_cols(M[0:8, 0:128], 0)
        for p in range(16):
            top = 8 * p
            below = ahead = None
            if p < 15:
                under = M[top + 8 : top + 16, 0:128]
                below, ahead = spread_cols(under, top), spread_cols(under, top + 8)
            (u0, u1), diag = panel(
                diag, M[top : top + 8, 0:128], M[top : top + 8, 128:256], below, ahead
            )
            M[top : top + 8, 0:128] = u0
            M[top : top + 8, 128:256] = u1
            if p < 15:
                h0, m0, l0 = split3(u0)
                h1, m1, l1 = split3(u1)
                lhs = jnp.concatenate([h0, h0, m0, m0, h0, l0], 0).astype(BF16)
                r0 = jnp.concatenate([h0, m0, h0, m0, l0, h0], 0)
                r1 = jnp.concatenate([h1, m1, h1, m1, l1, h1], 0)
                upd = dot_tn(lhs, jnp.concatenate([r0, r1], 1).astype(BF16))
                if p < 12:
                    M[top + 8 :, :] = M[top + 8 :, :] - upd[top + 8 :, :]
                else:
                    later = iota((32, 256), 0) + 96 >= top + 8
                    M[96:, :] = M[96:, :] - jnp.where(later, upd[96:, :], 0.0)
            for job in fill[per * p : per * p + per]:
                job()
        inv = M[:, 128:256]
        A[lo : lo + 128, lo : lo + 128] = jnp.where(upper, M[:, 0:128], 0.0)
        inv_h, inv_m = split2(inv)
        fill = []
        if k < 3:
            across(k, k + 1, inv)()
            trail(k, k + 1, k + 1)()
            fill += [across(k, i, inv) for i in range(k + 2, 4)]
            fill += [trail(k, i, j) for i in range(k + 1, 4) for j in range(i, 4) if j > k + 1]
        fill += [solve(k, r, inv_h, inv_m) for r in range(3)]
        fill += [apply(k, s) for s in range(CAP)]
        fill.append(store(k).start)
    for job in fill:
        job()
    share = COLS // N_ELEM
    start = pl.multiple_of(lax.axis_index("elem") * share, share)
    t_ref[...] = A[pl.ds(start, share), :]
    for k in range(4):
        store(k).wait()


def finish(gram, forces, band):
    share = COLS // N_ELEM
    rows = CAP * KROWS
    vm = pl.BlockSpec(memory_space=pltpu.VMEM)
    return pl.pallas_call(
        finish_kernel,
        out_shape=(
            jax.ShapeDtypeStruct((CAP, BAND, COLS), F32),
            jax.ShapeDtypeStruct((share, COLS), F32),
        ),
        in_specs=[vm, vm, vm],
        out_specs=(pl.BlockSpec(memory_space=pl.ANY), vm),
        scratch_shapes=[
            pltpu.VMEM((COLS, COLS), F32),
            pltpu.VMEM((128, 256), F32),
            pltpu.VMEM((COLS, COLS), BF16),
            pltpu.VMEM((COLS, COLS), BF16),
            pltpu.VMEM((rows, COLS), F32),
            pltpu.VMEM((rows, COLS), BF16),
            pltpu.VMEM((rows, COLS), BF16),
            pltpu.VMEM((rows, BAND), F32),
            pltpu.VMEM((CAP, BAND, COLS), F32),
            pltpu.SemaphoreType.DMA((4,)),
        ],
        name="factor_and_apply",
    )(gram, forces, band)


def shards(
    node_basis, stiff_terms, reduced_coords, sample_list, connectivity, node_slot, elem_device
):
    gram, forces, band = panel_call(
        sample_list.reshape(1, SAMPLED),
        connectivity.T,
        node_slot.reshape(512, 128),
        elem_device.reshape(1, SAMPLED),
        reduced_coords.T,
        stiff_terms.reshape(16 * KROWS, KROWS),
        node_basis,
    )
    return finish(gram.reshape(10, 16, 8, 128), forces, band)


def solution(mesh):
    placed = (P("elem", None), P(), P(None, "snap"), P(), P(), P(), P())
    return jax.shard_map(
        shards,
        mesh=mesh,
        in_specs=placed,
        out_specs=(P("elem", "snap", None), P("elem", None)),
        check_vma=False,
    )
```

```python
import jax
import jax.numpy as jnp
from jax import lax
from jax.experimental import pallas as pl
from jax.experimental.pallas import tpu as pltpu
from jax.sharding import PartitionSpec as P

F32, BF16, I32 = jnp.float32, jnp.bfloat16, jnp.int32
HI = lax.Precision.HIGHEST
MESH = pl.DeviceIdType.MESH
MODES = 512
COLS = 512
ENODES = 8
NDOF = 3
CAP = 16
SAMPLED = 512
N_ELEM = 64
N_SNAP = 4
NODE_DEV = 1024
BAND = MODES // N_SNAP
KROWS = ENODES * NDOF
BLOCKS = [(k, i) for k in range(4) for i in range(k, 4)]


def iota(shape, axis):
    return lax.broadcasted_iota(I32, shape, axis)


def hot(mask):
    return jnp.where(mask, 1.0, 0.0).astype(BF16)


def dot_nt(a, b):
    return lax.dot_general(a, b, (((1,), (1,)), ((), ())), preferred_element_type=F32)


def dot_tn(a, b, precision=None):
    return lax.dot_general(
        a, b, (((0,), (0,)), ((), ())), precision=precision, preferred_element_type=F32
    )


def dot_nn(a, b):
    return jnp.dot(a, b, preferred_element_type=F32)


def split3(x):
    h = x.astype(BF16).astype(F32)
    r = x - h
    m = r.astype(BF16).astype(F32)
    return h, m, r - m


def index_tables(sample_ref, conn_ref, slot_ref, dev_ref, ids_s, st_s, tab_s):
    me = lax.axis_index("elem")
    conn = conn_ref[...] + 1
    conn_t = jnp.concatenate([(conn >> 8).astype(F32), (conn & 255).astype(F32)], 0).astype(BF16)
    sample = sample_ref[...]
    ids = jnp.zeros((16, SAMPLED), F32)
    for part in range(4):
        picks = hot(iota((512, SAMPLED), 0) + 512 * part == sample)
        ids = ids + dot_nn(conn_t[:, 512 * part : 512 * part + 512], picks)
    ids1 = (ids[0:8] * 256.0 + ids[8:16]).astype(I32)
    live = ids1 > 0
    ids_s[...] = jnp.maximum(ids1 - 1, 0)
    table = slot_ref[...]
    tab_s[0:128, :] = (table >> 8).astype(F32).T.astype(BF16)
    tab_s[128:256, :] = (table & 255).astype(F32).T.astype(BF16)

    def lookup(p):
        row = ids_s[p : p + 1, :]
        picks = hot(iota((512, SAMPLED), 0) == (row >> 7))
        found = dot_nn(tab_s[...], picks)
        here = iota((128, SAMPLED), 0) == (row & 127)
        hi = jnp.sum(jnp.where(here, found[0:128], 0.0), axis=0, keepdims=True)
        lo = jnp.sum(jnp.where(here, found[128:256], 0.0), axis=0, keepdims=True)
        st_s[p : p + 1, :] = (hi * 256.0 + lo).astype(I32)

    for p in range(ENODES):
        lookup(p)
    stored = st_s[...]
    owner = stored >> 10
    mine = live & (owner == me)
    has = jnp.max(jnp.where(mine, 1.0, 0.0), axis=0, keepdims=True)
    row = jnp.sum(jnp.where(mine, stored & (NODE_DEV - 1), 0), axis=0, keepdims=True)
    dev = dev_ref[...]
    dev_f = dev.astype(F32)
    dev_col = jnp.broadcast_to(dev_f, (8, SAMPLED)).T[:, 0:1]
    same = hot((dev_col == dev_f) & (iota((SAMPLED, SAMPLED), 0) < iota((SAMPLED, SAMPLED), 1)))
    counts = dot_nn(jnp.where(iota((8, SAMPLED), 0) == 0, has, 1.0).astype(BF16), same)
    rank = counts[0:1].astype(I32)
    slot = counts[1:2].astype(I32)
    q = iota((2 * N_ELEM, SAMPLED), 0)
    goes = hot(((q >> 1) == dev) & ((q & 1) == rank) & (has > 0.5))
    r8 = iota((8, SAMPLED), 0)
    vals = jnp.where(r8 == 0, (row >> 8).astype(F32), jnp.where(r8 == 1, (row & 255).astype(F32), 1.0))
    tab = dot_nt(goes, vals.astype(BF16))
    pick = (tab[:, 0:1] * 256.0 + tab[:, 1:2]).astype(I32)
    valid = tab[:, 2:3] > 0.5
    select = hot((iota((2 * N_ELEM, NODE_DEV), 1) == pick) & valid)
    here = hot((slot == iota((CAP, SAMPLED), 0)) & (dev == me))
    own = dot_nt(here, jnp.where(live, owner + 1, 0).astype(F32).astype(BF16))
    spread = hot((iota((128, CAP), 0) >> 3) == iota((128, CAP), 1))
    wide = dot_nn(spread, own.astype(BF16))
    col = jnp.sum(
        jnp.where((iota((128, ENODES), 0) & 7) == iota((128, ENODES), 1), wide, 0.0),
        axis=1,
        keepdims=True,
    )
    by_row = jnp.broadcast_to(col, (128, 128))
    by_col = by_row.T
    before = (iota((128, 128), 1) >> 3) < (iota((128, 128), 0) >> 3)
    ahead = jnp.sum(jnp.where(before & (by_row == by_col), 1.0, 0.0), axis=1, keepdims=True)
    source = ((col - 1.0) * 2.0 + ahead).astype(I32)
    place = hot((iota((128, 128), 1) == source) & (col > 0.5))
    return select, place


def local_forces(place, rows, coords, stiff, b_s, fc_s):
    n = CAP * KROWS
    rows = dot_nn(place, rows).astype(BF16)
    basis = jnp.zeros((n, MODES), F32)
    for dof in range(NDOF):
        at = iota((n, 128), 0)
        rep = hot((at // NDOF == iota((n, 128), 1)) & (at % NDOF == dof))
        basis = basis + dot_nn(rep, rows[:, MODES * dof : MODES * dof + MODES])
    basis = basis.astype(BF16)
    b_s[...] = basis
    displaced = dot_nt(basis, coords).astype(BF16)
    every = hot(iota((32, COLS), 1) % 32 == iota((32, COLS), 0))
    wide = dot_nn(displaced, every)
    wide = jnp.where(iota((n, COLS), 0) // KROWS == iota((n, COLS), 1) // 32, wide, 0.0).astype(BF16)
    fold = hot(iota((n, KROWS), 0) % KROWS == iota((n, KROWS), 1))
    by_elem = dot_tn(fold, wide).astype(BF16)
    v = dot_nn(stiff, by_elem).astype(BF16).astype(F32)
    rolled = {}
    for g in range(4):
        part = v[:, 128 * g : 128 * g + 128]
        for shift in range(4):
            rolled[shift, g] = part if shift == 0 else pltpu.roll(part, 32 * shift, 1)
    quarter = iota((KROWS, 128), 1) // 32
    for s in range(CAP):
        for c in range(4):
            out = None
            for b in range(4):
                t = 4 * c + b
                piece = rolled[(b - s) % 4, s // 4][KROWS * t : KROWS * t + KROWS, :]
                out = piece if b == 0 else jnp.where(quarter == b, piece, out)
            fc_s[KROWS * s : KROWS * s + KROWS, 128 * c : 128 * c + 128] = out
    i0 = iota((COLS, COLS), 0)
    order = hot((i0 % 32) * 16 + i0 // 32 == iota((COLS, COLS), 1))
    return basis, dot_nn(fc_s[...].astype(BF16), order).astype(BF16)


def local_gram(basis, forces, c_s):
    n = CAP * KROWS
    inner = dot_nt(basis, basis)
    inner = jnp.where(iota((n, n), 0) // KROWS == iota((n, n), 1) // KROWS, inner, 0.0)
    h, m, l = split3(inner)
    moved = dot_nn(h.astype(BF16), forces) + dot_nn(m.astype(BF16), forces) + dot_nn(l.astype(BF16), forces)
    moved = moved * (1.0 / (SAMPLED * MODES))
    h, m, l = split3(moved)
    h, m, l = h.astype(BF16), m.astype(BF16), l.astype(BF16)
    at = 0
    for k in range(4):
        left = forces[:, 128 * k : 128 * k + 128]
        part = dot_tn(left, h[:, 128 * k :]) + dot_tn(left, m[:, 128 * k :]) + dot_tn(left, l[:, 128 * k :])
        for i in range(4 - k):
            c_s[16 * at : 16 * at + 16] = part[:, 128 * i : 128 * i + 128].reshape(16, 8, 128)
            at += 1


def panel_kernel(
    sample_ref, conn_ref, slot_ref, dev_ref, coords_ref, stiff_ref, basis_ref,
    gram_ref, f_ref, band_ref,
    basis_v, ids_s, st_s, tab_s, out_s, inc_s, ct_s, b_s, fc_s, c_ref, rbuf, o_ref, f_v, band_v,
    load_sem, x_send, x_recv, b_send, b_recv,
    rs_send, rs_recv, own_sem, z_send, z_recv, xy_send, xy_recv, c_send, c_recv,
    gram_sem, f_sem, band_sem,
):
    load = pltpu.make_async_copy(basis_ref, basis_v, load_sem)
    load.start()
    e = lax.axis_index("elem")
    x = lax.axis_index("snap")
    y, z, c = e >> 4, (e >> 1) & 7, e & 1
    barrier = pltpu.get_barrier_semaphore()

    def greet(j, carry):
        pl.semaphore_signal(barrier, inc=1, device_id=((e + j) & (N_ELEM - 1), x), device_id_type=MESH)
        return carry

    lax.fori_loop(1, N_ELEM, greet, 0)

    def greet_x(j, carry):
        x2 = (x + 1 + (j >> 2)) & 3
        y2 = j & 3
        pl.semaphore_signal(
            barrier, inc=1, device_id=(y2 * 16 + z * 2 + c, x2), device_id_type=MESH
        )
        return carry

    lax.fori_loop(0, 12, greet_x, 0)
    select, place = index_tables(sample_ref, conn_ref, slot_ref, dev_ref, ids_s, st_s, tab_s)
    load.wait()
    out_s[...] = dot_nn(select, basis_v[...]).astype(BF16).reshape(N_ELEM, 2, NDOF * MODES)
    pl.semaphore_wait(barrier, N_ELEM - 1 + 12)

    def rows_copy(j):
        peer = (e + j) & (N_ELEM - 1)
        return pltpu.make_async_remote_copy(
            src_ref=out_s.at[peer],
            dst_ref=inc_s.at[e],
            send_sem=b_send,
            recv_sem=b_recv,
            device_id=(peer, x),
            device_id_type=MESH,
        )

    def send_rows(j, carry):
        rows_copy(j).start()
        return carry

    lax.fori_loop(1, N_ELEM, send_rows, 0)
    for j in range(1, N_SNAP):
        pltpu.make_async_remote_copy(
            src_ref=coords_ref,
            dst_ref=ct_s.at[x],
            send_sem=x_send.at[j - 1],
            recv_sem=x_recv.at[j - 1],
            device_id=(e, (x + j) % N_SNAP),
            device_id_type=MESH,
        ).start()
    inc_s[e] = out_s[e]
    ct_s[x] = coords_ref[...]
    for j in range(1, N_SNAP):
        ref = ct_s.at[(x + N_SNAP - j) % N_SNAP]
        pltpu.make_async_copy(ref, ref, x_recv.at[j - 1]).wait()
    most = inc_s.at[pl.ds(0, N_ELEM - 1)]
    pltpu.make_async_copy(most, most, b_recv).wait()
    basis, forces = local_forces(
        place,
        inc_s[...].reshape(2 * N_ELEM, NDOF * MODES),
        ct_s[...].reshape(32, MODES),
        stiff_ref[...],
        b_s,
        fc_s,
    )
    f_v[...] = forces
    band_v[...] = b_s[:, pl.ds(pl.multiple_of(x * BAND, BAND), BAND)]
    f_out = pltpu.make_async_copy(f_v, f_ref, f_sem)
    band_out = pltpu.make_async_copy(band_v, band_ref, band_sem)
    local_gram(basis, forces, c_ref)
    line = y * 2 + c
    k_own = (5 * z + 7) >> 3
    owns = ((k_own * 104) >> 6) == z

    def scatter(i, carry):
        v = i + e
        t = v - 40 * ((v * 205) >> 13)
        ln = (t * 205) >> 10
        k = t - 5 * ln
        peer = ((ln >> 1) << 4) + (((k * 104) >> 6) << 1) + (ln & 1)

        @pl.when(peer != e)
        def _():
            pltpu.make_async_remote_copy(
                src_ref=c_ref.at[x * 40 + t],
                dst_ref=rbuf.at[e],
                send_sem=rs_send,
                recv_sem=rs_recv,
                device_id=(peer, x),
                device_id_type=MESH,
            ).start()

        return carry

    lax.fori_loop(0, 40, scatter, 0)
    f_out.start()
    band_out.start()
    first = x * 40 + line * 5
    tile = first + k_own

    @pl.when(owns)
    def _():
        mine = pltpu.make_async_copy(c_ref.at[tile], rbuf.at[e], own_sem)
        mine.start()
        mine.wait()
        most = rbuf.at[pl.ds(0, N_ELEM - 1)]
        pltpu.make_async_copy(most, most, rs_recv).wait()
        o_ref[tile] = jnp.sum(rbuf[...], axis=0)
        for dz in (1, 7, 2, 6, 3, 5, 4):
            z2 = (z + dz) & 7
            pltpu.make_async_remote_copy(
                src_ref=o_ref.at[tile],
                dst_ref=o_ref.at[tile],
                send_sem=z_send.at[dz - 1],
                recv_sem=z_recv.at[k_own],
                device_id=((y << 4) + (z2 << 1) + c, x),
                device_id_type=MESH,
            ).start()

    near = k_own - 5 * ((k_own * 205) >> 10)
    for step in (0, 1, 4, 2, 3):
        v = near + step
        k = v - 5 * ((v * 205) >> 10)
        at = first + k

        @pl.when(((k * 104) >> 6) != z)
        def _():
            pltpu.make_async_copy(o_ref.at[at], o_ref.at[at], z_recv.at[k]).wait()

        def send_tile(j, carry):
            x2, y2 = (x + (j >> 2)) & 3, (y + j) & 3
            pltpu.make_async_remote_copy(
                src_ref=o_ref.at[at],
                dst_ref=o_ref.at[at],
                send_sem=xy_send,
                recv_sem=xy_recv.at[x * 4 + y],
                device_id=((y2 << 4) + (z << 1) + c, x2),
                device_id_type=MESH,
            ).start()
            return carry

        lax.fori_loop(1, 16, send_tile, 0)

    def core_copy(j):
        x2, y2 = (x + (j >> 2)) & 3, (y + j) & 3
        n = x2 * 4 + y2
        at = (n * 2 + c) * 5
        return n, at, pltpu.make_async_remote_copy(
            src_ref=o_ref.at[pl.ds(at, 5)],
            dst_ref=o_ref.at[pl.ds(at, 5)],
            send_sem=c_send.at[n],
            recv_sem=c_recv.at[n],
            device_id=(e + 1 - 2 * c, x),
            device_id_type=MESH,
        )

    def put(at):
        pltpu.make_async_copy(o_ref.at[pl.ds(at, 5)], gram_ref.at[pl.ds(at, 5)], gram_sem).start()

    core_copy(0)[2].start()
    put(first)

    def forward(j, carry):
        n, at, copy = core_copy(j)
        ref = o_ref.at[pl.ds(at, 5)]
        pltpu.make_async_copy(ref, ref, xy_recv.at[n]).wait()
        copy.start()
        put(at)
        return carry

    lax.fori_loop(1, 16, forward, 0)

    def finish_core(n, carry):
        other = (n * 2 + 1 - c) * 5
        ref = o_ref.at[pl.ds(other, 5)]
        pltpu.make_async_copy(ref, ref, c_recv.at[n]).wait()
        put(other)
        pltpu.make_async_copy(ref, ref, c_send.at[n]).wait()
        return carry

    lax.fori_loop(0, 16, finish_core, 0)
    sent = o_ref.at[pl.ds(0, 75)]
    pltpu.make_async_copy(sent, sent, xy_send).wait()

    @pl.when(owns)
    def _():
        for dz in range(7):
            ref = o_ref.at[tile]
            pltpu.make_async_copy(ref, ref, z_send.at[dz]).wait()
        ref = c_ref.at[pl.ds(0, 39)]
        pltpu.make_async_copy(ref, ref, rs_send).wait()

    @pl.when(jnp.logical_not(owns))
    def _():
        ref = c_ref.at[pl.ds(0, 40)]
        pltpu.make_async_copy(ref, ref, rs_send).wait()

    f_out.wait()
    band_out.wait()
    pltpu.make_async_copy(o_ref, gram_ref, gram_sem).wait()
    most = inc_s.at[pl.ds(0, N_ELEM - 1)]
    pltpu.make_async_copy(most, most, b_send).wait()
    for j in range(1, N_SNAP):
        pltpu.make_async_copy(coords_ref, coords_ref, x_send.at[j - 1]).wait()


def panel_call(sample, conn, slots, dev, coords, stiff, basis):
    dma = pltpu.SemaphoreType.DMA
    vm = pl.BlockSpec(memory_space=pltpu.VMEM)
    n = CAP * KROWS
    width = NDOF * MODES
    return pl.pallas_call(
        panel_kernel,
        out_shape=(
            jax.ShapeDtypeStruct((160, 8, 128), F32),
            jax.ShapeDtypeStruct((n, COLS), BF16),
            jax.ShapeDtypeStruct((n, BAND), BF16),
        ),
        in_specs=[vm] * 6 + [pl.BlockSpec(memory_space=pl.ANY)],
        out_specs=(pl.BlockSpec(memory_space=pl.ANY),) * 3,
        scratch_shapes=[
            pltpu.VMEM((NODE_DEV, width), BF16),
            pltpu.VMEM((ENODES, SAMPLED), I32),
            pltpu.VMEM((ENODES, SAMPLED), I32),
            pltpu.VMEM((256, 512), BF16),
            pltpu.VMEM((N_ELEM, 2, width), BF16),
            pltpu.VMEM((N_ELEM, 2, width), BF16),
            pltpu.VMEM((N_SNAP, 8, MODES), BF16),
            pltpu.VMEM((n, MODES), BF16),
            pltpu.VMEM((n, COLS), F32),
            pltpu.VMEM((160, 8, 128), F32),
            pltpu.VMEM((N_ELEM, 8, 128), F32),
            pltpu.VMEM((160, 8, 128), F32),
            pltpu.VMEM((n, COLS), BF16),
            pltpu.VMEM((n, BAND), BF16),
            dma,
            dma((3,)),
            dma((3,)),
            dma,
            dma,
            dma,
            dma,
            dma,
            dma((7,)),
            dma((5,)),
            dma,
            dma((16,)),
            dma((16,)),
            dma((16,)),
            dma,
            dma,
            dma,
        ],
        compiler_params=pltpu.CompilerParams(collective_id=1, has_side_effects=True),
        name="panel_exchange",
    )(sample, conn, slots, dev, coords, stiff, basis)


def split2(x):
    hi = x.astype(BF16)
    return hi, (x - hi.astype(F32)).astype(BF16)


def rep(v, i):
    return jnp.broadcast_to(v[i : i + 1, :], (8, 128))


def spread_cols(v, lane):
    return [jnp.broadcast_to(v[:, lane + j : lane + j + 1], (8, 128)) for j in range(8)]


def panel(diag, p0, p1, below, ahead):
    sub = iota((8, 128), 0)
    out = [None, None]
    for k in range(8):
        r = lax.rsqrt(rep(diag[k], k))
        c = diag[k] * r
        at = {j: rep(c, j) for j in range(k + 1, 8)}
        for j in range(k + 1, 8):
            diag[j] = diag[j] - c * at[j]
        x0, x1 = rep(p0, k) * r, rep(p1, k) * r
        p0, p1 = p0 - c * x0, p1 - c * x1
        if k == 0:
            out = [x0, x1]
        else:
            out = [jnp.where(sub == k, x, o) for x, o in zip((x0, x1), out)]
        if below is not None:
            c2 = below[k] * r
            for j in range(k + 1, 8):
                below[j] = below[j] - c2 * at[j]
            for j in range(8):
                ahead[j] = ahead[j] - c2 * rep(c2, j)
    return out, ahead


def product6(a, b):
    ah, am, al = (v.astype(BF16) for v in split3(a))
    bh, bm, bl = (v.astype(BF16) for v in split3(b))
    out = dot_nn(jnp.concatenate([ah, am], 1), jnp.concatenate([bh, bh], 0))
    out = out + dot_nn(jnp.concatenate([ah, am], 1), jnp.concatenate([bm, bm], 0))
    return out + dot_nn(jnp.concatenate([ah, al], 1), jnp.concatenate([bl, bh], 0))


def product6_tn(a, b):
    ah, am, al = (v.astype(BF16) for v in split3(a))
    bh, bm, bl = (v.astype(BF16) for v in split3(b))
    out = dot_tn(jnp.concatenate([ah, am], 0), jnp.concatenate([bh, bh], 0))
    out = out + dot_tn(jnp.concatenate([ah, am], 0), jnp.concatenate([bm, bm], 0))
    return out + dot_tn(jnp.concatenate([ah, al], 0), jnp.concatenate([bl, bh], 0))


def finish_kernel(
    c_hbm, f_hbm, b_hbm, o_ref, t_ref, A, M, uh, um, gf, gh, gm, bf, o_v, c_ref, f_ref, b_ref, sems, loads
):
    get_c = pltpu.make_async_copy(c_hbm, c_ref, loads.at[0])
    get_f = pltpu.make_async_copy(f_hbm, f_ref, loads.at[1])
    get_b = pltpu.make_async_copy(b_hbm, b_ref, loads.at[2])
    get_c.start()
    get_f.start()
    get_b.start()
    get_c.wait()
    for n, (k, i) in enumerate(BLOCKS):
        A[128 * k : 128 * k + 128, 128 * i : 128 * i + 128] = c_ref[n].reshape(128, 128)
    for k in range(1, 4):
        A[128 * k : 128 * k + 128, 0 : 128 * k] = jnp.zeros((128, 128 * k), F32)
    eye = jnp.where(iota((128, 128), 0) == iota((128, 128), 1), 1.0, 0.0)
    upper = iota((128, 128), 0) <= iota((128, 128), 1)

    def across(k, i, inv):
        def run():
            rows, cols = slice(128 * k, 128 * k + 128), slice(128 * i, 128 * i + 128)
            u = product6(inv, A[rows, cols])
            A[rows, cols] = u
            uh[rows, cols], um[rows, cols] = split2(u)

        return run

    def trail(k, i, j):
        def run():
            done = slice(128 * k, 128 * k + 128)
            rows, cols = slice(128 * i, 128 * i + 128), slice(128 * j, 128 * j + 128)
            A[rows, cols] = A[rows, cols] - product6_tn(A[done, rows], A[done, cols])

        return run

    def solve(k, r, inv_h, inv_m):
        def run():
            rows = slice(128 * r, 128 * r + 128)
            cols = slice(128 * k, 128 * k + 128)
            g = f_ref[rows, cols].astype(F32)
            if k:
                done = slice(0, 128 * k)
                g = g - dot_nn(gh[rows, done], uh[done, cols])
                g = g - dot_nn(gh[rows, done], um[done, cols])
                g = g - dot_nn(gm[rows, done], uh[done, cols])
            h, m = split2(g)
            g = dot_nt(h, inv_h) + dot_nt(h, inv_m) + dot_nt(m, inv_h)
            gf[rows, cols] = g
            h, m = split2(g)
            gh[rows, cols] = h
            gm[rows, cols] = m

        return run

    def apply(k, s):
        def run():
            rows = slice(KROWS * s, KROWS * s + KROWS)
            cols = slice(128 * k, 128 * k + 128)
            g = gf[rows, cols]
            h = g.astype(BF16).astype(F32)
            b = bf[rows, :]
            lhs = jnp.concatenate([b, b], 0).astype(BF16)
            rhs = jnp.concatenate([h, g - h], 0).astype(BF16)
            o_v[s, :, cols] = dot_tn(lhs, rhs)

        return run

    def store(k):
        cols = pl.ds(128 * k, 128)
        return pltpu.make_async_copy(o_v.at[:, :, cols], o_ref.at[:, :, cols], sems.at[k])

    fill = []
    for k in range(4):
        lo = 128 * k
        M[:, 0:128] = A[lo : lo + 128, lo : lo + 128]
        M[:, 128:256] = eye
        per = -(-len(fill) // 16)
        diag = spread_cols(M[0:8, 0:128], 0)
        for p in range(16):
            top = 8 * p
            below = ahead = None
            if p < 15:
                under = M[top + 8 : top + 16, 0:128]
                below, ahead = spread_cols(under, top), spread_cols(under, top + 8)
            (u0, u1), diag = panel(
                diag, M[top : top + 8, 0:128], M[top : top + 8, 128:256], below, ahead
            )
            M[top : top + 8, 0:128] = u0
            M[top : top + 8, 128:256] = u1
            if p < 15:
                h0, m0, l0 = split3(u0)
                h1, m1, l1 = split3(u1)
                lhs = jnp.concatenate([h0, h0, m0, m0, h0, l0], 0).astype(BF16)
                r0 = jnp.concatenate([h0, m0, h0, m0, l0, h0], 0)
                r1 = jnp.concatenate([h1, m1, h1, m1, l1, h1], 0)
                upd = dot_tn(lhs, jnp.concatenate([r0, r1], 1).astype(BF16))
                if p < 12:
                    M[top + 8 :, :] = M[top + 8 :, :] - upd[top + 8 :, :]
                else:
                    later = iota((32, 256), 0) + 96 >= top + 8
                    M[96:, :] = M[96:, :] - jnp.where(later, upd[96:, :], 0.0)
            for job in fill[per * p : per * p + per]:
                job()
        inv = M[:, 128:256]
        A[lo : lo + 128, lo : lo + 128] = jnp.where(upper, M[:, 0:128], 0.0)
        inv_h, inv_m = split2(inv)
        fill = []
        if k == 0:
            get_f.wait()
            get_b.wait()
            bf[...] = b_ref[...].astype(F32)
        if k < 3:
            across(k, k + 1, inv)()
            trail(k, k + 1, k + 1)()
            fill += [across(k, i, inv) for i in range(k + 2, 4)]
            fill += [trail(k, i, j) for i in range(k + 1, 4) for j in range(i, 4) if j > k + 1]
        fill += [solve(k, r, inv_h, inv_m) for r in range(3)]
        fill += [apply(k, s) for s in range(CAP)]
        fill.append(store(k).start)
    for job in fill:
        job()
    share = COLS // N_ELEM
    start = pl.multiple_of(lax.axis_index("elem") * share, share)
    t_ref[...] = A[pl.ds(start, share), :]
    for k in range(4):
        store(k).wait()


def finish(gram, forces, band):
    share = COLS // N_ELEM
    rows = CAP * KROWS
    vm = pl.BlockSpec(memory_space=pltpu.VMEM)
    return pl.pallas_call(
        finish_kernel,
        out_shape=(
            jax.ShapeDtypeStruct((CAP, BAND, COLS), F32),
            jax.ShapeDtypeStruct((share, COLS), F32),
        ),
        in_specs=[pl.BlockSpec(memory_space=pl.ANY)] * 3,
        out_specs=(pl.BlockSpec(memory_space=pl.ANY), vm),
        scratch_shapes=[
            pltpu.VMEM((COLS, COLS), F32),
            pltpu.VMEM((128, 256), F32),
            pltpu.VMEM((COLS, COLS), BF16),
            pltpu.VMEM((COLS, COLS), BF16),
            pltpu.VMEM((rows, COLS), F32),
            pltpu.VMEM((rows, COLS), BF16),
            pltpu.VMEM((rows, COLS), BF16),
            pltpu.VMEM((rows, BAND), F32),
            pltpu.VMEM((CAP, BAND, COLS), F32),
            pltpu.VMEM((10, 16, 8, 128), F32),
            pltpu.VMEM((rows, COLS), BF16),
            pltpu.VMEM((rows, BAND), BF16),
            pltpu.SemaphoreType.DMA((4,)),
            pltpu.SemaphoreType.DMA((3,)),
        ],
        name="factor_and_apply",
    )(gram, forces, band)


def shards(
    node_basis, stiff_terms, reduced_coords, sample_list, connectivity, node_slot, elem_device
):
    gram, forces, band = panel_call(
        sample_list.reshape(1, SAMPLED),
        connectivity.T,
        node_slot.reshape(512, 128),
        elem_device.reshape(1, SAMPLED),
        reduced_coords.T,
        stiff_terms.reshape(16 * KROWS, KROWS),
        node_basis,
    )
    return finish(gram.reshape(10, 16, 8, 128), forces, band)


def solution(mesh):
    placed = (P("elem", None), P(), P(None, "snap"), P(), P(), P(), P())
    return jax.shard_map(
        shards,
        mesh=mesh,
        in_specs=placed,
        out_specs=(P("elem", "snap", None), P("elem", None)),
        check_vma=False,
    )
```

```python
import jax
import jax.numpy as jnp
from jax import lax
from jax.experimental import pallas as pl
from jax.experimental.pallas import tpu as pltpu
from jax.sharding import PartitionSpec as P

F32, BF16, I32 = jnp.float32, jnp.bfloat16, jnp.int32
HI = lax.Precision.HIGHEST
MESH = pl.DeviceIdType.MESH
MODES = 512
COLS = 512
ENODES = 8
NDOF = 3
CAP = 16
SAMPLED = 512
N_ELEM = 64
N_SNAP = 4
NODE_DEV = 1024
BAND = MODES // N_SNAP
KROWS = ENODES * NDOF
BLOCKS = [(k, i) for k in range(4) for i in range(k, 4)]


def iota(shape, axis):
    return lax.broadcasted_iota(I32, shape, axis)


def hot(mask):
    return jnp.where(mask, 1.0, 0.0).astype(BF16)


def dot_nt(a, b):
    return lax.dot_general(a, b, (((1,), (1,)), ((), ())), preferred_element_type=F32)


def dot_tn(a, b, precision=None):
    return lax.dot_general(
        a, b, (((0,), (0,)), ((), ())), precision=precision, preferred_element_type=F32
    )


def dot_nn(a, b):
    return jnp.dot(a, b, preferred_element_type=F32)


def split3(x):
    h = x.astype(BF16).astype(F32)
    r = x - h
    m = r.astype(BF16).astype(F32)
    return h, m, r - m


def index_tables(sample_ref, conn_ref, slot_ref, dev_ref, ids_s, st_s, tab_s):
    me = lax.axis_index("elem")
    conn = conn_ref[...] + 1
    conn_t = jnp.concatenate([(conn >> 8).astype(F32), (conn & 255).astype(F32)], 0)
    sample = sample_ref[...]
    groups = 2048 // 128
    stacked = jnp.concatenate([conn_t[:, 128 * g : 128 * g + 128] for g in range(groups)], 0)
    found = dot_nn(stacked.astype(BF16), hot(iota((128, SAMPLED), 0) == (sample & 127)))
    ids = jnp.zeros((16, SAMPLED), F32)
    for g in range(groups):
        ids = ids + jnp.where((sample >> 7) == g, found[16 * g : 16 * g + 16], 0.0)
    ids1 = (ids[0:8] * 256.0 + ids[8:16]).astype(I32)
    live = ids1 > 0
    ids_s[...] = jnp.maximum(ids1 - 1, 0)
    table = slot_ref[...]
    tab_s[0:128, :] = (table >> 8).astype(F32).T.astype(BF16)
    tab_s[128:256, :] = (table & 255).astype(F32).T.astype(BF16)

    def lookup(p):
        row = ids_s[p : p + 1, :]
        picks = hot(iota((512, SAMPLED), 0) == (row >> 7))
        found = dot_nn(tab_s[...], picks)
        here = iota((128, SAMPLED), 0) == (row & 127)
        hi = jnp.sum(jnp.where(here, found[0:128], 0.0), axis=0, keepdims=True)
        lo = jnp.sum(jnp.where(here, found[128:256], 0.0), axis=0, keepdims=True)
        st_s[p : p + 1, :] = (hi * 256.0 + lo).astype(I32)

    for p in range(ENODES):
        lookup(p)
    stored = st_s[...]
    owner = stored >> 10
    mine = live & (owner == me)
    has = jnp.max(jnp.where(mine, 1.0, 0.0), axis=0, keepdims=True)
    row = jnp.sum(jnp.where(mine, stored & (NODE_DEV - 1), 0), axis=0, keepdims=True)
    dev = dev_ref[...]
    dev_f = dev.astype(F32)
    dev_col = jnp.broadcast_to(dev_f, (8, SAMPLED)).T[:, 0:1]
    same = hot((dev_col == dev_f) & (iota((SAMPLED, SAMPLED), 0) < iota((SAMPLED, SAMPLED), 1)))
    counts = dot_nn(jnp.where(iota((8, SAMPLED), 0) == 0, has, 1.0).astype(BF16), same)
    rank = counts[0:1].astype(I32)
    slot = counts[1:2].astype(I32)
    q = iota((2 * N_ELEM, SAMPLED), 0)
    goes = hot(((q >> 1) == dev) & ((q & 1) == rank) & (has > 0.5))
    r8 = iota((8, SAMPLED), 0)
    vals = jnp.where(r8 == 0, (row >> 8).astype(F32), jnp.where(r8 == 1, (row & 255).astype(F32), 1.0))
    tab = dot_nt(goes, vals.astype(BF16))
    pick = (tab[:, 0:1] * 256.0 + tab[:, 1:2]).astype(I32)
    valid = tab[:, 2:3] > 0.5
    select = hot((iota((2 * N_ELEM, NODE_DEV), 1) == pick) & valid)
    here = hot((slot == iota((CAP, SAMPLED), 0)) & (dev == me))
    own = dot_nt(here, jnp.where(live, owner + 1, 0).astype(F32).astype(BF16))
    spread = hot((iota((128, CAP), 0) >> 3) == iota((128, CAP), 1))
    wide = dot_nn(spread, own.astype(BF16))
    col = jnp.sum(
        jnp.where((iota((128, ENODES), 0) & 7) == iota((128, ENODES), 1), wide, 0.0),
        axis=1,
        keepdims=True,
    )
    by_row = jnp.broadcast_to(col, (128, 128))
    by_col = by_row.T
    before = (iota((128, 128), 1) >> 3) < (iota((128, 128), 0) >> 3)
    ahead = jnp.sum(jnp.where(before & (by_row == by_col), 1.0, 0.0), axis=1, keepdims=True)
    source = ((col - 1.0) * 2.0 + ahead).astype(I32)
    place = hot((iota((128, 128), 1) == source) & (col > 0.5))
    return select, place


def local_forces(place, rows, coords, stiff, b_s, fc_s):
    n = CAP * KROWS
    rows = dot_nn(place, rows).astype(BF16)
    basis = jnp.zeros((n, MODES), F32)
    for dof in range(NDOF):
        at = iota((n, 128), 0)
        rep = hot((at // NDOF == iota((n, 128), 1)) & (at % NDOF == dof))
        basis = basis + dot_nn(rep, rows[:, MODES * dof : MODES * dof + MODES])
    basis = basis.astype(BF16)
    b_s[...] = basis
    displaced = dot_nt(basis, coords).astype(BF16)
    every = hot(iota((32, COLS), 1) % 32 == iota((32, COLS), 0))
    wide = dot_nn(displaced, every)
    wide = jnp.where(iota((n, COLS), 0) // KROWS == iota((n, COLS), 1) // 32, wide, 0.0).astype(BF16)
    fold = hot(iota((n, KROWS), 0) % KROWS == iota((n, KROWS), 1))
    by_elem = dot_tn(fold, wide).astype(BF16)
    v = dot_nn(stiff, by_elem).astype(BF16).astype(F32)
    rolled = {}
    for g in range(4):
        part = v[:, 128 * g : 128 * g + 128]
        for shift in range(4):
            rolled[shift, g] = part if shift == 0 else pltpu.roll(part, 32 * shift, 1)
    quarter = iota((KROWS, 128), 1) // 32
    for s in range(CAP):
        for c in range(4):
            out = None
            for b in range(4):
                t = 4 * c + b
                piece = rolled[(b - s) % 4, s // 4][KROWS * t : KROWS * t + KROWS, :]
                out = piece if b == 0 else jnp.where(quarter == b, piece, out)
            fc_s[KROWS * s : KROWS * s + KROWS, 128 * c : 128 * c + 128] = out
    i0 = iota((COLS, COLS), 0)
    order = hot((i0 % 32) * 16 + i0 // 32 == iota((COLS, COLS), 1))
    return basis, dot_nn(fc_s[...].astype(BF16), order).astype(BF16)


def local_gram(basis, forces, c_s):
    n = CAP * KROWS
    inner = dot_nt(basis, basis)
    inner = jnp.where(iota((n, n), 0) // KROWS == iota((n, n), 1) // KROWS, inner, 0.0)
    h, m, l = split3(inner)
    moved = dot_nn(h.astype(BF16), forces) + dot_nn(m.astype(BF16), forces) + dot_nn(l.astype(BF16), forces)
    moved = moved * (1.0 / (SAMPLED * MODES))
    h, m, l = split3(moved)
    h, m, l = h.astype(BF16), m.astype(BF16), l.astype(BF16)
    at = 0
    for k in range(4):
        left = forces[:, 128 * k : 128 * k + 128]
        part = dot_tn(left, h[:, 128 * k :]) + dot_tn(left, m[:, 128 * k :]) + dot_tn(left, l[:, 128 * k :])
        for i in range(4 - k):
            c_s[16 * at : 16 * at + 16] = part[:, 128 * i : 128 * i + 128].reshape(16, 8, 128)
            at += 1


def panel_kernel(
    sample_ref, conn_ref, slot_ref, dev_ref, coords_ref, stiff_ref, basis_ref,
    gram_ref, f_ref, band_ref,
    basis_v, ids_s, st_s, tab_s, out_s, inc_s, ct_s, b_s, fc_s, c_ref, rbuf, o_ref, f_v, band_v,
    load_sem, x_send, x_recv, b_send, b_recv,
    rs_send, rs_recv, own_sem, z_send, z_recv, xy_send, xy_recv, c_send, c_recv,
    gram_sem, f_sem, band_sem,
):
    load = pltpu.make_async_copy(basis_ref, basis_v, load_sem)
    load.start()
    e = lax.axis_index("elem")
    x = lax.axis_index("snap")
    y, z, c = e >> 4, (e >> 1) & 7, e & 1
    barrier = pltpu.get_barrier_semaphore()

    def greet(j, carry):
        pl.semaphore_signal(barrier, inc=1, device_id=((e + j) & (N_ELEM - 1), x), device_id_type=MESH)
        return carry

    lax.fori_loop(1, N_ELEM, greet, 0)

    def greet_x(j, carry):
        x2 = (x + 1 + (j >> 2)) & 3
        y2 = j & 3
        pl.semaphore_signal(
            barrier, inc=1, device_id=(y2 * 16 + z * 2 + c, x2), device_id_type=MESH
        )
        return carry

    lax.fori_loop(0, 12, greet_x, 0)
    select, place = index_tables(sample_ref, conn_ref, slot_ref, dev_ref, ids_s, st_s, tab_s)
    load.wait()
    out_s[...] = dot_nn(select, basis_v[...]).astype(BF16).reshape(N_ELEM, 2, NDOF * MODES)
    pl.semaphore_wait(barrier, N_ELEM - 1 + 12)

    def rows_copy(j):
        peer = (e + j) & (N_ELEM - 1)
        return pltpu.make_async_remote_copy(
            src_ref=out_s.at[peer],
            dst_ref=inc_s.at[e],
            send_sem=b_send,
            recv_sem=b_recv,
            device_id=(peer, x),
            device_id_type=MESH,
        )

    def send_rows(j, carry):
        rows_copy(j).start()
        return carry

    lax.fori_loop(1, N_ELEM, send_rows, 0)
    for j in range(1, N_SNAP):
        pltpu.make_async_remote_copy(
            src_ref=coords_ref,
            dst_ref=ct_s.at[x],
            send_sem=x_send.at[j - 1],
            recv_sem=x_recv.at[j - 1],
            device_id=(e, (x + j) % N_SNAP),
            device_id_type=MESH,
        ).start()
    inc_s[e] = out_s[e]
    ct_s[x] = coords_ref[...]
    for j in range(1, N_SNAP):
        ref = ct_s.at[(x + N_SNAP - j) % N_SNAP]
        pltpu.make_async_copy(ref, ref, x_recv.at[j - 1]).wait()
    most = inc_s.at[pl.ds(0, N_ELEM - 1)]
    pltpu.make_async_copy(most, most, b_recv).wait()
    basis, forces = local_forces(
        place,
        inc_s[...].reshape(2 * N_ELEM, NDOF * MODES),
        ct_s[...].reshape(32, MODES),
        stiff_ref[...],
        b_s,
        fc_s,
    )
    f_v[...] = forces
    band_v[...] = b_s[:, pl.ds(pl.multiple_of(x * BAND, BAND), BAND)]
    f_out = pltpu.make_async_copy(f_v, f_ref, f_sem)
    band_out = pltpu.make_async_copy(band_v, band_ref, band_sem)
    local_gram(basis, forces, c_ref)
    line = y * 2 + c
    k_own = (5 * z + 7) >> 3
    owns = ((k_own * 104) >> 6) == z

    def scatter(i, carry):
        v = i + e
        t = v - 40 * ((v * 205) >> 13)
        ln = (t * 205) >> 10
        k = t - 5 * ln
        peer = ((ln >> 1) << 4) + (((k * 104) >> 6) << 1) + (ln & 1)

        @pl.when(peer != e)
        def _():
            pltpu.make_async_remote_copy(
                src_ref=c_ref.at[x * 40 + t],
                dst_ref=rbuf.at[e],
                send_sem=rs_send,
                recv_sem=rs_recv,
                device_id=(peer, x),
                device_id_type=MESH,
            ).start()

        return carry

    lax.fori_loop(0, 40, scatter, 0)
    f_out.start()
    band_out.start()
    first = x * 40 + line * 5
    tile = first + k_own

    @pl.when(owns)
    def _():
        mine = pltpu.make_async_copy(c_ref.at[tile], rbuf.at[e], own_sem)
        mine.start()
        mine.wait()
        most = rbuf.at[pl.ds(0, N_ELEM - 1)]
        pltpu.make_async_copy(most, most, rs_recv).wait()
        o_ref[tile] = jnp.sum(rbuf[...], axis=0)
        for dz in (1, 7, 2, 6, 3, 5, 4):
            z2 = (z + dz) & 7
            pltpu.make_async_remote_copy(
                src_ref=o_ref.at[tile],
                dst_ref=o_ref.at[tile],
                send_sem=z_send.at[dz - 1],
                recv_sem=z_recv.at[k_own],
                device_id=((y << 4) + (z2 << 1) + c, x),
                device_id_type=MESH,
            ).start()

    near = k_own - 5 * ((k_own * 205) >> 10)
    for step in (0, 1, 4, 2, 3):
        v = near + step
        k = v - 5 * ((v * 205) >> 10)
        at = first + k

        @pl.when(((k * 104) >> 6) != z)
        def _():
            pltpu.make_async_copy(o_ref.at[at], o_ref.at[at], z_recv.at[k]).wait()

        def send_tile(j, carry):
            x2, y2 = (x + (j >> 2)) & 3, (y + j) & 3
            pltpu.make_async_remote_copy(
                src_ref=o_ref.at[at],
                dst_ref=o_ref.at[at],
                send_sem=xy_send,
                recv_sem=xy_recv.at[x * 4 + y],
                device_id=((y2 << 4) + (z << 1) + c, x2),
                device_id_type=MESH,
            ).start()
            return carry

        lax.fori_loop(1, 16, send_tile, 0)

    def core_copy(j):
        x2, y2 = (x + (j >> 2)) & 3, (y + j) & 3
        n = x2 * 4 + y2
        at = (n * 2 + c) * 5
        return n, at, pltpu.make_async_remote_copy(
            src_ref=o_ref.at[pl.ds(at, 5)],
            dst_ref=o_ref.at[pl.ds(at, 5)],
            send_sem=c_send.at[n],
            recv_sem=c_recv.at[n],
            device_id=(e + 1 - 2 * c, x),
            device_id_type=MESH,
        )

    def put(at):
        pltpu.make_async_copy(o_ref.at[pl.ds(at, 5)], gram_ref.at[pl.ds(at, 5)], gram_sem).start()

    core_copy(0)[2].start()
    put(first)

    def forward(j, carry):
        n, at, copy = core_copy(j)
        ref = o_ref.at[pl.ds(at, 5)]
        pltpu.make_async_copy(ref, ref, xy_recv.at[n]).wait()
        copy.start()
        put(at)
        return carry

    lax.fori_loop(1, 16, forward, 0)

    def finish_core(n, carry):
        other = (n * 2 + 1 - c) * 5
        ref = o_ref.at[pl.ds(other, 5)]
        pltpu.make_async_copy(ref, ref, c_recv.at[n]).wait()
        put(other)
        pltpu.make_async_copy(ref, ref, c_send.at[n]).wait()
        return carry

    lax.fori_loop(0, 16, finish_core, 0)
    sent = o_ref.at[pl.ds(0, 75)]
    pltpu.make_async_copy(sent, sent, xy_send).wait()

    @pl.when(owns)
    def _():
        for dz in range(7):
            ref = o_ref.at[tile]
            pltpu.make_async_copy(ref, ref, z_send.at[dz]).wait()
        ref = c_ref.at[pl.ds(0, 39)]
        pltpu.make_async_copy(ref, ref, rs_send).wait()

    @pl.when(jnp.logical_not(owns))
    def _():
        ref = c_ref.at[pl.ds(0, 40)]
        pltpu.make_async_copy(ref, ref, rs_send).wait()

    f_out.wait()
    band_out.wait()
    pltpu.make_async_copy(o_ref, gram_ref, gram_sem).wait()
    most = inc_s.at[pl.ds(0, N_ELEM - 1)]
    pltpu.make_async_copy(most, most, b_send).wait()
    for j in range(1, N_SNAP):
        pltpu.make_async_copy(coords_ref, coords_ref, x_send.at[j - 1]).wait()


def panel_call(sample, conn, slots, dev, coords, stiff, basis):
    dma = pltpu.SemaphoreType.DMA
    vm = pl.BlockSpec(memory_space=pltpu.VMEM)
    n = CAP * KROWS
    width = NDOF * MODES
    return pl.pallas_call(
        panel_kernel,
        out_shape=(
            jax.ShapeDtypeStruct((160, 8, 128), F32),
            jax.ShapeDtypeStruct((n, COLS), BF16),
            jax.ShapeDtypeStruct((n, BAND), BF16),
        ),
        in_specs=[vm] * 6 + [pl.BlockSpec(memory_space=pl.ANY)],
        out_specs=(pl.BlockSpec(memory_space=pl.ANY),) * 3,
        scratch_shapes=[
            pltpu.VMEM((NODE_DEV, width), BF16),
            pltpu.VMEM((ENODES, SAMPLED), I32),
            pltpu.VMEM((ENODES, SAMPLED), I32),
            pltpu.VMEM((256, 512), BF16),
            pltpu.VMEM((N_ELEM, 2, width), BF16),
            pltpu.VMEM((N_ELEM, 2, width), BF16),
            pltpu.VMEM((N_SNAP, 8, MODES), BF16),
            pltpu.VMEM((n, MODES), BF16),
            pltpu.VMEM((n, COLS), F32),
            pltpu.VMEM((160, 8, 128), F32),
            pltpu.VMEM((N_ELEM, 8, 128), F32),
            pltpu.VMEM((160, 8, 128), F32),
            pltpu.VMEM((n, COLS), BF16),
            pltpu.VMEM((n, BAND), BF16),
            dma,
            dma((3,)),
            dma((3,)),
            dma,
            dma,
            dma,
            dma,
            dma,
            dma((7,)),
            dma((5,)),
            dma,
            dma((16,)),
            dma((16,)),
            dma((16,)),
            dma,
            dma,
            dma,
        ],
        compiler_params=pltpu.CompilerParams(collective_id=1, has_side_effects=True),
        name="panel_exchange",
    )(sample, conn, slots, dev, coords, stiff, basis)


def split2(x):
    hi = x.astype(BF16)
    return hi, (x - hi.astype(F32)).astype(BF16)


def rep(v, i):
    return jnp.broadcast_to(v[i : i + 1, :], (8, 128))


def spread_cols(v, lane):
    return [jnp.broadcast_to(v[:, lane + j : lane + j + 1], (8, 128)) for j in range(8)]


def panel(diag, p0, p1, below, ahead, q0, q1):
    sub = iota((8, 128), 0)
    out = [None, None]
    for k in range(8):
        r = lax.rsqrt(rep(diag[k], k))
        c = diag[k] * r
        at = {j: rep(c, j) for j in range(k + 1, 8)}
        for j in range(k + 1, 8):
            diag[j] = diag[j] - c * at[j]
        x0, x1 = rep(p0, k) * r, rep(p1, k) * r
        p0, p1 = p0 - c * x0, p1 - c * x1
        if k == 0:
            out = [x0, x1]
        else:
            out = [jnp.where(sub == k, x, o) for x, o in zip((x0, x1), out)]
        if below is not None:
            c2 = below[k] * r
            for j in range(k + 1, 8):
                below[j] = below[j] - c2 * at[j]
            for j in range(8):
                ahead[j] = ahead[j] - c2 * rep(c2, j)
            q0, q1 = q0 - c2 * x0, q1 - c2 * x1
    return out, ahead, q0, q1


def product6(a, b):
    ah, am, al = (v.astype(BF16) for v in split3(a))
    bh, bm, bl = (v.astype(BF16) for v in split3(b))
    out = dot_nn(jnp.concatenate([ah, am], 1), jnp.concatenate([bh, bh], 0))
    out = out + dot_nn(jnp.concatenate([ah, am], 1), jnp.concatenate([bm, bm], 0))
    return out + dot_nn(jnp.concatenate([ah, al], 1), jnp.concatenate([bl, bh], 0))


def product6_tn(a, b):
    ah, am, al = (v.astype(BF16) for v in split3(a))
    bh, bm, bl = (v.astype(BF16) for v in split3(b))
    out = dot_tn(jnp.concatenate([ah, am], 0), jnp.concatenate([bh, bh], 0))
    out = out + dot_tn(jnp.concatenate([ah, am], 0), jnp.concatenate([bm, bm], 0))
    return out + dot_tn(jnp.concatenate([ah, al], 0), jnp.concatenate([bl, bh], 0))


def finish_kernel(
    c_hbm, f_hbm, b_hbm, o_ref, t_ref, A, M, uh, um, gf, gh, gm, bf, bt, o_v, c_ref, f_ref, b_ref, sems, loads
):
    get_c = pltpu.make_async_copy(c_hbm, c_ref, loads.at[0])
    get_f = pltpu.make_async_copy(f_hbm, f_ref, loads.at[1])
    get_b = pltpu.make_async_copy(b_hbm, b_ref, loads.at[2])
    get_c.start()
    get_f.start()
    get_b.start()
    get_b.wait()
    get_f.wait()
    get_c.wait()
    for n, (k, i) in enumerate(BLOCKS):
        A[128 * k : 128 * k + 128, 128 * i : 128 * i + 128] = c_ref[n].reshape(128, 128)
    for k in range(1, 4):
        A[128 * k : 128 * k + 128, 0 : 128 * k] = jnp.zeros((128, 128 * k), F32)
    eye = jnp.where(iota((128, 128), 0) == iota((128, 128), 1), 1.0, 0.0)
    upper = iota((128, 128), 0) <= iota((128, 128), 1)

    def across(k, i, inv):
        def run():
            rows, cols = slice(128 * k, 128 * k + 128), slice(128 * i, 128 * i + 128)
            u = product6(inv, A[rows, cols])
            A[rows, cols] = u
            uh[rows, cols], um[rows, cols] = split2(u)

        return run

    def trail(k, i, j):
        def run():
            done = slice(128 * k, 128 * k + 128)
            rows, cols = slice(128 * i, 128 * i + 128), slice(128 * j, 128 * j + 128)
            A[rows, cols] = A[rows, cols] - product6_tn(A[done, rows], A[done, cols])

        return run

    def reduce(k, r):
        def run():
            rows = slice(128 * r, 128 * r + 128)
            cols = slice(128 * k, 128 * k + 128)
            g = f_ref[rows, cols].astype(F32)
            if k:
                done = slice(0, 128 * k)
                g = g - dot_nn(gh[rows, done], uh[done, cols])
                g = g - dot_nn(gh[rows, done], um[done, cols])
                g = g - dot_nn(gm[rows, done], uh[done, cols])
            gf[rows, cols] = g

        return run

    def solve(k, r, inv_h, inv_m):
        def run():
            rows = slice(128 * r, 128 * r + 128)
            cols = slice(128 * k, 128 * k + 128)
            h, m = split2(gf[rows, cols])
            g = dot_nt(h, inv_h) + dot_nt(m, inv_h)
            if inv_m is not None:
                g = g + dot_nt(h, inv_m)
            gf[rows, cols] = g
            h, m = split2(g)
            gh[rows, cols] = h
            gm[rows, cols] = m

        return run

    def flip(s):
        def run():
            b = b_ref[...] if s is None else bf[KROWS * s : KROWS * s + KROWS, :]
            if s is None:
                bf[...] = b.astype(F32)
            else:
                bt[s] = jnp.concatenate([b, b], 0).T

        return run

    def apply(k, s):
        def run():
            rows = slice(KROWS * s, KROWS * s + KROWS)
            cols = slice(128 * k, 128 * k + 128)
            g = gf[rows, cols]
            h = g.astype(BF16).astype(F32)
            rhs = jnp.concatenate([h, g - h], 0).astype(BF16)
            o_v[s, :, cols] = dot_nn(bt[s].astype(BF16), rhs)

        return run

    def store(k):
        cols = pl.ds(128 * k, 128)
        return pltpu.make_async_copy(o_v.at[:, :, cols], o_ref.at[:, :, cols], sems.at[k])

    fill = [flip(None)] + [flip(s) for s in range(CAP)] + [reduce(0, r) for r in range(3)]
    for k in range(4):
        lo = 128 * k
        M[:, 0:128] = A[lo : lo + 128, lo : lo + 128]
        M[:, 128:256] = eye
        per = -(-len(fill) // 16)
        diag = spread_cols(M[0:8, 0:128], 0)
        p0, p1 = M[0:8, 0:128], M[0:8, 128:256]
        for p in range(16):
            top = 8 * p
            below = ahead = q0 = q1 = None
            if p < 15:
                q0, q1 = M[top + 8 : top + 16, 0:128], M[top + 8 : top + 16, 128:256]
                below, ahead = spread_cols(q0, top), spread_cols(q0, top + 8)
            (u0, u1), diag, p0, p1 = panel(diag, p0, p1, below, ahead, q0, q1)
            M[top : top + 8, 0:128] = u0
            M[top : top + 8, 128:256] = u1
            if p < 14:
                h0, m0, l0 = split3(u0)
                h1, m1, l1 = split3(u1)
                lhs = jnp.concatenate([h0, h0, m0, m0, h0, l0], 0).astype(BF16)
                r0 = jnp.concatenate([h0, m0, h0, m0, l0, h0], 0)
                r1 = jnp.concatenate([h1, m1, h1, m1, l1, h1], 0)
                start = min((top + 16) // 16 * 16, 96)
                upd = dot_nn(lhs.T[start:, :], jnp.concatenate([r0, r1], 1).astype(BF16))
                if start < top + 8:
                    upd = jnp.where(iota((128 - start, 256), 0) + start >= top + 16, upd, 0.0)
                M[start:, :] = M[start:, :] - upd
            for job in fill[per * p : per * p + per]:
                job()
        inv = M[:, 128:256]
        A[lo : lo + 128, lo : lo + 128] = jnp.where(upper, M[:, 0:128], 0.0)
        inv_h, inv_m = split2(inv)
        fill = []
        if k < 3:
            across(k, k + 1, inv)()
            trail(k, k + 1, k + 1)()
            fill += [across(k, i, inv) for i in range(k + 2, 4)]
            fill += [trail(k, i, j) for i in range(k + 1, 4) for j in range(i, 4) if j > k + 1]
        fill += [solve(k, r, inv_h, inv_m) for r in range(3)]
        if k < 3:
            fill += [reduce(k + 1, r) for r in range(3)]
        fill += [apply(k, s) for s in range(CAP)]
        fill.append(store(k).start)
    for job in fill:
        job()
    share = COLS // N_ELEM
    start = pl.multiple_of(lax.axis_index("elem") * share, share)
    t_ref[...] = A[pl.ds(start, share), :]
    for k in range(4):
        store(k).wait()


def finish(gram, forces, band):
    share = COLS // N_ELEM
    rows = CAP * KROWS
    vm = pl.BlockSpec(memory_space=pltpu.VMEM)
    return pl.pallas_call(
        finish_kernel,
        out_shape=(
            jax.ShapeDtypeStruct((CAP, BAND, COLS), F32),
            jax.ShapeDtypeStruct((share, COLS), F32),
        ),
        in_specs=[pl.BlockSpec(memory_space=pl.ANY)] * 3,
        out_specs=(pl.BlockSpec(memory_space=pl.ANY), vm),
        scratch_shapes=[
            pltpu.VMEM((COLS, COLS), F32),
            pltpu.VMEM((128, 256), F32),
            pltpu.VMEM((COLS, COLS), BF16),
            pltpu.VMEM((COLS, COLS), BF16),
            pltpu.VMEM((rows, COLS), F32),
            pltpu.VMEM((rows, COLS), BF16),
            pltpu.VMEM((rows, COLS), BF16),
            pltpu.VMEM((rows, BAND), F32),
            pltpu.VMEM((CAP, BAND, 2 * KROWS), F32),
            pltpu.VMEM((CAP, BAND, COLS), F32),
            pltpu.VMEM((10, 16, 8, 128), F32),
            pltpu.VMEM((rows, COLS), BF16),
            pltpu.VMEM((rows, BAND), BF16),
            pltpu.SemaphoreType.DMA((4,)),
            pltpu.SemaphoreType.DMA((3,)),
        ],
        name="factor_and_apply",
    )(gram, forces, band)


def shards(
    node_basis, stiff_terms, reduced_coords, sample_list, connectivity, node_slot, elem_device
):
    gram, forces, band = panel_call(
        sample_list.reshape(1, SAMPLED),
        connectivity.T,
        node_slot.reshape(512, 128),
        elem_device.reshape(1, SAMPLED),
        reduced_coords.T,
        stiff_terms.reshape(16 * KROWS, KROWS),
        node_basis,
    )
    return finish(gram.reshape(10, 16, 8, 128), forces, band)


def solution(mesh):
    placed = (P("elem", None), P(), P(None, "snap"), P(), P(), P(), P())
    return jax.shard_map(
        shards,
        mesh=mesh,
        in_specs=placed,
        out_specs=(P("elem", "snap", None), P("elem", None)),
        check_vma=False,
    )
```

```python
import jax
import jax.numpy as jnp
from jax import lax
from jax.experimental import pallas as pl
from jax.experimental.pallas import tpu as pltpu
from jax.sharding import PartitionSpec as P

F32, BF16, I32 = jnp.float32, jnp.bfloat16, jnp.int32
HI = lax.Precision.HIGHEST
MESH = pl.DeviceIdType.MESH
MODES = 512
COLS = 512
ENODES = 8
NDOF = 3
CAP = 16
SAMPLED = 512
N_ELEM = 64
N_SNAP = 4
NODE_DEV = 1024
BAND = MODES // N_SNAP
KROWS = ENODES * NDOF
BLOCKS = [(k, i) for k in range(4) for i in range(k, 4)]


def iota(shape, axis):
    return lax.broadcasted_iota(I32, shape, axis)


def hot(mask):
    return jnp.where(mask, 1.0, 0.0).astype(BF16)


def dot_nt(a, b):
    return lax.dot_general(a, b, (((1,), (1,)), ((), ())), preferred_element_type=F32)


def dot_tn(a, b, precision=None):
    return lax.dot_general(
        a, b, (((0,), (0,)), ((), ())), precision=precision, preferred_element_type=F32
    )


def dot_nn(a, b):
    return jnp.dot(a, b, preferred_element_type=F32)


def split3(x):
    h = x.astype(BF16).astype(F32)
    r = x - h
    m = r.astype(BF16).astype(F32)
    return h, m, r - m


def index_tables(sample_ref, conn_ref, slot_ref, dev_ref, ids_s, st_s, tab_s):
    me = lax.axis_index("elem")
    conn = conn_ref[...] + 1
    conn_t = jnp.concatenate([(conn >> 8).astype(F32), (conn & 255).astype(F32)], 0)
    sample = sample_ref[...]
    groups = 2048 // 128
    stacked = jnp.concatenate([conn_t[:, 128 * g : 128 * g + 128] for g in range(groups)], 0)
    found = dot_nn(stacked.astype(BF16), hot(iota((128, SAMPLED), 0) == (sample & 127)))
    ids = jnp.zeros((16, SAMPLED), F32)
    for g in range(groups):
        ids = ids + jnp.where((sample >> 7) == g, found[16 * g : 16 * g + 16], 0.0)
    ids1 = (ids[0:8] * 256.0 + ids[8:16]).astype(I32)
    live = ids1 > 0
    ids_s[...] = jnp.maximum(ids1 - 1, 0)
    table = slot_ref[...]
    tab_s[0:128, :] = (table >> 8).astype(F32).T.astype(BF16)
    tab_s[128:256, :] = (table & 255).astype(F32).T.astype(BF16)

    def lookup(p):
        row = ids_s[p : p + 1, :]
        picks = hot(iota((512, SAMPLED), 0) == (row >> 7))
        found = dot_nn(tab_s[...], picks)
        here = iota((128, SAMPLED), 0) == (row & 127)
        hi = jnp.sum(jnp.where(here, found[0:128], 0.0), axis=0, keepdims=True)
        lo = jnp.sum(jnp.where(here, found[128:256], 0.0), axis=0, keepdims=True)
        st_s[p : p + 1, :] = (hi * 256.0 + lo).astype(I32)

    for p in range(ENODES):
        lookup(p)
    stored = st_s[...]
    owner = stored >> 10
    mine = live & (owner == me)
    has = jnp.max(jnp.where(mine, 1.0, 0.0), axis=0, keepdims=True)
    row = jnp.sum(jnp.where(mine, stored & (NODE_DEV - 1), 0), axis=0, keepdims=True)
    dev = dev_ref[...]
    dev_f = dev.astype(F32)
    dev_col = jnp.broadcast_to(dev_f, (8, SAMPLED)).T[:, 0:1]
    same = hot((dev_col == dev_f) & (iota((SAMPLED, SAMPLED), 0) < iota((SAMPLED, SAMPLED), 1)))
    counts = dot_nn(jnp.where(iota((8, SAMPLED), 0) == 0, has, 1.0).astype(BF16), same)
    rank = counts[0:1].astype(I32)
    slot = counts[1:2].astype(I32)
    q = iota((2 * N_ELEM, SAMPLED), 0)
    goes = hot(((q >> 1) == dev) & ((q & 1) == rank) & (has > 0.5))
    r8 = iota((8, SAMPLED), 0)
    vals = jnp.where(r8 == 0, (row >> 8).astype(F32), jnp.where(r8 == 1, (row & 255).astype(F32), 1.0))
    tab = dot_nt(goes, vals.astype(BF16))
    pick = (tab[:, 0:1] * 256.0 + tab[:, 1:2]).astype(I32)
    valid = tab[:, 2:3] > 0.5
    select = hot((iota((2 * N_ELEM, NODE_DEV), 1) == pick) & valid)
    here = hot((slot == iota((CAP, SAMPLED), 0)) & (dev == me))
    own = dot_nt(here, jnp.where(live, owner + 1, 0).astype(F32).astype(BF16))
    spread = hot((iota((128, CAP), 0) >> 3) == iota((128, CAP), 1))
    wide = dot_nn(spread, own.astype(BF16))
    col = jnp.sum(
        jnp.where((iota((128, ENODES), 0) & 7) == iota((128, ENODES), 1), wide, 0.0),
        axis=1,
        keepdims=True,
    )
    by_row = jnp.broadcast_to(col, (128, 128))
    by_col = by_row.T
    before = (iota((128, 128), 1) >> 3) < (iota((128, 128), 0) >> 3)
    ahead = jnp.sum(jnp.where(before & (by_row == by_col), 1.0, 0.0), axis=1, keepdims=True)
    source = ((col - 1.0) * 2.0 + ahead).astype(I32)
    place = hot((iota((128, 128), 1) == source) & (col > 0.5))
    return select, place


def local_forces(place, rows, coords, stiff, b_s, fc_s):
    n = CAP * KROWS
    rows = dot_nn(place, rows).astype(BF16)
    basis = jnp.zeros((n, MODES), F32)
    for dof in range(NDOF):
        at = iota((n, 128), 0)
        rep = hot((at // NDOF == iota((n, 128), 1)) & (at % NDOF == dof))
        basis = basis + dot_nn(rep, rows[:, MODES * dof : MODES * dof + MODES])
    basis = basis.astype(BF16)
    b_s[...] = basis
    displaced = dot_nt(basis, coords).astype(BF16)
    every = hot(iota((32, COLS), 1) % 32 == iota((32, COLS), 0))
    wide = dot_nn(displaced, every)
    wide = jnp.where(iota((n, COLS), 0) // KROWS == iota((n, COLS), 1) // 32, wide, 0.0).astype(BF16)
    fold = hot(iota((n, KROWS), 0) % KROWS == iota((n, KROWS), 1))
    by_elem = dot_tn(fold, wide).astype(BF16)
    v = dot_nn(stiff, by_elem).astype(BF16).astype(F32)
    rolled = {}
    for g in range(4):
        part = v[:, 128 * g : 128 * g + 128]
        for shift in range(4):
            rolled[shift, g] = part if shift == 0 else pltpu.roll(part, 32 * shift, 1)
    quarter = iota((KROWS, 128), 1) // 32
    for s in range(CAP):
        for c in range(4):
            out = None
            for b in range(4):
                t = 4 * c + b
                piece = rolled[(b - s) % 4, s // 4][KROWS * t : KROWS * t + KROWS, :]
                out = piece if b == 0 else jnp.where(quarter == b, piece, out)
            fc_s[KROWS * s : KROWS * s + KROWS, 128 * c : 128 * c + 128] = out
    i0 = iota((COLS, COLS), 0)
    order = hot((i0 % 32) * 16 + i0 // 32 == iota((COLS, COLS), 1))
    return basis, dot_nn(fc_s[...].astype(BF16), order).astype(BF16)


def local_gram(basis, forces, c_s):
    n = CAP * KROWS
    inner = dot_nt(basis, basis)
    inner = jnp.where(iota((n, n), 0) // KROWS == iota((n, n), 1) // KROWS, inner, 0.0)
    h, m, l = split3(inner)
    moved = dot_nn(h.astype(BF16), forces) + dot_nn(m.astype(BF16), forces) + dot_nn(l.astype(BF16), forces)
    moved = moved * (1.0 / (SAMPLED * MODES))
    h, m, l = split3(moved)
    h, m, l = h.astype(BF16), m.astype(BF16), l.astype(BF16)
    at = 0
    for k in range(4):
        left = forces[:, 128 * k : 128 * k + 128]
        part = dot_tn(left, h[:, 128 * k :]) + dot_tn(left, m[:, 128 * k :]) + dot_tn(left, l[:, 128 * k :])
        for i in range(4 - k):
            c_s[16 * at : 16 * at + 16] = part[:, 128 * i : 128 * i + 128].reshape(16, 8, 128)
            at += 1


def panel_kernel(
    sample_in, conn_in, slot_in, dev_in, coords_in, stiff_in, basis_ref,
    gram_ref, f_ref, band_ref,
    sample_ref, conn_ref, slot_ref, dev_ref, coords_ref, stiff_ref, in_sems,
    basis_v, ids_s, st_s, tab_s, out_s, inc_s, ct_s, b_s, fc_s, c_ref, rbuf, o_ref, f_v, band_v,
    load_sem, x_send, x_recv, b_send, b_recv,
    rs_send, rs_recv, own_sem, z_send, z_recv, xy_send, xy_recv, c_send, c_recv,
    gram_sem, f_sem, band_sem,
):
    load = pltpu.make_async_copy(basis_ref, basis_v, load_sem)
    pairs = (
        (sample_in, sample_ref),
        (conn_in, conn_ref),
        (slot_in, slot_ref),
        (dev_in, dev_ref),
        (coords_in, coords_ref),
        (stiff_in, stiff_ref),
    )
    gets = [pltpu.make_async_copy(a, b, in_sems.at[i]) for i, (a, b) in enumerate(pairs)]
    e = lax.axis_index("elem")
    x = lax.axis_index("snap")
    y, z, c = e >> 4, (e >> 1) & 7, e & 1
    barrier = pltpu.get_barrier_semaphore()

    def greet(j, carry):
        v = j - 63 * (j >> 6)
        pl.semaphore_signal(barrier, inc=1, device_id=((e + v) & (N_ELEM - 1), x), device_id_type=MESH)
        return carry

    def greet_x(j, carry):
        x2 = (x + 1 + (j >> 2)) & 3
        y2 = j & 3
        pl.semaphore_signal(
            barrier, inc=1, device_id=((y2 << 4) + (z << 1) + c, x2), device_id_type=MESH
        )
        return carry

    lax.fori_loop(32, 48, greet, 0)
    lax.fori_loop(0, 12, greet_x, 0)
    lax.fori_loop(48, 95, greet, 0)
    for get in gets:
        get.start()
    load.start()
    for get in gets:
        get.wait()
    select, place = index_tables(sample_ref, conn_ref, slot_ref, dev_ref, ids_s, st_s, tab_s)
    load.wait()
    out_s[...] = dot_nn(select, basis_v[...]).astype(BF16).reshape(N_ELEM, 2, NDOF * MODES)
    pl.semaphore_wait(barrier, N_ELEM - 1 + 12)

    def rows_copy(j):
        peer = (e + j) & (N_ELEM - 1)
        return pltpu.make_async_remote_copy(
            src_ref=out_s.at[peer],
            dst_ref=inc_s.at[e],
            send_sem=b_send,
            recv_sem=b_recv,
            device_id=(peer, x),
            device_id_type=MESH,
        )

    def send_rows(j, carry):
        rows_copy(j).start()
        return carry

    lax.fori_loop(1, N_ELEM, send_rows, 0)
    for j in range(1, N_SNAP):
        pltpu.make_async_remote_copy(
            src_ref=coords_ref,
            dst_ref=ct_s.at[x],
            send_sem=x_send.at[j - 1],
            recv_sem=x_recv.at[j - 1],
            device_id=(e, (x + j) % N_SNAP),
            device_id_type=MESH,
        ).start()
    inc_s[e] = out_s[e]
    ct_s[x] = coords_ref[...]
    for j in range(1, N_SNAP):
        ref = ct_s.at[(x + N_SNAP - j) % N_SNAP]
        pltpu.make_async_copy(ref, ref, x_recv.at[j - 1]).wait()
    most = inc_s.at[pl.ds(0, N_ELEM - 1)]
    pltpu.make_async_copy(most, most, b_recv).wait()
    basis, forces = local_forces(
        place,
        inc_s[...].reshape(2 * N_ELEM, NDOF * MODES),
        ct_s[...].reshape(32, MODES),
        stiff_ref[...],
        b_s,
        fc_s,
    )
    f_v[...] = forces
    band_v[...] = b_s[:, pl.ds(pl.multiple_of(x * BAND, BAND), BAND)]
    f_out = pltpu.make_async_copy(f_v, f_ref, f_sem)
    band_out = pltpu.make_async_copy(band_v, band_ref, band_sem)
    local_gram(basis, forces, c_ref)
    line = y * 2 + c
    k_own = (5 * z + 7) >> 3
    owns = ((k_own * 104) >> 6) == z

    def scatter(i, carry):
        v = i + e
        t = v - 40 * ((v * 205) >> 13)
        ln = (t * 205) >> 10
        k = t - 5 * ln
        peer = ((ln >> 1) << 4) + (((k * 104) >> 6) << 1) + (ln & 1)

        @pl.when(peer != e)
        def _():
            pltpu.make_async_remote_copy(
                src_ref=c_ref.at[x * 40 + t],
                dst_ref=rbuf.at[e],
                send_sem=rs_send,
                recv_sem=rs_recv,
                device_id=(peer, x),
                device_id_type=MESH,
            ).start()

        return carry

    lax.fori_loop(0, 40, scatter, 0)
    f_out.start()
    band_out.start()
    first = x * 40 + line * 5
    tile = first + k_own

    @pl.when(owns)
    def _():
        mine = pltpu.make_async_copy(c_ref.at[tile], rbuf.at[e], own_sem)
        mine.start()
        mine.wait()
        most = rbuf.at[pl.ds(0, N_ELEM - 1)]
        pltpu.make_async_copy(most, most, rs_recv).wait()
        o_ref[tile] = jnp.sum(rbuf[...], axis=0)
        for dz in (1, 7, 2, 6, 3, 5, 4):
            z2 = (z + dz) & 7
            pltpu.make_async_remote_copy(
                src_ref=o_ref.at[tile],
                dst_ref=o_ref.at[tile],
                send_sem=z_send.at[dz - 1],
                recv_sem=z_recv.at[k_own],
                device_id=((y << 4) + (z2 << 1) + c, x),
                device_id_type=MESH,
            ).start()

    near = k_own - 5 * ((k_own * 205) >> 10)
    for step in (0, 1, 4, 2, 3):
        v = near + step
        k = v - 5 * ((v * 205) >> 10)
        at = first + k

        @pl.when(((k * 104) >> 6) != z)
        def _():
            pltpu.make_async_copy(o_ref.at[at], o_ref.at[at], z_recv.at[k]).wait()

        def send_tile(j, carry):
            x2, y2 = (x + (j >> 2)) & 3, (y + j) & 3
            pltpu.make_async_remote_copy(
                src_ref=o_ref.at[at],
                dst_ref=o_ref.at[at],
                send_sem=xy_send,
                recv_sem=xy_recv.at[x * 4 + y],
                device_id=((y2 << 4) + (z << 1) + c, x2),
                device_id_type=MESH,
            ).start()
            return carry

        lax.fori_loop(1, 16, send_tile, 0)

    def core_copy(j):
        x2, y2 = (x + (j >> 2)) & 3, (y + j) & 3
        n = x2 * 4 + y2
        at = (n * 2 + c) * 5
        return n, at, pltpu.make_async_remote_copy(
            src_ref=o_ref.at[pl.ds(at, 5)],
            dst_ref=o_ref.at[pl.ds(at, 5)],
            send_sem=c_send.at[n],
            recv_sem=c_recv.at[n],
            device_id=(e + 1 - 2 * c, x),
            device_id_type=MESH,
        )

    def put(at):
        pltpu.make_async_copy(o_ref.at[pl.ds(at, 5)], gram_ref.at[pl.ds(at, 5)], gram_sem).start()

    core_copy(0)[2].start()
    put(first)

    def forward(j, carry):
        n, at, copy = core_copy(j)
        ref = o_ref.at[pl.ds(at, 5)]
        pltpu.make_async_copy(ref, ref, xy_recv.at[n]).wait()
        copy.start()
        put(at)
        return carry

    lax.fori_loop(1, 16, forward, 0)

    def finish_core(n, carry):
        other = (n * 2 + 1 - c) * 5
        ref = o_ref.at[pl.ds(other, 5)]
        pltpu.make_async_copy(ref, ref, c_recv.at[n]).wait()
        put(other)
        pltpu.make_async_copy(ref, ref, c_send.at[n]).wait()
        return carry

    lax.fori_loop(0, 16, finish_core, 0)
    sent = o_ref.at[pl.ds(0, 75)]
    pltpu.make_async_copy(sent, sent, xy_send).wait()

    @pl.when(owns)
    def _():
        for dz in range(7):
            ref = o_ref.at[tile]
            pltpu.make_async_copy(ref, ref, z_send.at[dz]).wait()
        ref = c_ref.at[pl.ds(0, 39)]
        pltpu.make_async_copy(ref, ref, rs_send).wait()

    @pl.when(jnp.logical_not(owns))
    def _():
        ref = c_ref.at[pl.ds(0, 40)]
        pltpu.make_async_copy(ref, ref, rs_send).wait()

    f_out.wait()
    band_out.wait()
    pltpu.make_async_copy(o_ref, gram_ref, gram_sem).wait()
    most = inc_s.at[pl.ds(0, N_ELEM - 1)]
    pltpu.make_async_copy(most, most, b_send).wait()
    for j in range(1, N_SNAP):
        pltpu.make_async_copy(coords_ref, coords_ref, x_send.at[j - 1]).wait()


def panel_call(sample, conn, slots, dev, coords, stiff, basis):
    dma = pltpu.SemaphoreType.DMA
    n = CAP * KROWS
    width = NDOF * MODES
    return pl.pallas_call(
        panel_kernel,
        out_shape=(
            jax.ShapeDtypeStruct((160, 8, 128), F32),
            jax.ShapeDtypeStruct((n, COLS), BF16),
            jax.ShapeDtypeStruct((n, BAND), BF16),
        ),
        in_specs=[pl.BlockSpec(memory_space=pl.ANY)] * 7,
        out_specs=(pl.BlockSpec(memory_space=pl.ANY),) * 3,
        scratch_shapes=[
            pltpu.VMEM((1, SAMPLED), I32),
            pltpu.VMEM((ENODES, 2048), I32),
            pltpu.VMEM((512, 128), I32),
            pltpu.VMEM((1, SAMPLED), I32),
            pltpu.VMEM((8, MODES), BF16),
            pltpu.VMEM((16 * KROWS, KROWS), BF16),
            dma((6,)),
            pltpu.VMEM((NODE_DEV, width), BF16),
            pltpu.VMEM((ENODES, SAMPLED), I32),
            pltpu.VMEM((ENODES, SAMPLED), I32),
            pltpu.VMEM((256, 512), BF16),
            pltpu.VMEM((N_ELEM, 2, width), BF16),
            pltpu.VMEM((N_ELEM, 2, width), BF16),
            pltpu.VMEM((N_SNAP, 8, MODES), BF16),
            pltpu.VMEM((n, MODES), BF16),
            pltpu.VMEM((n, COLS), F32),
            pltpu.VMEM((160, 8, 128), F32),
            pltpu.VMEM((N_ELEM, 8, 128), F32),
            pltpu.VMEM((160, 8, 128), F32),
            pltpu.VMEM((n, COLS), BF16),
            pltpu.VMEM((n, BAND), BF16),
            dma,
            dma((3,)),
            dma((3,)),
            dma,
            dma,
            dma,
            dma,
            dma,
            dma((7,)),
            dma((5,)),
            dma,
            dma((16,)),
            dma((16,)),
            dma((16,)),
            dma,
            dma,
            dma,
        ],
        compiler_params=pltpu.CompilerParams(collective_id=1, has_side_effects=True),
        name="panel_exchange",
    )(sample, conn, slots, dev, coords, stiff, basis)


def split2(x):
    hi = x.astype(BF16)
    return hi, (x - hi.astype(F32)).astype(BF16)


def rep(v, i):
    return jnp.broadcast_to(v[i : i + 1, :], (8, 128))


def spread_cols(v, lane):
    return [jnp.broadcast_to(v[:, lane + j : lane + j + 1], (8, 128)) for j in range(8)]


def panel(diag, p0, p1, below, ahead, q0, q1):
    sub = iota((8, 128), 0)
    out = [None, None]
    for k in range(8):
        r = lax.rsqrt(rep(diag[k], k))
        c = diag[k] * r
        at = {j: rep(c, j) for j in range(k + 1, 8)}
        for j in range(k + 1, 8):
            diag[j] = diag[j] - c * at[j]
        x0, x1 = rep(p0, k) * r, rep(p1, k) * r
        p0, p1 = p0 - c * x0, p1 - c * x1
        if k == 0:
            out = [x0, x1]
        else:
            out = [jnp.where(sub == k, x, o) for x, o in zip((x0, x1), out)]
        if below is not None:
            c2 = below[k] * r
            for j in range(k + 1, 8):
                below[j] = below[j] - c2 * at[j]
            for j in range(8):
                ahead[j] = ahead[j] - c2 * rep(c2, j)
            q0, q1 = q0 - c2 * x0, q1 - c2 * x1
    return out, ahead, q0, q1


def product6(a, b):
    ah, am, al = (v.astype(BF16) for v in split3(a))
    bh, bm, bl = (v.astype(BF16) for v in split3(b))
    out = dot_nn(jnp.concatenate([ah, am], 1), jnp.concatenate([bh, bh], 0))
    out = out + dot_nn(jnp.concatenate([ah, am], 1), jnp.concatenate([bm, bm], 0))
    return out + dot_nn(jnp.concatenate([ah, al], 1), jnp.concatenate([bl, bh], 0))


def product6_tn(a, b):
    ah, am, al = (v.astype(BF16) for v in split3(a))
    bh, bm, bl = (v.astype(BF16) for v in split3(b))
    out = dot_tn(jnp.concatenate([ah, am], 0), jnp.concatenate([bh, bh], 0))
    out = out + dot_tn(jnp.concatenate([ah, am], 0), jnp.concatenate([bm, bm], 0))
    return out + dot_tn(jnp.concatenate([ah, al], 0), jnp.concatenate([bl, bh], 0))


def finish_kernel(
    c_hbm, f_hbm, b_hbm, o_ref, t_ref, A, M, uh, um, gf, gh, gm, bf, bt, o_v, c_ref, f_ref, b_ref, sems, loads
):
    get_c0 = pltpu.make_async_copy(c_hbm.at[pl.ds(0, 1)], c_ref.at[pl.ds(0, 1)], loads.at[3])
    get_c = pltpu.make_async_copy(c_hbm.at[pl.ds(1, 9)], c_ref.at[pl.ds(1, 9)], loads.at[0])
    get_f = pltpu.make_async_copy(f_hbm, f_ref, loads.at[1])
    get_b = pltpu.make_async_copy(b_hbm, b_ref, loads.at[2])
    get_c0.start()
    get_c.start()
    get_f.start()
    get_b.start()
    get_c0.wait()
    A[0:128, 0:128] = c_ref[0].reshape(128, 128)

    def rest():
        get_b.wait()
        get_f.wait()
        get_c.wait()

    def unpack(n, k, i):
        def run():
            A[128 * k : 128 * k + 128, 128 * i : 128 * i + 128] = c_ref[n].reshape(128, 128)
            if i > k:
                A[128 * i : 128 * i + 128, 128 * k : 128 * k + 128] = jnp.zeros((128, 128), F32)

        return run

    eye = jnp.where(iota((128, 128), 0) == iota((128, 128), 1), 1.0, 0.0)
    upper = iota((128, 128), 0) <= iota((128, 128), 1)

    def across(k, i, inv):
        def run():
            rows, cols = slice(128 * k, 128 * k + 128), slice(128 * i, 128 * i + 128)
            u = product6(inv, A[rows, cols])
            A[rows, cols] = u
            uh[rows, cols], um[rows, cols] = split2(u)

        return run

    def trail(k, i, j):
        def run():
            done = slice(128 * k, 128 * k + 128)
            rows, cols = slice(128 * i, 128 * i + 128), slice(128 * j, 128 * j + 128)
            A[rows, cols] = A[rows, cols] - product6_tn(A[done, rows], A[done, cols])

        return run

    def reduce(k, r):
        def run():
            rows = slice(128 * r, 128 * r + 128)
            cols = slice(128 * k, 128 * k + 128)
            g = f_ref[rows, cols].astype(F32)
            if k:
                done = slice(0, 128 * k)
                g = g - dot_nn(gh[rows, done], uh[done, cols])
                g = g - dot_nn(gh[rows, done], um[done, cols])
                g = g - dot_nn(gm[rows, done], uh[done, cols])
            gf[rows, cols] = g

        return run

    def solve(k, r, inv_h, inv_m):
        def run():
            rows = slice(128 * r, 128 * r + 128)
            cols = slice(128 * k, 128 * k + 128)
            h, m = split2(gf[rows, cols])
            g = dot_nt(h, inv_h) + dot_nt(m, inv_h)
            if inv_m is not None:
                g = g + dot_nt(h, inv_m)
            gf[rows, cols] = g
            h, m = split2(g)
            gh[rows, cols] = h
            gm[rows, cols] = m

        return run

    def flip(s):
        def run():
            b = b_ref[...] if s is None else bf[KROWS * s : KROWS * s + KROWS, :]
            if s is None:
                bf[...] = b.astype(F32)
            else:
                bt[s] = jnp.concatenate([b, b], 0).T

        return run

    def apply(k, s):
        def run():
            rows = slice(KROWS * s, KROWS * s + KROWS)
            cols = slice(128 * k, 128 * k + 128)
            g = gf[rows, cols]
            h = g.astype(BF16).astype(F32)
            rhs = jnp.concatenate([h, g - h], 0).astype(BF16)
            o_v[s, :, cols] = dot_nn(bt[s].astype(BF16), rhs)

        return run

    def store(k):
        cols = pl.ds(128 * k, 128)
        return pltpu.make_async_copy(o_v.at[:, :, cols], o_ref.at[:, :, cols], sems.at[k])

    fill = [rest] + [unpack(n, k, i) for n, (k, i) in enumerate(BLOCKS) if n]
    fill += [flip(None)] + [flip(s) for s in range(CAP)] + [reduce(0, r) for r in range(3)]
    for k in range(4):
        lo = 128 * k
        M[:, 0:128] = A[lo : lo + 128, lo : lo + 128]
        M[:, 128:256] = eye
        per = -(-len(fill) // 16)
        diag = spread_cols(M[0:8, 0:128], 0)
        p0, p1 = M[0:8, 0:128], M[0:8, 128:256]
        for p in range(16):
            top = 8 * p
            below = ahead = q0 = q1 = None
            if p < 15:
                q0, q1 = M[top + 8 : top + 16, 0:128], M[top + 8 : top + 16, 128:256]
                below, ahead = spread_cols(q0, top), spread_cols(q0, top + 8)
            (u0, u1), diag, p0, p1 = panel(diag, p0, p1, below, ahead, q0, q1)
            M[top : top + 8, 0:128] = u0
            M[top : top + 8, 128:256] = u1
            if p < 14:
                h0, m0, l0 = split3(u0)
                h1, m1, l1 = split3(u1)
                lhs = jnp.concatenate([h0, h0, m0, m0, h0, l0], 0).astype(BF16)
                r0 = jnp.concatenate([h0, m0, h0, m0, l0, h0], 0)
                r1 = jnp.concatenate([h1, m1, h1, m1, l1, h1], 0)
                start = min((top + 16) // 16 * 16, 96)
                upd = dot_nn(lhs.T[start:, :], jnp.concatenate([r0, r1], 1).astype(BF16))
                if start < top + 8:
                    upd = jnp.where(iota((128 - start, 256), 0) + start >= top + 16, upd, 0.0)
                M[start:, :] = M[start:, :] - upd
            for job in fill[per * p : per * p + per]:
                job()
        inv = M[:, 128:256]
        A[lo : lo + 128, lo : lo + 128] = jnp.where(upper, M[:, 0:128], 0.0)
        inv_h, inv_m = split2(inv)
        fill = []
        if k < 3:
            across(k, k + 1, inv)()
            trail(k, k + 1, k + 1)()
            fill += [across(k, i, inv) for i in range(k + 2, 4)]
            fill += [trail(k, i, j) for i in range(k + 1, 4) for j in range(i, 4) if j > k + 1]
        fill += [solve(k, r, inv_h, inv_m) for r in range(3)]
        if k < 3:
            fill += [reduce(k + 1, r) for r in range(3)]
        fill += [apply(k, s) for s in range(CAP)]
        fill.append(store(k).start)
    for job in fill:
        job()
    share = COLS // N_ELEM
    start = pl.multiple_of(lax.axis_index("elem") * share, share)
    t_ref[...] = A[pl.ds(start, share), :]
    for k in range(4):
        store(k).wait()


def finish(gram, forces, band):
    share = COLS // N_ELEM
    rows = CAP * KROWS
    vm = pl.BlockSpec(memory_space=pltpu.VMEM)
    return pl.pallas_call(
        finish_kernel,
        out_shape=(
            jax.ShapeDtypeStruct((CAP, BAND, COLS), F32),
            jax.ShapeDtypeStruct((share, COLS), F32),
        ),
        in_specs=[pl.BlockSpec(memory_space=pl.ANY)] * 3,
        out_specs=(pl.BlockSpec(memory_space=pl.ANY), vm),
        scratch_shapes=[
            pltpu.VMEM((COLS, COLS), F32),
            pltpu.VMEM((128, 256), F32),
            pltpu.VMEM((COLS, COLS), BF16),
            pltpu.VMEM((COLS, COLS), BF16),
            pltpu.VMEM((rows, COLS), F32),
            pltpu.VMEM((rows, COLS), BF16),
            pltpu.VMEM((rows, COLS), BF16),
            pltpu.VMEM((rows, BAND), F32),
            pltpu.VMEM((CAP, BAND, 2 * KROWS), F32),
            pltpu.VMEM((CAP, BAND, COLS), F32),
            pltpu.VMEM((10, 16, 8, 128), F32),
            pltpu.VMEM((rows, COLS), BF16),
            pltpu.VMEM((rows, BAND), BF16),
            pltpu.SemaphoreType.DMA((4,)),
            pltpu.SemaphoreType.DMA((4,)),
        ],
        name="factor_and_apply",
    )(gram, forces, band)


def shards(
    node_basis, stiff_terms, reduced_coords, sample_list, connectivity, node_slot, elem_device
):
    gram, forces, band = panel_call(
        sample_list.reshape(1, SAMPLED),
        connectivity.T,
        node_slot.reshape(512, 128),
        elem_device.reshape(1, SAMPLED),
        reduced_coords.T,
        stiff_terms.reshape(16 * KROWS, KROWS),
        node_basis,
    )
    return finish(gram.reshape(10, 16, 8, 128), forces, band)


def solution(mesh):
    placed = (P("elem", None), P(), P(None, "snap"), P(), P(), P(), P())
    return jax.shard_map(
        shards,
        mesh=mesh,
        in_specs=placed,
        out_specs=(P("elem", "snap", None), P("elem", None)),
        check_vma=False,
    )
```

```python
import jax
import jax.numpy as jnp
from jax import lax
from jax.experimental import pallas as pl
from jax.experimental.pallas import tpu as pltpu
from jax.sharding import PartitionSpec as P

F32, BF16, I32 = jnp.float32, jnp.bfloat16, jnp.int32
HI = lax.Precision.HIGHEST
MESH = pl.DeviceIdType.MESH
MODES = 512
COLS = 512
ENODES = 8
NDOF = 3
CAP = 16
SAMPLED = 512
N_ELEM = 64
N_SNAP = 4
NODE_DEV = 1024
BAND = MODES // N_SNAP
KROWS = ENODES * NDOF
BLOCKS = [(k, i) for k in range(4) for i in range(k, 4)]


def iota(shape, axis):
    return lax.broadcasted_iota(I32, shape, axis)


def hot(mask):
    return jnp.where(mask, 1.0, 0.0).astype(BF16)


def dot_nt(a, b):
    return lax.dot_general(a, b, (((1,), (1,)), ((), ())), preferred_element_type=F32)


def dot_tn(a, b, precision=None):
    return lax.dot_general(
        a, b, (((0,), (0,)), ((), ())), precision=precision, preferred_element_type=F32
    )


def dot_nn(a, b):
    return jnp.dot(a, b, preferred_element_type=F32)


def split3(x):
    h = x.astype(BF16).astype(F32)
    r = x - h
    m = r.astype(BF16).astype(F32)
    return h, m, r - m


def index_tables(sample_ref, conn_ref, slot_ref, dev_ref, ids_s, st_s, tab_s):
    me = lax.axis_index("elem")
    conn = conn_ref[...] + 1
    conn_t = jnp.concatenate([(conn >> 8).astype(F32), (conn & 255).astype(F32)], 0)
    sample = sample_ref[...]
    groups = 2048 // 128
    stacked = jnp.concatenate([conn_t[:, 128 * g : 128 * g + 128] for g in range(groups)], 0)
    found = dot_nn(stacked.astype(BF16), hot(iota((128, SAMPLED), 0) == (sample & 127)))
    ids = jnp.zeros((16, SAMPLED), F32)
    for g in range(groups):
        ids = ids + jnp.where((sample >> 7) == g, found[16 * g : 16 * g + 16], 0.0)
    ids1 = (ids[0:8] * 256.0 + ids[8:16]).astype(I32)
    live = ids1 > 0
    ids_s[...] = jnp.maximum(ids1 - 1, 0)
    table = slot_ref[...]
    tab_s[0:128, :] = (table >> 8).astype(F32).T.astype(BF16)
    tab_s[128:256, :] = (table & 255).astype(F32).T.astype(BF16)

    def lookup(p):
        row = ids_s[p : p + 1, :]
        picks = hot(iota((512, SAMPLED), 0) == (row >> 7))
        found = dot_nn(tab_s[...], picks)
        here = iota((128, SAMPLED), 0) == (row & 127)
        hi = jnp.sum(jnp.where(here, found[0:128], 0.0), axis=0, keepdims=True)
        lo = jnp.sum(jnp.where(here, found[128:256], 0.0), axis=0, keepdims=True)
        st_s[p : p + 1, :] = (hi * 256.0 + lo).astype(I32)

    for p in range(ENODES):
        lookup(p)
    stored = st_s[...]
    owner = stored >> 10
    mine = live & (owner == me)
    has = jnp.max(jnp.where(mine, 1.0, 0.0), axis=0, keepdims=True)
    row = jnp.sum(jnp.where(mine, stored & (NODE_DEV - 1), 0), axis=0, keepdims=True)
    dev = dev_ref[...]
    dev_f = dev.astype(F32)
    dev_col = jnp.broadcast_to(dev_f, (8, SAMPLED)).T[:, 0:1]
    same = hot((dev_col == dev_f) & (iota((SAMPLED, SAMPLED), 0) < iota((SAMPLED, SAMPLED), 1)))
    counts = dot_nn(jnp.where(iota((8, SAMPLED), 0) == 0, has, 1.0).astype(BF16), same)
    rank = counts[0:1].astype(I32)
    slot = counts[1:2].astype(I32)
    q = iota((2 * N_ELEM, SAMPLED), 0)
    goes = hot(((q >> 1) == dev) & ((q & 1) == rank) & (has > 0.5))
    r8 = iota((8, SAMPLED), 0)
    vals = jnp.where(r8 == 0, (row >> 8).astype(F32), jnp.where(r8 == 1, (row & 255).astype(F32), 1.0))
    tab = dot_nt(goes, vals.astype(BF16))
    pick = (tab[:, 0:1] * 256.0 + tab[:, 1:2]).astype(I32)
    valid = tab[:, 2:3] > 0.5
    select = hot((iota((2 * N_ELEM, NODE_DEV), 1) == pick) & valid)
    here = hot((slot == iota((CAP, SAMPLED), 0)) & (dev == me))
    own = dot_nt(here, jnp.where(live, owner + 1, 0).astype(F32).astype(BF16))
    spread = hot((iota((128, CAP), 0) >> 3) == iota((128, CAP), 1))
    wide = dot_nn(spread, own.astype(BF16))
    col = jnp.sum(
        jnp.where((iota((128, ENODES), 0) & 7) == iota((128, ENODES), 1), wide, 0.0),
        axis=1,
        keepdims=True,
    )
    by_row = jnp.broadcast_to(col, (128, 128))
    by_col = by_row.T
    before = (iota((128, 128), 1) >> 3) < (iota((128, 128), 0) >> 3)
    ahead = jnp.sum(jnp.where(before & (by_row == by_col), 1.0, 0.0), axis=1, keepdims=True)
    source = ((col - 1.0) * 2.0 + ahead).astype(I32)
    place = hot((iota((128, 128), 1) == source) & (col > 0.5))
    return select, place


def local_forces(place, rows, coords, stiff, b_s, fc_s):
    n = CAP * KROWS
    rows = dot_nn(place, rows).astype(BF16)
    basis = jnp.zeros((n, MODES), F32)
    for dof in range(NDOF):
        at = iota((n, 128), 0)
        rep = hot((at // NDOF == iota((n, 128), 1)) & (at % NDOF == dof))
        basis = basis + dot_nn(rep, rows[:, MODES * dof : MODES * dof + MODES])
    basis = basis.astype(BF16)
    b_s[...] = basis
    displaced = dot_nt(basis, coords).astype(BF16)
    every = hot(iota((32, COLS), 1) % 32 == iota((32, COLS), 0))
    wide = dot_nn(displaced, every)
    wide = jnp.where(iota((n, COLS), 0) // KROWS == iota((n, COLS), 1) // 32, wide, 0.0).astype(BF16)
    fold = hot(iota((n, KROWS), 0) % KROWS == iota((n, KROWS), 1))
    by_elem = dot_tn(fold, wide).astype(BF16)
    v = dot_nn(stiff, by_elem).astype(BF16).astype(F32)
    rolled = {}
    for g in range(4):
        part = v[:, 128 * g : 128 * g + 128]
        for shift in range(4):
            rolled[shift, g] = part if shift == 0 else pltpu.roll(part, 32 * shift, 1)
    quarter = iota((KROWS, 128), 1) // 32
    for s in range(CAP):
        for c in range(4):
            out = None
            for b in range(4):
                t = 4 * c + b
                piece = rolled[(b - s) % 4, s // 4][KROWS * t : KROWS * t + KROWS, :]
                out = piece if b == 0 else jnp.where(quarter == b, piece, out)
            fc_s[KROWS * s : KROWS * s + KROWS, 128 * c : 128 * c + 128] = out
    i0 = iota((COLS, COLS), 0)
    order = hot((i0 % 32) * 16 + i0 // 32 == iota((COLS, COLS), 1))
    return basis, dot_nn(fc_s[...].astype(BF16), order).astype(BF16)


def local_gram(basis, forces, c_s):
    n = CAP * KROWS
    inner = dot_nt(basis, basis)
    inner = jnp.where(iota((n, n), 0) // KROWS == iota((n, n), 1) // KROWS, inner, 0.0)
    h, m, l = split3(inner)
    moved = dot_nn(h.astype(BF16), forces) + dot_nn(m.astype(BF16), forces) + dot_nn(l.astype(BF16), forces)
    moved = moved * (1.0 / (SAMPLED * MODES))
    h, m, l = split3(moved)
    h, m, l = h.astype(BF16), m.astype(BF16), l.astype(BF16)
    at = 0
    for k in range(4):
        left = forces[:, 128 * k : 128 * k + 128]
        part = dot_tn(left, h[:, 128 * k :]) + dot_tn(left, m[:, 128 * k :]) + dot_tn(left, l[:, 128 * k :])
        for i in range(4 - k):
            c_s[16 * at : 16 * at + 16] = part[:, 128 * i : 128 * i + 128].reshape(16, 8, 128)
            at += 1


def panel_kernel(
    sample_in, conn_in, slot_in, dev_in, coords_in, stiff_in, basis_ref,
    gram_ref, f_ref, band_ref,
    sample_ref, conn_ref, slot_ref, dev_ref, coords_ref, stiff_ref, in_sems,
    basis_v, ids_s, st_s, tab_s, out_s, inc_s, ct_s, b_s, fc_s, c_ref, rbuf, o_ref, f_v, band_v,
    load_sem, x_send, x_recv, b_send, b_recv,
    rs_send, rs_recv, own_sem, z_send, z_recv, xy_send, xy_recv, c_send, c_recv,
    gram_sem, f_sem, band_sem,
):
    load = pltpu.make_async_copy(basis_ref, basis_v, load_sem)
    pairs = (
        (sample_in, sample_ref),
        (conn_in, conn_ref),
        (slot_in, slot_ref),
        (dev_in, dev_ref),
        (coords_in, coords_ref),
        (stiff_in, stiff_ref),
    )
    gets = [pltpu.make_async_copy(a, b, in_sems.at[i]) for i, (a, b) in enumerate(pairs)]
    e = lax.axis_index("elem")
    x = lax.axis_index("snap")
    y, z, c = e >> 4, (e >> 1) & 7, e & 1
    barrier = pltpu.get_barrier_semaphore()

    def greet(j, carry):
        v = j - 63 * (j >> 6)
        pl.semaphore_signal(barrier, inc=1, device_id=((e + v) & (N_ELEM - 1), x), device_id_type=MESH)
        return carry

    def greet_x(j, carry):
        x2 = (x + 1 + (j >> 2)) & 3
        y2 = j & 3
        pl.semaphore_signal(
            barrier, inc=1, device_id=((y2 << 4) + (z << 1) + c, x2), device_id_type=MESH
        )
        return carry

    lax.fori_loop(32, 48, greet, 0)
    lax.fori_loop(0, 12, greet_x, 0)
    lax.fori_loop(48, 95, greet, 0)
    for get in gets:
        get.start()
    load.start()
    for get in gets:
        get.wait()
    select, place = index_tables(sample_ref, conn_ref, slot_ref, dev_ref, ids_s, st_s, tab_s)
    load.wait()
    out_s[...] = dot_nn(select, basis_v[...]).astype(BF16).reshape(N_ELEM, 2, NDOF * MODES)
    pl.semaphore_wait(barrier, N_ELEM - 1 + 12)

    def rows_copy(j):
        peer = (e + j) & (N_ELEM - 1)
        return pltpu.make_async_remote_copy(
            src_ref=out_s.at[peer],
            dst_ref=inc_s.at[e],
            send_sem=b_send,
            recv_sem=b_recv,
            device_id=(peer, x),
            device_id_type=MESH,
        )

    def send_rows(j, carry):
        rows_copy(j).start()
        return carry

    lax.fori_loop(1, N_ELEM, send_rows, 0)
    for j in range(1, N_SNAP):
        pltpu.make_async_remote_copy(
            src_ref=coords_ref,
            dst_ref=ct_s.at[x],
            send_sem=x_send.at[j - 1],
            recv_sem=x_recv.at[j - 1],
            device_id=(e, (x + j) % N_SNAP),
            device_id_type=MESH,
        ).start()
    inc_s[e] = out_s[e]
    ct_s[x] = coords_ref[...]
    for j in range(1, N_SNAP):
        ref = ct_s.at[(x + N_SNAP - j) % N_SNAP]
        pltpu.make_async_copy(ref, ref, x_recv.at[j - 1]).wait()
    most = inc_s.at[pl.ds(0, N_ELEM - 1)]
    pltpu.make_async_copy(most, most, b_recv).wait()
    basis, forces = local_forces(
        place,
        inc_s[...].reshape(2 * N_ELEM, NDOF * MODES),
        ct_s[...].reshape(32, MODES),
        stiff_ref[...],
        b_s,
        fc_s,
    )
    f_v[...] = forces
    band_v[...] = b_s[:, pl.ds(pl.multiple_of(x * BAND, BAND), BAND)]
    f_out = pltpu.make_async_copy(f_v, f_ref, f_sem)
    band_out = pltpu.make_async_copy(band_v, band_ref, band_sem)
    local_gram(basis, forces, c_ref)
    line = y * 2 + c
    k_own = (5 * z + 7) >> 3
    owns = ((k_own * 104) >> 6) == z

    def scatter(i, carry):
        v = i + e
        t = v - 40 * ((v * 205) >> 13)
        ln = (t * 205) >> 10
        k = t - 5 * ln
        peer = ((ln >> 1) << 4) + (((k * 104) >> 6) << 1) + (ln & 1)

        @pl.when(peer != e)
        def _():
            pltpu.make_async_remote_copy(
                src_ref=c_ref.at[x * 40 + t],
                dst_ref=rbuf.at[e],
                send_sem=rs_send,
                recv_sem=rs_recv,
                device_id=(peer, x),
                device_id_type=MESH,
            ).start()

        return carry

    lax.fori_loop(0, 40, scatter, 0)
    f_out.start()
    band_out.start()
    first = x * 40 + line * 5
    tile = first + k_own

    @pl.when(owns)
    def _():
        mine = pltpu.make_async_copy(c_ref.at[tile], rbuf.at[e], own_sem)
        mine.start()
        mine.wait()
        most = rbuf.at[pl.ds(0, N_ELEM - 1)]
        pltpu.make_async_copy(most, most, rs_recv).wait()
        o_ref[tile] = jnp.sum(rbuf[...], axis=0)
        for dz in (1, 7, 2, 6, 3, 5, 4):
            z2 = (z + dz) & 7
            pltpu.make_async_remote_copy(
                src_ref=o_ref.at[tile],
                dst_ref=o_ref.at[tile],
                send_sem=z_send.at[dz - 1],
                recv_sem=z_recv.at[k_own],
                device_id=((y << 4) + (z2 << 1) + c, x),
                device_id_type=MESH,
            ).start()

    near = k_own - 5 * ((k_own * 205) >> 10)
    for step in (0, 1, 4, 2, 3):
        v = near + step
        k = v - 5 * ((v * 205) >> 10)
        at = first + k

        @pl.when(((k * 104) >> 6) != z)
        def _():
            pltpu.make_async_copy(o_ref.at[at], o_ref.at[at], z_recv.at[k]).wait()

        def send_tile(i, carry):
            j = i - 15 * (i >> 4)
            x2, y2 = (x + (j >> 2)) & 3, (y + j) & 3
            pltpu.make_async_remote_copy(
                src_ref=o_ref.at[at],
                dst_ref=o_ref.at[at],
                send_sem=xy_send,
                recv_sem=xy_recv.at[x * 4 + y],
                device_id=((y2 << 4) + (z << 1) + c, x2),
                device_id_type=MESH,
            ).start()
            return carry

        lax.fori_loop(10, 25, send_tile, 0)

    def core_copy(j):
        x2, y2 = (x + (j >> 2)) & 3, (y + j) & 3
        n = x2 * 4 + y2
        at = (n * 2 + c) * 5
        return n, at, pltpu.make_async_remote_copy(
            src_ref=o_ref.at[pl.ds(at, 5)],
            dst_ref=o_ref.at[pl.ds(at, 5)],
            send_sem=c_send.at[n],
            recv_sem=c_recv.at[n],
            device_id=(e + 1 - 2 * c, x),
            device_id_type=MESH,
        )

    def put(at):
        pltpu.make_async_copy(o_ref.at[pl.ds(at, 5)], gram_ref.at[pl.ds(at, 5)], gram_sem).start()

    core_copy(0)[2].start()
    put(first)

    def forward(j, carry):
        n, at, copy = core_copy(j)
        ref = o_ref.at[pl.ds(at, 5)]
        pltpu.make_async_copy(ref, ref, xy_recv.at[n]).wait()
        copy.start()
        put(at)
        return carry

    lax.fori_loop(1, 16, forward, 0)

    def finish_core(n, carry):
        other = (n * 2 + 1 - c) * 5
        ref = o_ref.at[pl.ds(other, 5)]
        pltpu.make_async_copy(ref, ref, c_recv.at[n]).wait()
        put(other)
        pltpu.make_async_copy(ref, ref, c_send.at[n]).wait()
        return carry

    lax.fori_loop(0, 16, finish_core, 0)
    sent = o_ref.at[pl.ds(0, 75)]
    pltpu.make_async_copy(sent, sent, xy_send).wait()

    @pl.when(owns)
    def _():
        for dz in range(7):
            ref = o_ref.at[tile]
            pltpu.make_async_copy(ref, ref, z_send.at[dz]).wait()
        ref = c_ref.at[pl.ds(0, 39)]
        pltpu.make_async_copy(ref, ref, rs_send).wait()

    @pl.when(jnp.logical_not(owns))
    def _():
        ref = c_ref.at[pl.ds(0, 40)]
        pltpu.make_async_copy(ref, ref, rs_send).wait()

    f_out.wait()
    band_out.wait()
    pltpu.make_async_copy(o_ref, gram_ref, gram_sem).wait()
    most = inc_s.at[pl.ds(0, N_ELEM - 1)]
    pltpu.make_async_copy(most, most, b_send).wait()
    for j in range(1, N_SNAP):
        pltpu.make_async_copy(coords_ref, coords_ref, x_send.at[j - 1]).wait()


def panel_call(sample, conn, slots, dev, coords, stiff, basis):
    dma = pltpu.SemaphoreType.DMA
    n = CAP * KROWS
    width = NDOF * MODES
    return pl.pallas_call(
        panel_kernel,
        out_shape=(
            jax.ShapeDtypeStruct((160, 8, 128), F32),
            jax.ShapeDtypeStruct((n, COLS), BF16),
            jax.ShapeDtypeStruct((n, BAND), BF16),
        ),
        in_specs=[pl.BlockSpec(memory_space=pl.ANY)] * 7,
        out_specs=(pl.BlockSpec(memory_space=pl.ANY),) * 3,
        scratch_shapes=[
            pltpu.VMEM((1, SAMPLED), I32),
            pltpu.VMEM((ENODES, 2048), I32),
            pltpu.VMEM((512, 128), I32),
            pltpu.VMEM((1, SAMPLED), I32),
            pltpu.VMEM((8, MODES), BF16),
            pltpu.VMEM((16 * KROWS, KROWS), BF16),
            dma((6,)),
            pltpu.VMEM((NODE_DEV, width), BF16),
            pltpu.VMEM((ENODES, SAMPLED), I32),
            pltpu.VMEM((ENODES, SAMPLED), I32),
            pltpu.VMEM((256, 512), BF16),
            pltpu.VMEM((N_ELEM, 2, width), BF16),
            pltpu.VMEM((N_ELEM, 2, width), BF16),
            pltpu.VMEM((N_SNAP, 8, MODES), BF16),
            pltpu.VMEM((n, MODES), BF16),
            pltpu.VMEM((n, COLS), F32),
            pltpu.VMEM((160, 8, 128), F32),
            pltpu.VMEM((N_ELEM, 8, 128), F32),
            pltpu.VMEM((160, 8, 128), F32),
            pltpu.VMEM((n, COLS), BF16),
            pltpu.VMEM((n, BAND), BF16),
            dma,
            dma((3,)),
            dma((3,)),
            dma,
            dma,
            dma,
            dma,
            dma,
            dma((7,)),
            dma((5,)),
            dma,
            dma((16,)),
            dma((16,)),
            dma((16,)),
            dma,
            dma,
            dma,
        ],
        compiler_params=pltpu.CompilerParams(collective_id=1, has_side_effects=True),
        name="panel_exchange",
    )(sample, conn, slots, dev, coords, stiff, basis)


def split2(x):
    hi = x.astype(BF16)
    return hi, (x - hi.astype(F32)).astype(BF16)


def rep(v, i):
    return jnp.broadcast_to(v[i : i + 1, :], (8, 128))


def spread_cols(v, lane):
    return [jnp.broadcast_to(v[:, lane + j : lane + j + 1], (8, 128)) for j in range(8)]


def panel(diag, p0, p1, below, ahead, q0, q1):
    sub = iota((8, 128), 0)
    out = [None, None]
    for k in range(8):
        r = lax.rsqrt(rep(diag[k], k))
        c = diag[k] * r
        at = {j: rep(c, j) for j in range(k + 1, 8)}
        for j in range(k + 1, 8):
            diag[j] = diag[j] - c * at[j]
        x0, x1 = rep(p0, k) * r, rep(p1, k) * r
        p0, p1 = p0 - c * x0, p1 - c * x1
        if k == 0:
            out = [x0, x1]
        else:
            out = [jnp.where(sub == k, x, o) for x, o in zip((x0, x1), out)]
        if below is not None:
            c2 = below[k] * r
            for j in range(k + 1, 8):
                below[j] = below[j] - c2 * at[j]
            for j in range(8):
                ahead[j] = ahead[j] - c2 * rep(c2, j)
            q0, q1 = q0 - c2 * x0, q1 - c2 * x1
    return out, ahead, q0, q1


def product6(a, b):
    ah, am, al = (v.astype(BF16) for v in split3(a))
    bh, bm, bl = (v.astype(BF16) for v in split3(b))
    out = dot_nn(jnp.concatenate([ah, am], 1), jnp.concatenate([bh, bh], 0))
    out = out + dot_nn(jnp.concatenate([ah, am], 1), jnp.concatenate([bm, bm], 0))
    return out + dot_nn(jnp.concatenate([ah, al], 1), jnp.concatenate([bl, bh], 0))


def product6_tn(a, b):
    ah, am, al = (v.astype(BF16) for v in split3(a))
    bh, bm, bl = (v.astype(BF16) for v in split3(b))
    out = dot_tn(jnp.concatenate([ah, am], 0), jnp.concatenate([bh, bh], 0))
    out = out + dot_tn(jnp.concatenate([ah, am], 0), jnp.concatenate([bm, bm], 0))
    return out + dot_tn(jnp.concatenate([ah, al], 0), jnp.concatenate([bl, bh], 0))


def finish_kernel(
    c_hbm, f_hbm, b_hbm, o_ref, t_ref, A, M, uh, um, gf, gh, gm, bf, bt, o_v, c_ref, f_ref, b_ref, sems, loads
):
    get_c0 = pltpu.make_async_copy(c_hbm.at[pl.ds(0, 1)], c_ref.at[pl.ds(0, 1)], loads.at[3])
    get_c = pltpu.make_async_copy(c_hbm.at[pl.ds(1, 9)], c_ref.at[pl.ds(1, 9)], loads.at[0])
    get_f = pltpu.make_async_copy(f_hbm, f_ref, loads.at[1])
    get_b = pltpu.make_async_copy(b_hbm, b_ref, loads.at[2])
    get_c0.start()
    get_c.start()
    get_f.start()
    get_b.start()
    get_c0.wait()
    A[0:128, 0:128] = c_ref[0].reshape(128, 128)

    def rest():
        get_b.wait()
        get_f.wait()
        get_c.wait()

    def unpack(n, k, i):
        def run():
            A[128 * k : 128 * k + 128, 128 * i : 128 * i + 128] = c_ref[n].reshape(128, 128)
            if i > k:
                A[128 * i : 128 * i + 128, 128 * k : 128 * k + 128] = jnp.zeros((128, 128), F32)

        return run

    eye = jnp.where(iota((128, 128), 0) == iota((128, 128), 1), 1.0, 0.0)
    upper = iota((128, 128), 0) <= iota((128, 128), 1)

    def across(k, i, inv):
        def run():
            rows, cols = slice(128 * k, 128 * k + 128), slice(128 * i, 128 * i + 128)
            u = product6(inv, A[rows, cols])
            A[rows, cols] = u
            uh[rows, cols], um[rows, cols] = split2(u)

        return run

    def trail(k, i, j):
        def run():
            done = slice(128 * k, 128 * k + 128)
            rows, cols = slice(128 * i, 128 * i + 128), slice(128 * j, 128 * j + 128)
            A[rows, cols] = A[rows, cols] - product6_tn(A[done, rows], A[done, cols])

        return run

    def reduce(k, r):
        def run():
            rows = slice(128 * r, 128 * r + 128)
            cols = slice(128 * k, 128 * k + 128)
            g = f_ref[rows, cols].astype(F32)
            if k:
                done = slice(0, 128 * k)
                g = g - dot_nn(gh[rows, done], uh[done, cols])
                g = g - dot_nn(gh[rows, done], um[done, cols])
                g = g - dot_nn(gm[rows, done], uh[done, cols])
            gf[rows, cols] = g

        return run

    def solve(k, r, inv_h, inv_m):
        def run():
            rows = slice(128 * r, 128 * r + 128)
            cols = slice(128 * k, 128 * k + 128)
            h, m = split2(gf[rows, cols])
            g = dot_nt(h, inv_h) + dot_nt(m, inv_h)
            if inv_m is not None:
                g = g + dot_nt(h, inv_m)
            gf[rows, cols] = g
            h, m = split2(g)
            gh[rows, cols] = h
            gm[rows, cols] = m

        return run

    def flip(s):
        def run():
            b = b_ref[...] if s is None else bf[KROWS * s : KROWS * s + KROWS, :]
            if s is None:
                bf[...] = b.astype(F32)
            else:
                bt[s] = jnp.concatenate([b, b], 0).T

        return run

    def apply(k, s):
        def run():
            rows = slice(KROWS * s, KROWS * s + KROWS)
            cols = slice(128 * k, 128 * k + 128)
            g = gf[rows, cols]
            h = g.astype(BF16).astype(F32)
            rhs = jnp.concatenate([h, g - h], 0).astype(BF16)
            o_v[s, :, cols] = dot_nn(bt[s].astype(BF16), rhs)

        return run

    def store(k, part=None):
        cols = pl.ds(128 * k, 128)
        some = pl.ds(0, CAP) if part is None else pl.ds(4 * part, 4)
        sem = sems.at[k if part is None else k + part]
        return pltpu.make_async_copy(o_v.at[some, :, cols], o_ref.at[some, :, cols], sem)

    fill = [rest] + [unpack(n, k, i) for n, (k, i) in enumerate(BLOCKS) if n]
    fill += [flip(None)] + [flip(s) for s in range(CAP)] + [reduce(0, r) for r in range(3)]
    for k in range(4):
        lo = 128 * k
        M[:, 0:128] = A[lo : lo + 128, lo : lo + 128]
        M[:, 128:256] = eye
        per = -(-len(fill) // 16)
        diag = spread_cols(M[0:8, 0:128], 0)
        p0, p1 = M[0:8, 0:128], M[0:8, 128:256]
        for p in range(16):
            top = 8 * p
            below = ahead = q0 = q1 = None
            if p < 15:
                q0, q1 = M[top + 8 : top + 16, 0:128], M[top + 8 : top + 16, 128:256]
                below, ahead = spread_cols(q0, top), spread_cols(q0, top + 8)
            (u0, u1), diag, p0, p1 = panel(diag, p0, p1, below, ahead, q0, q1)
            M[top : top + 8, 0:128] = u0
            M[top : top + 8, 128:256] = u1
            if p < 14:
                h0, m0, l0 = split3(u0)
                h1, m1, l1 = split3(u1)
                lhs = jnp.concatenate([h0, h0, m0, m0, h0, l0], 0).astype(BF16)
                r0 = jnp.concatenate([h0, m0, h0, m0, l0, h0], 0)
                r1 = jnp.concatenate([h1, m1, h1, m1, l1, h1], 0)
                start = min((top + 16) // 16 * 16, 96)
                upd = dot_nn(lhs.T[start:, :], jnp.concatenate([r0, r1], 1).astype(BF16))
                if start < top + 8:
                    upd = jnp.where(iota((128 - start, 256), 0) + start >= top + 16, upd, 0.0)
                M[start:, :] = M[start:, :] - upd
            for job in fill[per * p : per * p + per]:
                job()
        inv = M[:, 128:256]
        A[lo : lo + 128, lo : lo + 128] = jnp.where(upper, M[:, 0:128], 0.0)
        inv_h, inv_m = split2(inv)
        fill = []
        if k < 3:
            across(k, k + 1, inv)()
            trail(k, k + 1, k + 1)()
            fill += [across(k, i, inv) for i in range(k + 2, 4)]
            fill += [trail(k, i, j) for i in range(k + 1, 4) for j in range(i, 4) if j > k + 1]
        fill += [solve(k, r, inv_h, inv_m) for r in range(3)]
        if k < 3:
            fill += [reduce(k + 1, r) for r in range(3)]
            fill += [apply(k, s) for s in range(CAP)]
            fill.append(store(k).start)
        else:
            for part in range(4):
                fill += [apply(k, s) for s in range(4 * part, 4 * part + 4)]
                fill.append(store(k, part).start)
    for job in fill:
        job()
    share = COLS // N_ELEM
    start = pl.multiple_of(lax.axis_index("elem") * share, share)
    t_ref[...] = A[pl.ds(start, share), :]
    for k in range(3):
        store(k).wait()
    for part in range(4):
        store(3, part).wait()


def finish(gram, forces, band):
    share = COLS // N_ELEM
    rows = CAP * KROWS
    vm = pl.BlockSpec(memory_space=pltpu.VMEM)
    return pl.pallas_call(
        finish_kernel,
        out_shape=(
            jax.ShapeDtypeStruct((CAP, BAND, COLS), F32),
            jax.ShapeDtypeStruct((share, COLS), F32),
        ),
        in_specs=[pl.BlockSpec(memory_space=pl.ANY)] * 3,
        out_specs=(pl.BlockSpec(memory_space=pl.ANY), vm),
        scratch_shapes=[
            pltpu.VMEM((COLS, COLS), F32),
            pltpu.VMEM((128, 256), F32),
            pltpu.VMEM((COLS, COLS), BF16),
            pltpu.VMEM((COLS, COLS), BF16),
            pltpu.VMEM((rows, COLS), F32),
            pltpu.VMEM((rows, COLS), BF16),
            pltpu.VMEM((rows, COLS), BF16),
            pltpu.VMEM((rows, BAND), F32),
            pltpu.VMEM((CAP, BAND, 2 * KROWS), F32),
            pltpu.VMEM((CAP, BAND, COLS), F32),
            pltpu.VMEM((10, 16, 8, 128), F32),
            pltpu.VMEM((rows, COLS), BF16),
            pltpu.VMEM((rows, BAND), BF16),
            pltpu.SemaphoreType.DMA((7,)),
            pltpu.SemaphoreType.DMA((4,)),
        ],
        name="factor_and_apply",
    )(gram, forces, band)


def shards(
    node_basis, stiff_terms, reduced_coords, sample_list, connectivity, node_slot, elem_device
):
    gram, forces, band = panel_call(
        sample_list.reshape(1, SAMPLED),
        connectivity.T,
        node_slot.reshape(512, 128),
        elem_device.reshape(1, SAMPLED),
        reduced_coords.T,
        stiff_terms.reshape(16 * KROWS, KROWS),
        node_basis,
    )
    return finish(gram.reshape(10, 16, 8, 128), forces, band)


def solution(mesh):
    placed = (P("elem", None), P(), P(None, "snap"), P(), P(), P(), P())
    return jax.shard_map(
        shards,
        mesh=mesh,
        in_specs=placed,
        out_specs=(P("elem", "snap", None), P("elem", None)),
        check_vma=False,
    )
```
